32 devices in a mesh: brick: 8 (over z, y), depth: 4 (over x, core).
Axes of the slice: x: 2, y: 2, z: 4, core: 2. Of those that a mesh axis runs over, the one named last changes fastest.
Arguments:
- conductivity: float32 [64, 64, 256], P('brick', 'depth'), may hold values from 0.03 to 10.5, as said below
- initial_field: float32 [2, 64, 64, 256], P(None, 'brick', 'depth'), may hold values from -1.2 to 1.2
- adjoint_initial: float32 [2, 64, 64, 256], P(None, 'brick', 'depth'), may hold values from -0.36 to 0.36
- src_cell: int32 [8, 4, 64], P('brick', 'depth'), may hold values from 0 to 32767
- src_amp: float32 [8, 4, 2, 64], P('brick', 'depth'), may hold values from -24 to 24
- rec_cell: int32 [8, 4, 64], P('brick', 'depth'), may hold values from 0 to 32767
- observed: float32 [8, 4, 2, 64], P('brick', 'depth'), may hold values from -12 to 12
- cov_blocks: bfloat16 [8, 4, 16, 512, 512], P('brick', 'depth'), may hold values from -0.25 to 0.25
- cov_rows: int32 [8, 4, 16], P('brick', 'depth'), may hold values from 0 to 63
- cov_cols: int32 [8, 4, 16], P('brick', 'depth'), may hold values from 0 to 255
Outputs:
- forward: float32 [2, 64, 64, 256], P(None, 'brick', 'depth')
- preconditioned: float32 [64, 64, 256], P('brick', 'depth')
The draws below stay inside these ranges and needn't reach their ends.
Inputs may be any that keep to these rules, and one draw needn't show every extreme that they name: `conductivity`: positive everywhere.
All inputs are finite; a program needn't handle non-finite values.
Results may differ from the reference program's by a relative error of at most 0.0032.
Values may be sent and summed in bfloat16 or wider, within the bound.
No kernel may reach another device: no remote copies, remote signals or barrier semaphores. Data moves between devices by JAX's collectives and lax.ppermute only.
A program may use at most 128 MiB of HBM per device.

```python
import math
import jax
import jax.numpy as jnp
from jax import lax

CX = 8
CZ = 16
NY = 256
FREQS = 2
ITERS = 3
BLOCK = 512
NNZ = 16
NS = 64
NR = 64
NX = 64
NZ = 64
BLK_DEV = 64
COL_BLOCKS = 256
N_BRICK = 8
N_DEPTH = 4


def coordinates():
    x_frac = ((jnp.arange(NX, dtype=jnp.float32) + 0.5) / NX)[:, None, None]
    z_frac = ((jnp.arange(NZ, dtype=jnp.float32) + 0.5) / NZ)[None, :, None]
    y_frac = ((jnp.arange(NY, dtype=jnp.float32) + 0.5) / NY)[None, None, :]
    return (x_frac, z_frac, y_frac)


def draw_conductivity(key, part):
    own_key = jax.random.fold_in(key, 5)
    x_frac, z_frac, y_frac = coordinates()
    trend = jnp.exp((0.4 - 1.5 * z_frac + 0.3 * x_frac) * math.log(10.0))
    rough = jnp.exp(jax.random.uniform(own_key, (NX, NZ, NY), jnp.float32, -math.log(2.0), math.log(2.0)))
    return trend * rough


def field_draw(key, magnitude):
    key_phase, key_rough = jax.random.split(key)
    x_frac, z_frac, y_frac = coordinates()
    x_frac = x_frac[None]
    z_frac = z_frac[None]
    y_frac = y_frac[None]
    freq = jnp.arange(FREQS, dtype=jnp.float32)[:, None, None, None]
    phases = jax.random.uniform(key_phase, (3, FREQS, 1, 1, 1), jnp.float32, 0.0, 1.0)
    two_pi = 2.0 * math.pi
    smooth = jnp.sin(two_pi * (2.0 * x_frac + phases[0])) * jnp.sin(two_pi * (1.5 * z_frac + phases[1])) * jnp.cos(two_pi * (3.0 * y_frac + phases[2]))
    shape = (FREQS, NX, NZ, NY)
    envelope = jnp.exp((0.3 * x_frac - (0.5 + 0.3 * freq) * z_frac) * math.log(10.0))
    rough = 0.7 * jax.random.truncated_normal(key_rough, -4.0, 4.0, shape, jnp.float32)
    return magnitude * envelope * (0.8 * smooth + rough)


def draw_initial_field(key, part):
    return field_draw(jax.random.fold_in(key, 11), 0.1)


def draw_adjoint_initial(key, part):
    return field_draw(jax.random.fold_in(key, 23), 0.03)


def touch_ends(entries, rng, low, high):
    longest = entries.shape.index(max(entries.shape))
    spots = []
    for shift in (0, 1):
        where = [jax.random.randint(jax.random.fold_in(rng, axis), (), 0, length) for axis, length in enumerate(entries.shape)]
        where[longest] = (where[longest] + shift) % entries.shape[longest]
        spots.append(tuple(where))
    return entries.at[spots[0]].set(low).at[spots[1]].set(high)


def block_levels(rng, dims, cuts, smallest, high):
    gain = 1.0
    for position, parts in cuts:
        heights = jax.random.uniform(jax.random.fold_in(jax.random.fold_in(rng, 6), position), (parts,), jnp.float32, smallest / len(cuts), high / len(cuts))
        gain = gain * jnp.repeat(jnp.exp(heights), dims[position] // parts).reshape((-1,) + (1,) * (len(dims) - 1 - position))
    return gain


def scatter_about(stream_key, shape, width, bound, cuts=(), kind=jnp.bfloat16):
    drawn = width * jax.random.normal(stream_key, shape, jnp.float32)
    if cuts:
        drawn = drawn * block_levels(stream_key, shape, cuts, -0.22, 0.18)
    return jnp.clip(drawn, -bound, bound).astype(kind)


def setup_inputs(seed: int = 0) -> dict:
    splits = jax.random.split(jax.random.key(seed), 11)
    conductivity = draw_conductivity(jax.random.fold_in(splits[10], 71), 0)
    initial_field = draw_initial_field(jax.random.fold_in(splits[10], 71), 0)
    adjoint_initial = draw_adjoint_initial(jax.random.fold_in(splits[10], 71), 0)
    src_cell = touch_ends(jax.random.randint(splits[3], (N_BRICK, N_DEPTH, NS), 0, CX * CZ * NY), jax.random.fold_in(splits[3], 1), 0, (CX * CZ * NY) - 1).astype(jnp.int32)
    src_amp = scatter_about(splits[4], (N_BRICK, N_DEPTH, FREQS, NS), 4.0, 24.0, ((0, 8), (1, 4)), jnp.float32)
    rec_cell = touch_ends(jax.random.randint(splits[5], (N_BRICK, N_DEPTH, NR), 0, CX * CZ * NY), jax.random.fold_in(splits[5], 1), 0, (CX * CZ * NY) - 1).astype(jnp.int32)
    observed = scatter_about(splits[6], (N_BRICK, N_DEPTH, FREQS, NR), 2.0, 12.0, ((0, 8), (1, 4)), jnp.float32)
    cov_blocks = scatter_about(splits[7], (N_BRICK, N_DEPTH, NNZ, BLOCK, BLOCK), BLOCK ** -0.5, 0.25, ((0, 8), (1, 4)))
    cov_rows = touch_ends(jax.random.randint(splits[8], (N_BRICK, N_DEPTH, NNZ), 0, BLK_DEV), jax.random.fold_in(splits[8], 1), 0, BLK_DEV - 1).astype(jnp.int32)
    cov_cols = touch_ends(jax.random.randint(splits[9], (N_BRICK, N_DEPTH, NNZ), 0, COL_BLOCKS), jax.random.fold_in(splits[9], 1), 0, COL_BLOCKS - 1).astype(jnp.int32)
    return dict(conductivity=conductivity, initial_field=initial_field, adjoint_initial=adjoint_initial, src_cell=src_cell, src_amp=src_amp, rec_cell=rec_cell, observed=observed, cov_blocks=cov_blocks, cov_rows=cov_rows, cov_cols=cov_cols)


LAPLACE_SHIFTS = (0.5, 2.0)


def to_local(volume):
    leading = volume.shape[:-3]
    pieces = volume.reshape(leading + (N_BRICK, CX, N_DEPTH, CZ, NY))
    pieces = jnp.swapaxes(pieces, -4, -3)
    return pieces.reshape(leading + (N_BRICK, N_DEPTH, CX * CZ * NY))


def from_local(flat_cells):
    leading = flat_cells.shape[:-3]
    pieces = flat_cells.reshape(leading + (N_BRICK, N_DEPTH, CX, CZ, NY))
    pieces = jnp.swapaxes(pieces, -4, -3)
    return pieces.reshape(leading + (N_BRICK * CX, N_DEPTH * CZ, NY))


def spread(values):
    return values[:, None, None, None]


def operate(volume, damping):
    padded = jnp.pad(volume, ((0, 0), (1, 1), (1, 1), (1, 1)))
    beside = padded[:, 2:, 1:-1, 1:-1] + padded[:, :-2, 1:-1, 1:-1]
    beside = beside + padded[:, 1:-1, 2:, 1:-1] + padded[:, 1:-1, :-2, 1:-1]
    beside = beside + padded[:, 1:-1, 1:-1, 2:] + padded[:, 1:-1, 1:-1, :-2]
    return (6.0 + damping) * volume - beside


def conjugate(source_term, initial, damping):
    solution = initial
    residual = source_term - operate(initial, damping)
    direction = residual
    norm_now = jnp.sum(residual * residual, axis=(1, 2, 3))
    for iteration in range(ITERS):
        applied = operate(direction, damping)
        step_len = norm_now / jnp.sum(direction * applied, axis=(1, 2, 3))
        solution = solution + spread(step_len) * direction
        residual = residual - spread(step_len) * applied
        if iteration + 1 < ITERS:
            norm_next = jnp.sum(residual * residual, axis=(1, 2, 3))
            direction = residual + spread(norm_next / norm_now) * direction
            norm_now = norm_next
    return solution


def place_points(cells, amounts):
    def one_device(cell_list, amount_list):
        return jnp.zeros((2, CX * CZ * NY), jnp.float32).at[:, cell_list].add(amount_list)

    placed = jax.vmap(jax.vmap(one_device))(cells, amounts)
    return from_local(jnp.moveaxis(placed, 2, 0))


def read_points(volume, cells):
    local_cells = jnp.moveaxis(to_local(volume), 0, 2)

    def one_device(values_here, cell_list):
        return values_here[:, cell_list]

    return jax.vmap(jax.vmap(one_device))(local_cells, cells)


def reference(conductivity, initial_field, adjoint_initial, src_cell, src_amp, rec_cell, observed, cov_blocks, cov_rows, cov_cols):
    shifts = jnp.array(LAPLACE_SHIFTS, jnp.float32)
    damping = spread(shifts) * conductivity[None]
    forward = conjugate(place_points(src_cell, src_amp), initial_field, damping)
    misfit = read_points(forward, rec_cell) - observed
    adjoint = conjugate(place_points(rec_cell, misfit), adjoint_initial, damping)
    gradient = (-jnp.sum(spread(shifts) * forward * adjoint, axis=0)).astype(jnp.bfloat16)
    blocks_dev = CX * CZ * NY // BLOCK
    grad_blocks = to_local(gradient).reshape(N_BRICK, N_DEPTH * blocks_dev, BLOCK)

    def per_brick(operands):
        brick_grad, brick_blocks, brick_rows, brick_cols = operands
        picked = brick_grad[brick_cols]
        terms = jnp.einsum("dkij,dkj->dki", brick_blocks.astype(jnp.float32), picked.astype(jnp.float32), precision=lax.Precision.HIGHEST)
        targets = jnp.arange(N_DEPTH, dtype=jnp.int32)[:, None] * blocks_dev + brick_rows
        return jnp.zeros((N_DEPTH * blocks_dev, BLOCK), jnp.float32).at[targets].add(terms)

    added = lax.map(per_brick, (grad_blocks, cov_blocks, cov_rows, cov_cols))
    combined = grad_blocks.astype(jnp.float32) + added
    preconditioned = from_local(combined.reshape(N_BRICK, N_DEPTH, CX * CZ * NY))
    return forward, preconditioned
```

```python
import jax
import jax.numpy as jnp
from jax import lax
from jax.sharding import PartitionSpec as P

LAPLACE_SHIFTS = (0.5, 2.0)
HX = 6
HC = 5
HA = 4
THETA = 6.0
BOTH = ("brick", "depth")


def spread(values):
    return values[:, None, None, None]


def exchange(to_low, to_high, axis):
    size = lax.axis_size(axis)
    odd = lax.axis_index(axis) % 2 == 1
    first = [(i, i ^ 1) for i in range(size) if (i ^ 1) < size]
    second = [(i, j) for i in range(size) for j in [((i + 1) ^ 1) - 1] if 0 <= j < size]
    got_first = lax.ppermute(jnp.where(odd, to_low, to_high), axis, first)
    got_second = lax.ppermute(jnp.where(odd, to_high, to_low), axis, second)
    from_low = jnp.where(odd, got_first, got_second)
    from_high = jnp.where(odd, got_second, got_first)
    return from_low, from_high


def widen(fields, lists, axis, dim):
    lows = [lax.slice_in_dim(a, 0, w, axis=dim).reshape(-1) for a, w in fields]
    highs = [lax.slice_in_dim(a, a.shape[dim] - w, a.shape[dim], axis=dim).reshape(-1) for a, w in fields]
    flat = lists.reshape(-1)
    from_low, from_high = exchange(jnp.concatenate(lows + [flat]), jnp.concatenate(highs + [flat]), axis)
    out = []
    at = 0
    for a, w in fields:
        shape = list(a.shape)
        shape[dim] = w
        count = 1
        for n in shape:
            count *= n
        before = from_low[at : at + count].reshape(shape)
        after = from_high[at : at + count].reshape(shape)
        out.append(jnp.concatenate([before, a, after], axis=dim))
        at += count
    n = flat.shape[0]
    low_list = from_low[at : at + n].reshape(lists.shape)
    high_list = from_high[at : at + n].reshape(lists.shape)
    return out, (low_list, lists, high_list)


def trim(a, w):
    return a[..., w : a.shape[-3] - w, w : a.shape[-2] - w, :]


def shifted(v, damping, inside):
    c = v[..., 1:-1, 1:-1, :]
    beside = v[..., 2:, 1:-1, :] + v[..., :-2, 1:-1, :] + v[..., 1:-1, 2:, :] + v[..., 1:-1, :-2, :]
    pad = [(0, 0)] * (v.ndim - 1) + [(1, 1)]
    lateral = jnp.pad(c, pad)
    beside = beside + lateral[..., 2:] + lateral[..., :-2]
    return inside * (damping * c - beside)


def coefficients(mu):
    a = [[mu[i + j + 1] + THETA * mu[i + j] for j in range(3)] for i in range(3)]

    def inverse(pivot, size):
        good = pivot > 1e-6 * size
        return jnp.where(good, 1.0 / jnp.where(good, pivot, 1.0), 0.0)

    i0 = inverse(a[0][0], 0.0)
    l10 = a[0][1] * i0
    l20 = a[0][2] * i0
    i1 = inverse(a[1][1] - l10 * a[0][1], a[1][1])
    e21 = a[1][2] - l10 * a[0][2]
    l21 = e21 * i1
    i2 = inverse(a[2][2] - l20 * a[0][2] - l21 * e21, a[2][2])
    y0 = mu[0]
    y1 = mu[1] - l10 * y0
    y2 = mu[2] - l20 * y0 - l21 * y1
    c2 = y2 * i2
    c1 = y1 * i1 - l21 * c2
    c0 = y0 * i0 - l10 * c1 - l20 * c2
    return c0, c1, c2


def local(
    conductivity,
    initial_field,
    adjoint_initial,
    src_cell,
    src_amp,
    rec_cell,
    observed,
    cov_blocks,
    cov_rows,
    cov_cols,
):
    size_x, size_z, size_y = conductivity.shape
    total_cells = size_x * size_z * size_y
    block_size = cov_blocks.shape[-1]
    blocks_here = total_cells // block_size
    shifts = jnp.array(LAPLACE_SHIFTS, jnp.float32)
    n_src = src_cell.shape[-1]
    n_rec = rec_cell.shape[-1]

    table = jnp.concatenate(
        [
            src_cell[0, 0][None].astype(jnp.float32),
            src_amp[0, 0],
            rec_cell[0, 0][None].astype(jnp.float32),
            jnp.ones((1, n_rec), jnp.float32),
            observed[0, 0],
        ]
    )
    fields = [(initial_field, HX), (conductivity[None], HC), (adjoint_initial, HA)]
    wide, lists_x = widen(fields, table, "brick", 1)
    wide = [(a, w) for a, (_, w) in zip(wide, fields)]
    stacked = jnp.stack(lists_x)
    (x0, cond, a0), lists = widen(wide, stacked, "depth", 2)
    lists = jnp.stack(lists)

    def inside_of(axis, size):
        at = lax.axis_index(axis) * size + jnp.arange(size + 2 * HX) - HX
        return ((at >= 0) & (at < lax.axis_size(axis) * size)).astype(jnp.float32)

    inside = inside_of("brick", size_x)[:, None, None] * inside_of("depth", size_z)[None, :, None]
    damping = spread(shifts) * cond

    def split3(v):
        one = lax.reduce_precision(v, 8, 7)
        two = lax.reduce_precision(v - one, 8, 7)
        three = v - one - two
        return jnp.stack([one, two, three]).astype(jnp.bfloat16)

    def place(cells, amounts, halo):
        idx = cells.astype(jnp.int32)
        off = jnp.arange(3) - 1
        ix = idx // (size_z * size_y) + halo + size_x * off[None, :, None]
        iz = (idx // size_y) % size_z + halo + size_z * off[:, None, None]
        iy = (idx % size_y).reshape(-1)
        nx = size_x + 2 * halo
        nz = size_z + 2 * halo
        ok = (ix >= 0) & (ix < nx) & (iz >= 0) & (iz < nz)
        row = jnp.where(ok, ix * nz + iz, -1).reshape(-1)
        rows = (jnp.arange(nx * nz)[:, None] == row[None, :]).astype(jnp.bfloat16)
        cols = iy[:, None] == jnp.arange(size_y)[None, :]
        parts = split3(amounts.reshape(amounts.shape[0], -1))
        right = jnp.where(cols[None, None], parts[..., None], 0)
        placed = jnp.einsum("rp,scpy->crsy", rows, right, preferred_element_type=jnp.float32)
        return jnp.sum(placed, axis=2).reshape(-1, nx, nz, size_y)

    source = place(lists[:, :, 0], jnp.moveaxis(lists[:, :, 1:3], 2, 0), HX - 1)
    placed = place(lists[:, :, 3], jnp.moveaxis(lists[:, :, 4:7], 2, 0), HA - 1)
    many = placed[0]
    obs = placed[1:3]

    def window(a, w):
        return trim(a, HX - w)

    def damp_at(w):
        return trim(damping, HC - w)

    v0 = source - window(inside, HX - 1) * THETA * trim(x0, 1) - shifted(x0, damp_at(5), window(inside, 5))
    v1 = shifted(v0, damp_at(4), window(inside, 4))
    v2 = shifted(v1, damp_at(3), window(inside, 3))
    v3 = shifted(trim(v2, 2), damp_at(0), 1.0)
    own = [trim(v0, 5), trim(v1, 4), trim(v2, 3), v3]

    u0 = many * trim(x0, 3) - obs - window(inside, 3) * THETA * trim(a0, 1) - shifted(a0, damp_at(3), window(inside, 3))
    u = jnp.stack([u0, many * trim(v0, 2), many * trim(v1, 1), many * v2], axis=1)
    w1 = shifted(u, damp_at(2)[:, None], window(inside, 2))
    w2 = shifted(w1, damp_at(1)[:, None], window(inside, 1))
    w3 = shifted(w2, damp_at(0)[:, None], 1.0)
    owna = [trim(u, 3), trim(w1, 2), trim(w2, 1), w3]

    def dot(a, b):
        return jnp.sum(a * b, axis=(-3, -2, -1))

    mu = jnp.stack([dot(own[j // 2], own[j - j // 2]) for j in range(6)])
    pairs = [(k, l) for k in range(4) for l in range(k, 4)]
    gram = jnp.stack(
        [
            jnp.stack([dot(owna[j // 2][:, k], owna[j - j // 2][:, l]) for k, l in pairs])
            for j in range(6)
        ]
    )
    sums = jnp.concatenate([mu.reshape(-1), gram.reshape(-1)])
    count = sums.shape[0]
    lanes = -(-count // 128) * 128
    sums = jnp.pad(sums, (0, lanes - count)).reshape(1, lanes)
    n_dev = lax.axis_size("brick") * lax.axis_size("depth")
    every = lax.all_to_all(jnp.broadcast_to(sums, (n_dev, lanes)), BOTH, 0, 0, tiled=True)
    sums = jnp.sum(every, axis=0)[:count]
    mu = sums[:12].reshape(6, 2)
    gram = sums[12:].reshape(6, len(pairs), 2)
    c = coefficients([mu[j] for j in range(6)])
    g = (1.0,) + c
    nu = []
    for j in range(6):
        total = 0.0
        for i, (k, l) in enumerate(pairs):
            total = total + (1.0 if k == l else 2.0) * g[k] * g[l] * gram[j, i]
        nu.append(total)
    d = coefficients(nu)
    forward = initial_field + sum(spread(c[k]) * own[k] for k in range(3))
    adjoint = adjoint_initial
    for j in range(3):
        level = owna[j][:, 0] + sum(spread(c[k]) * owna[j][:, k + 1] for k in range(3))
        adjoint = adjoint + spread(d[j]) * level

    gradient = (-jnp.sum(spread(shifts) * forward * adjoint, axis=0)).astype(jnp.bfloat16)
    grad_blocks = gradient.reshape(blocks_here, block_size)
    columns = cov_cols[0, 0]
    every_block = lax.all_gather(grad_blocks, "depth", axis=0, tiled=True)
    picked = jnp.take(every_block, columns, axis=0)
    terms = jnp.einsum("kij,kj->ki", cov_blocks[0, 0], picked, preferred_element_type=jnp.float32)
    row_table = (
        jnp.arange(blocks_here, dtype=jnp.int32)[:, None] == cov_rows[0, 0][None, :]
    ).astype(jnp.float32)
    added = jnp.dot(row_table, terms, precision=lax.Precision.HIGHEST)
    preconditioned = (grad_blocks.astype(jnp.float32) + added).reshape(size_x, size_z, size_y)
    return (forward, preconditioned)


def solution(mesh):
    return jax.shard_map(
        local,
        mesh=mesh,
        in_specs=(
            P("brick", "depth", None),
            P(None, "brick", "depth", None),
            P(None, "brick", "depth", None),
            P("brick", "depth", None),
            P("brick", "depth", None, None),
            P("brick", "depth", None),
            P("brick", "depth", None, None),
            P("brick", "depth", None, None, None),
            P("brick", "depth", None),
            P("brick", "depth", None),
        ),
        out_specs=(P(None, "brick", "depth", None), P("brick", "depth", None)),
        check_vma=False,
    )
```

```python
import jax
import jax.numpy as jnp
from jax import lax
from jax.sharding import PartitionSpec as P

LAPLACE_SHIFTS = (0.5, 2.0)
HX = 6
HC = 5
HA = 4
THETA = 6.0
BOTH = ("brick", "depth")


def spread(values):
    return values[:, None, None, None]


def exchange(to_low, to_high, axis):
    size = lax.axis_size(axis)
    odd = lax.axis_index(axis) % 2 == 1
    first = [(i, i ^ 1) for i in range(size) if (i ^ 1) < size]
    second = [(i, j) for i in range(size) for j in [((i + 1) ^ 1) - 1] if 0 <= j < size]
    got_first = lax.ppermute(jnp.where(odd, to_low, to_high), axis, first)
    got_second = lax.ppermute(jnp.where(odd, to_high, to_low), axis, second)
    from_low = jnp.where(odd, got_first, got_second)
    from_high = jnp.where(odd, got_second, got_first)
    return from_low, from_high


def widen(fields, lists, axis, dim):
    lows = [lax.slice_in_dim(a, 0, w, axis=dim).reshape(-1).astype(jnp.bfloat16) for a, w in fields]
    highs = [lax.slice_in_dim(a, a.shape[dim] - w, a.shape[dim], axis=dim).reshape(-1).astype(jnp.bfloat16) for a, w in fields]
    flat = lists.reshape(-1)
    from_low, from_high = exchange(jnp.concatenate(lows + [flat]), jnp.concatenate(highs + [flat]), axis)
    out = []
    at = 0
    for a, w in fields:
        shape = list(a.shape)
        shape[dim] = w
        count = 1
        for n in shape:
            count *= n
        before = from_low[at : at + count].reshape(shape).astype(jnp.float32)
        after = from_high[at : at + count].reshape(shape).astype(jnp.float32)
        out.append(jnp.concatenate([before, a, after], axis=dim))
        at += count
    n = flat.shape[0]
    low_list = from_low[at : at + n].reshape(lists.shape)
    high_list = from_high[at : at + n].reshape(lists.shape)
    return out, (low_list, lists, high_list)


def trim(a, w):
    return a[..., w : a.shape[-3] - w, w : a.shape[-2] - w, :]


def shifted(v, damping, inside):
    c = v[..., 1:-1, 1:-1, :]
    beside = v[..., 2:, 1:-1, :] + v[..., :-2, 1:-1, :] + v[..., 1:-1, 2:, :] + v[..., 1:-1, :-2, :]
    pad = [(0, 0)] * (v.ndim - 1) + [(1, 1)]
    lateral = jnp.pad(c, pad)
    beside = beside + lateral[..., 2:] + lateral[..., :-2]
    return inside * (damping * c - beside)


def coefficients(mu):
    a = [[mu[i + j + 1] + THETA * mu[i + j] for j in range(3)] for i in range(3)]

    def inverse(pivot, size):
        good = pivot > 1e-6 * size
        return jnp.where(good, 1.0 / jnp.where(good, pivot, 1.0), 0.0)

    i0 = inverse(a[0][0], 0.0)
    l10 = a[0][1] * i0
    l20 = a[0][2] * i0
    i1 = inverse(a[1][1] - l10 * a[0][1], a[1][1])
    e21 = a[1][2] - l10 * a[0][2]
    l21 = e21 * i1
    i2 = inverse(a[2][2] - l20 * a[0][2] - l21 * e21, a[2][2])
    y0 = mu[0]
    y1 = mu[1] - l10 * y0
    y2 = mu[2] - l20 * y0 - l21 * y1
    c2 = y2 * i2
    c1 = y1 * i1 - l21 * c2
    c0 = y0 * i0 - l10 * c1 - l20 * c2
    return c0, c1, c2


def local(
    conductivity,
    initial_field,
    adjoint_initial,
    src_cell,
    src_amp,
    rec_cell,
    observed,
    cov_blocks,
    cov_rows,
    cov_cols,
):
    size_x, size_z, size_y = conductivity.shape
    total_cells = size_x * size_z * size_y
    block_size = cov_blocks.shape[-1]
    blocks_here = total_cells // block_size
    shifts = jnp.array(LAPLACE_SHIFTS, jnp.float32)
    n_src = src_cell.shape[-1]
    n_rec = rec_cell.shape[-1]

    def split3(v):
        one = lax.reduce_precision(v, 8, 7)
        two = lax.reduce_precision(v - one, 8, 7)
        three = v - one - two
        return jnp.stack([one, two, three]).astype(jnp.bfloat16)

    def halves(cells):
        return jnp.stack([cells // 256, cells % 256]).astype(jnp.bfloat16)

    table = jnp.concatenate(
        [
            halves(src_cell[0, 0]),
            split3(src_amp[0, 0]).reshape(6, n_src),
            halves(rec_cell[0, 0]),
            jnp.ones((1, n_rec), jnp.bfloat16),
            split3(observed[0, 0]).reshape(6, n_rec),
        ]
    )
    fields = [(initial_field, HX), (conductivity[None], HC), (adjoint_initial, HA)]
    wide, lists_x = widen(fields, table, "brick", 1)
    wide = [(a, w) for a, (_, w) in zip(wide, fields)]
    stacked = jnp.stack(lists_x)
    (x0, cond, a0), lists = widen(wide, stacked, "depth", 2)
    lists = jnp.stack(lists)

    def inside_of(axis, size):
        at = lax.axis_index(axis) * size + jnp.arange(size + 2 * HX) - HX
        return ((at >= 0) & (at < lax.axis_size(axis) * size)).astype(jnp.float32)

    inside = inside_of("brick", size_x)[:, None, None] * inside_of("depth", size_z)[None, :, None]
    damping = spread(shifts) * cond

    def cells_of(pair):
        return pair[:, :, 0].astype(jnp.int32) * 256 + pair[:, :, 1].astype(jnp.int32)

    def joined(six):
        three = six.astype(jnp.float32).reshape(six.shape[:2] + (3, 2, -1))
        return jnp.moveaxis(three[:, :, 0] + three[:, :, 1] + three[:, :, 2], 2, 0)

    def place(cells, amounts, halo):
        idx = cells
        off = jnp.arange(3) - 1
        ix = idx // (size_z * size_y) + halo + size_x * off[None, :, None]
        iz = (idx // size_y) % size_z + halo + size_z * off[:, None, None]
        iy = (idx % size_y).reshape(-1)
        nx = size_x + 2 * halo
        nz = size_z + 2 * halo
        ok = (ix >= 0) & (ix < nx) & (iz >= 0) & (iz < nz)
        row = jnp.where(ok, ix * nz + iz, -1).reshape(-1)
        rows = (jnp.arange(nx * nz)[:, None] == row[None, :]).astype(jnp.bfloat16)
        cols = iy[:, None] == jnp.arange(size_y)[None, :]
        parts = split3(amounts.reshape(amounts.shape[0], -1))
        right = jnp.where(cols[None, None], parts[..., None], 0)
        placed = jnp.einsum("rp,scpy->crsy", rows, right, preferred_element_type=jnp.float32)
        return jnp.sum(placed, axis=2).reshape(-1, nx, nz, size_y)

    source = place(cells_of(lists[:, :, 0:2]), joined(lists[:, :, 2:8]), HX - 1)
    weights = lists[:, :, 10].astype(jnp.float32)[None]
    placed = place(
        cells_of(lists[:, :, 8:10]), jnp.concatenate([weights, joined(lists[:, :, 11:17])]), HA - 1
    )
    many = placed[0]
    obs = placed[1:3]

    def window(a, w):
        return trim(a, HX - w)

    def damp_at(w):
        return trim(damping, HC - w)

    v0 = source - window(inside, HX - 1) * THETA * trim(x0, 1) - shifted(x0, damp_at(5), window(inside, 5))
    v1 = shifted(v0, damp_at(4), window(inside, 4))
    v2 = shifted(v1, damp_at(3), window(inside, 3))
    v3 = shifted(trim(v2, 2), damp_at(0), 1.0)
    own = [trim(v0, 5), trim(v1, 4), trim(v2, 3), v3]

    u0 = many * trim(x0, 3) - obs - window(inside, 3) * THETA * trim(a0, 1) - shifted(a0, damp_at(3), window(inside, 3))
    u = jnp.stack([u0, many * trim(v0, 2), many * trim(v1, 1), many * v2], axis=1)
    w1 = shifted(u, damp_at(2)[:, None], window(inside, 2))
    w2 = shifted(w1, damp_at(1)[:, None], window(inside, 1))
    w3 = shifted(w2, damp_at(0)[:, None], 1.0)
    owna = [trim(u, 3), trim(w1, 2), trim(w2, 1), w3]

    def dot(a, b):
        return jnp.sum(a * b, axis=(-3, -2, -1))

    mu = jnp.stack([dot(own[j // 2], own[j - j // 2]) for j in range(6)])
    pairs = [(k, l) for k in range(4) for l in range(k, 4)]
    gram = jnp.stack(
        [
            jnp.stack([dot(owna[j // 2][:, k], owna[j - j // 2][:, l]) for k, l in pairs])
            for j in range(6)
        ]
    )
    sums = jnp.concatenate([mu.reshape(-1), gram.reshape(-1)])
    count = sums.shape[0]
    lanes = -(-count // 128) * 128
    sums = jnp.pad(sums, (0, lanes - count)).reshape(1, lanes)
    n_dev = lax.axis_size("brick") * lax.axis_size("depth")
    every = lax.all_to_all(jnp.broadcast_to(sums, (n_dev, lanes)), BOTH, 0, 0, tiled=True)
    sums = jnp.sum(every, axis=0)[:count]
    mu = sums[:12].reshape(6, 2)
    gram = sums[12:].reshape(6, len(pairs), 2)
    c = coefficients([mu[j] for j in range(6)])
    g = (1.0,) + c
    nu = []
    for j in range(6):
        total = 0.0
        for i, (k, l) in enumerate(pairs):
            total = total + (1.0 if k == l else 2.0) * g[k] * g[l] * gram[j, i]
        nu.append(total)
    d = coefficients(nu)
    forward = initial_field + sum(spread(c[k]) * own[k] for k in range(3))
    adjoint = adjoint_initial
    for j in range(3):
        level = owna[j][:, 0] + sum(spread(c[k]) * owna[j][:, k + 1] for k in range(3))
        adjoint = adjoint + spread(d[j]) * level

    gradient = (-jnp.sum(spread(shifts) * forward * adjoint, axis=0)).astype(jnp.bfloat16)
    grad_blocks = gradient.reshape(blocks_here, block_size)
    columns = cov_cols[0, 0]
    every_block = lax.all_gather(grad_blocks, "depth", axis=0, tiled=True)
    picked = jnp.take(every_block, columns, axis=0)
    terms = jnp.einsum("kij,kj->ki", cov_blocks[0, 0], picked, preferred_element_type=jnp.float32)
    row_table = (
        jnp.arange(blocks_here, dtype=jnp.int32)[:, None] == cov_rows[0, 0][None, :]
    ).astype(jnp.float32)
    added = jnp.dot(row_table, terms, precision=lax.Precision.HIGHEST)
    preconditioned = (grad_blocks.astype(jnp.float32) + added).reshape(size_x, size_z, size_y)
    return (forward, preconditioned)


def solution(mesh):
    return jax.shard_map(
        local,
        mesh=mesh,
        in_specs=(
            P("brick", "depth", None),
            P(None, "brick", "depth", None),
            P(None, "brick", "depth", None),
            P("brick", "depth", None),
            P("brick", "depth", None, None),
            P("brick", "depth", None),
            P("brick", "depth", None, None),
            P("brick", "depth", None, None, None),
            P("brick", "depth", None),
            P("brick", "depth", None),
        ),
        out_specs=(P(None, "brick", "depth", None), P("brick", "depth", None)),
        check_vma=False,
    )
```

```python
import functools

import jax
import jax.numpy as jnp
from jax import lax
from jax.experimental import pallas as pl
from jax.experimental.pallas import tpu as pltpu
from jax.sharding import PartitionSpec as P

LAPLACE_SHIFTS = (0.5, 2.0)
HX = 6
HC = 5
HA = 4
HU = 3
ZP = 8
THETA = 6.0
BOTH = ("brick", "depth")
PAIRS = tuple((k, l) for k in range(4) for l in range(k, 4))
VMEM = pl.BlockSpec(memory_space=pltpu.VMEM)
SMEM = pl.BlockSpec(memory_space=pltpu.SMEM)
NT = (((1,), (1,)), ((), ()))


def exchange(to_low, to_high, axis):
    size = lax.axis_size(axis)
    odd = lax.axis_index(axis) % 2 == 1
    first = [(i, i ^ 1) for i in range(size) if (i ^ 1) < size]
    second = [(i, j) for i in range(size) for j in [((i + 1) ^ 1) - 1] if 0 <= j < size]
    got_first = lax.ppermute(jnp.where(odd, to_low, to_high), axis, first)
    got_second = lax.ppermute(jnp.where(odd, to_high, to_low), axis, second)
    from_low = jnp.where(odd, got_first, got_second)
    from_high = jnp.where(odd, got_second, got_first)
    return from_low, from_high


def widen(fields, lists, axis, dim):
    lows = [lax.slice_in_dim(a, 0, w, axis=dim).reshape(-1).astype(jnp.bfloat16) for a, w in fields]
    highs = [lax.slice_in_dim(a, a.shape[dim] - w, a.shape[dim], axis=dim).reshape(-1).astype(jnp.bfloat16) for a, w in fields]
    flat = lists.reshape(-1)
    from_low, from_high = exchange(jnp.concatenate(lows + [flat]), jnp.concatenate(highs + [flat]), axis)
    out = []
    at = 0
    for a, w in fields:
        shape = list(a.shape)
        shape[dim] = w
        count = 1
        for n in shape:
            count *= n
        before = from_low[at : at + count].reshape(shape).astype(jnp.float32)
        after = from_high[at : at + count].reshape(shape).astype(jnp.float32)
        out.append(jnp.concatenate([before, a, after], axis=dim))
        at += count
    n = flat.shape[0]
    low_list = from_low[at : at + n].reshape(lists.shape)
    high_list = from_high[at : at + n].reshape(lists.shape)
    return out, (low_list, lists, high_list)


def beside_z_y(c):
    rows, width = c.shape
    half = width // 2
    total = pltpu.roll(c, 1, 0) + pltpu.roll(c, rows - 1, 0)
    lane = lax.broadcasted_iota(jnp.int32, (rows, half), 1)
    first = lane == 0
    last = lane == half - 1
    a, b = c[:, :half], c[:, half:]
    ra, rb = pltpu.roll(a, 1, 1), pltpu.roll(b, 1, 1)
    la, lb = pltpu.roll(a, half - 1, 1), pltpu.roll(b, half - 1, 1)
    ya = jnp.where(first, 0.0, ra) + jnp.where(last, lb, la)
    yb = jnp.where(first, ra, rb) + jnp.where(last, 0.0, lb)
    return total + jnp.concatenate([ya, yb], axis=1)


def chain_kernel(size_x, size_z, edges, x0, cond, a0, lists, v_out, w_out, sums_out,
                 src, rec, v0, v1, v2, u, w1, w2, w3, acc):
    rows_z = x0.shape[-2]
    size_y = x0.shape[-1]
    n_list = lists.shape[-1] // 3
    each = n_list // 4
    own = slice(ZP, ZP + size_z)

    lane = lax.broadcasted_iota(jnp.int32, (1, n_list), 1)
    dx = jnp.where(lane < each, -1, jnp.where(lane < 2 * each, 0, 1))

    def place(t, q, weights, halo, dst):
        nx = size_x + 2 * halo
        at = slice(t * n_list, (t + 1) * n_list)
        hi = lists[q : q + 1, at] - 1.0
        lo = lists[q + 1 : q + 2, at].astype(jnp.int32)
        x = jnp.floor((hi + 0.5) * (1.0 / size_z))
        z = (hi - x * size_z).astype(jnp.int32)
        row_x = x.astype(jnp.int32) + halo + size_x * dx
        ok = (hi >= 0.0) & (row_x >= 0) & (row_x < nx)
        if t == 1:
            depth, z0 = size_z, ZP
            target = row_x * size_z + z
        elif t == 0:
            depth, z0 = ZP, 0
            target = row_x * ZP + z - (size_z - ZP)
            ok = ok & (z >= size_z - ZP)
        else:
            depth, z0 = ZP, ZP + size_z
            target = row_x * ZP + z
            ok = ok & (z < ZP)
        target = jnp.where(ok, target, -1)
        hit = lax.broadcasted_iota(jnp.int32, (nx * depth, n_list), 0) == target
        right = (lax.broadcasted_iota(jnp.int32, (size_y, n_list), 0) == lo).astype(jnp.float32).astype(jnp.bfloat16)
        for at_out, parts in weights:
            total = None
            for p in parts:
                amount = 1.0 if p is None else lists[p : p + 1, at]
                left = jnp.where(hit, amount, 0.0).astype(jnp.bfloat16)
                d = lax.dot_general(left, right, NT, preferred_element_type=jnp.float32)
                total = d if total is None else total + d
            dst[at_out, :, z0 : z0 + depth, :] = total.reshape(nx, depth, size_y)

    for t in range(3):
        place(t, 0, ((0, (2, 4, 6)), (1, (3, 5, 7))), HC, src)
        place(t, 8, ((0, (10, 12, 14)), (1, (11, 13, 15)), (2, (None,))), HU, rec)

    row = lax.broadcasted_iota(jnp.int32, (rows_z, size_y), 0)
    in_z = jnp.where(row < ZP, edges[2], jnp.where(row >= ZP + size_z, edges[3], 1.0))

    def mask(i, halo):
        return in_z * jnp.where(i < halo, edges[0], jnp.where(i >= halo + size_x, edges[1], 1.0))

    def apply(ref, idx, i, damp):
        c = ref[idx + (i,)]
        return damp * c - (ref[idx + (i - 1,)] + ref[idx + (i + 1,)] + beside_z_y(c))

    def loop(n, body):
        def step(i, carry):
            body(i)
            return carry
        lax.fori_loop(0, n, step, 0)

    def first(i):
        m = mask(i, HC)
        for f, s in enumerate(LAPLACE_SHIFTS):
            v0[f, i] = m * (src[f, i] - apply(x0, (f,), i + 1, s * cond[i] + THETA))

    loop(size_x + 2 * HC, first)

    def second(i):
        m = mask(i, 4)
        for f, s in enumerate(LAPLACE_SHIFTS):
            v1[f, i] = m * apply(v0, (f,), i + 1, s * cond[i + 1])

    loop(size_x + 8, second)

    def third(i):
        m = mask(i, 3)
        for f, s in enumerate(LAPLACE_SHIFTS):
            v2[f, i] = m * apply(v1, (f,), i + 1, s * cond[i + 2])

    loop(size_x + 6, third)

    def start(i):
        m = mask(i, HU)
        many = rec[2, i]
        for f, s in enumerate(LAPLACE_SHIFTS):
            u[0, f, i] = m * (many * x0[f, i + 3] - rec[f, i] - apply(a0, (f,), i + 1, s * cond[i + 2] + THETA))
            u[1, f, i] = many * v0[f, i + 2]
            u[2, f, i] = many * v1[f, i + 1]
            u[3, f, i] = many * v2[f, i]

    loop(size_x + 2 * HU, start)

    def level(src_ref, dst_ref, halo):
        def body(i):
            m = mask(i, halo)
            for f, s in enumerate(LAPLACE_SHIFTS):
                damp = s * cond[i + HC - halo]
                for k in range(4):
                    dst_ref[k, f, i] = m * apply(src_ref, (k, f), i + 1, damp)
        loop(size_x + 2 * halo, body)

    level(u, w1, 2)
    level(w1, w2, 1)

    def last(i):
        for f, s in enumerate(LAPLACE_SHIFTS):
            damp = s * cond[i + HC]
            for k in range(4):
                w3[k, f, i] = apply(w2, (k, f), i + 1, damp)[own]

    loop(size_x, last)

    def tiles(a):
        total = None
        for z in range(0, a.shape[0], 8):
            for y in range(0, a.shape[1], 128):
                t = a[z : z + 8, y : y + 128]
                total = t if total is None else total + t
        return total

    zero = jnp.zeros((8, 128), jnp.float32)
    for f, s in enumerate(LAPLACE_SHIFTS):
        def forward_sums(i, carry, f=f, s=s):
            p0 = v0[f, i + 5, own]
            p1 = v1[f, i + 4, own]
            p2 = v2[f, i + 3, own]
            p3 = apply(v2, (f,), i + 3, s * cond[i + 5])[own]
            v_out[0, f, i] = p0
            v_out[1, f, i] = p1
            v_out[2, f, i] = p2
            made = (p0 * p0, p0 * p1, p1 * p1, p1 * p2, p2 * p2, p2 * p3)
            return tuple(c + tiles(a) for c, a in zip(carry, made))
        done = lax.fori_loop(0, size_x, forward_sums, (zero,) * 6)
        for j in range(6):
            acc[j * 2 + f] = done[j]

    levels = ((u, 3, own), (w1, 2, own), (w2, 1, own), (w3, 0, slice(0, size_z)))
    for j in range(6):
        ra, oa, za = levels[j // 2]
        rb, ob, zb = levels[j - j // 2]
        for f in range(2):
            def pair_sums(i, carry, f=f, j=j):
                a = [ra[k, f, i + oa, za] for k in range(4)]
                b = a if j % 2 == 0 else [rb[k, f, i + ob, zb] for k in range(4)]
                if j % 2 == 0:
                    for k in range(4):
                        w_out[j // 2, k, f, i] = a[k]
                return tuple(c + tiles(a[k] * b[l]) for c, (k, l) in zip(carry, PAIRS))
            done = lax.fori_loop(0, size_x, pair_sums, (zero,) * len(PAIRS))
            for n in range(len(PAIRS)):
                acc[12 + (j * len(PAIRS) + n) * 2 + f] = done[n]

    count = acc.shape[0]
    for n in range(12 + 12 * len(PAIRS), count):
        acc[n] = zero
    by_lane = jnp.sum(acc[...], axis=1)
    ones = jnp.ones((8, 128), jnp.float32)
    out = lax.dot_general(ones, by_lane, NT, precision=lax.Precision.HIGHEST, preferred_element_type=jnp.float32)
    sums_out[...] = jnp.broadcast_to(out[0:1][None], sums_out.shape)


def chain(edges, x0, cond, a0, lists, size_x, size_z, n_dev):
    f, _, rows_z, size_y = x0.shape
    f32 = jnp.float32
    slab = (rows_z, size_y)
    outs = (
        jax.ShapeDtypeStruct((3, 2, size_x, size_z, size_y), f32),
        jax.ShapeDtypeStruct((3, 4, 2, size_x, size_z, size_y), f32),
        jax.ShapeDtypeStruct((n_dev, 1, 256), f32),
    )
    scratch = [
        pltpu.VMEM((2, size_x + 2 * HC) + slab, f32),
        pltpu.VMEM((3, size_x + 2 * HU) + slab, f32),
        pltpu.VMEM((2, size_x + 2 * HC) + slab, f32),
        pltpu.VMEM((2, size_x + 8) + slab, f32),
        pltpu.VMEM((2, size_x + 6) + slab, f32),
        pltpu.VMEM((4, 2, size_x + 6) + slab, f32),
        pltpu.VMEM((4, 2, size_x + 4) + slab, f32),
        pltpu.VMEM((4, 2, size_x + 2) + slab, f32),
        pltpu.VMEM((4, 2, size_x, size_z, size_y), f32),
        pltpu.VMEM((256, 8, 128), f32),
    ]
    return pl.pallas_call(
        functools.partial(chain_kernel, size_x, size_z),
        out_shape=outs,
        in_specs=[SMEM, VMEM, VMEM, VMEM, VMEM],
        out_specs=(VMEM, VMEM, VMEM),
        scratch_shapes=scratch,
        name="chain",
    )(edges, x0, cond, a0, lists)


def combine_kernel(coef, x0, a0, v, w, forward, gradient):
    total = None
    for f, s in enumerate(LAPLACE_SHIFTS):
        field = x0[f]
        for k in range(3):
            field = field + coef[f, k] * v[k, f]
        other = a0[f]
        for j in range(3):
            for k in range(4):
                other = other + coef[f, 3 + 4 * j + k] * w[j, k, f]
        forward[f] = field
        part = s * field * other
        total = part if total is None else total + part
    gradient[...] = (-total).reshape(gradient.shape).astype(gradient.dtype)


def combine(coef, x0, a0, v, w):
    _, size_x, size_z, size_y = x0.shape
    return pl.pallas_call(
        combine_kernel,
        out_shape=(
            jax.ShapeDtypeStruct(x0.shape, jnp.float32),
            jax.ShapeDtypeStruct((size_x * size_z, size_y), jnp.bfloat16),
        ),
        in_specs=[SMEM, VMEM, VMEM, VMEM, VMEM],
        out_specs=(VMEM, VMEM),
        name="combine",
    )(coef, x0, a0, v, w)


def covariance_kernel(rows, cols, every, own, blocks, out, wide):
    n_dev, n_rows, width = every.shape
    per = blocks.shape[-1] // width
    for d in range(n_dev):
        wide[d * n_rows : (d + 1) * n_rows, :] = every[d].astype(jnp.float32)
    out[...] = own[...].astype(jnp.float32)
    for k in range(blocks.shape[0]):
        picked = jnp.concatenate([wide[pl.ds(cols[k] * per + i, 1), :] for i in range(per)], axis=1)
        picked = jnp.broadcast_to(picked, (16, picked.shape[1])).astype(jnp.bfloat16)
        term = lax.dot_general(picked, blocks[k], NT, preferred_element_type=jnp.float32)[0:1]
        for i in range(per):
            at = pl.ds(rows[k] * per + i, 1)
            out[at, :] = out[at, :] + term[:, i * width : (i + 1) * width]


def covariance(rows, cols, every, own, blocks):
    n_dev, n_rows, width = every.shape
    return pl.pallas_call(
        covariance_kernel,
        out_shape=jax.ShapeDtypeStruct((n_rows, width), jnp.float32),
        in_specs=[SMEM, SMEM, VMEM, VMEM, VMEM],
        out_specs=VMEM,
        scratch_shapes=[pltpu.VMEM((n_dev * n_rows, width), jnp.float32)],
        name="covariance",
    )(rows, cols, every, own, blocks)


def coefficients(mu):
    a = [[mu[i + j + 1] + THETA * mu[i + j] for j in range(3)] for i in range(3)]

    def inverse(pivot, size):
        good = pivot > 1e-6 * size
        return jnp.where(good, 1.0 / jnp.where(good, pivot, 1.0), 0.0)

    i0 = inverse(a[0][0], 0.0)
    l10 = a[0][1] * i0
    l20 = a[0][2] * i0
    i1 = inverse(a[1][1] - l10 * a[0][1], a[1][1])
    e21 = a[1][2] - l10 * a[0][2]
    l21 = e21 * i1
    i2 = inverse(a[2][2] - l20 * a[0][2] - l21 * e21, a[2][2])
    y0 = mu[0]
    y1 = mu[1] - l10 * y0
    y2 = mu[2] - l20 * y0 - l21 * y1
    c2 = y2 * i2
    c1 = y1 * i1 - l21 * c2
    c0 = y0 * i0 - l10 * c1 - l20 * c2
    return c0, c1, c2


def local(
    conductivity,
    initial_field,
    adjoint_initial,
    src_cell,
    src_amp,
    rec_cell,
    observed,
    cov_blocks,
    cov_rows,
    cov_cols,
):
    size_x, size_z, size_y = conductivity.shape
    n_src = src_cell.shape[-1]
    n_rec = rec_cell.shape[-1]

    def split3(v):
        one = lax.reduce_precision(v, 8, 7)
        two = lax.reduce_precision(v - one, 8, 7)
        three = v - one - two
        return jnp.stack([one, two, three]).astype(jnp.bfloat16)

    def halves(cells):
        return jnp.stack([cells // size_y + 1, cells % size_y]).astype(jnp.bfloat16)

    table = jnp.concatenate(
        [
            halves(src_cell[0, 0]),
            split3(src_amp[0, 0]).reshape(6, n_src),
            halves(rec_cell[0, 0]),
            split3(observed[0, 0]).reshape(6, n_rec),
        ]
    )
    fields = [(initial_field, HX), (conductivity[None], HC), (adjoint_initial, HA)]
    wide, lists_x = widen(fields, table, "brick", 1)
    wide = [(a, ZP) for a in wide]
    stacked = jnp.concatenate(lists_x + (jnp.zeros_like(table),), axis=1)
    (x0, cond, a0), lists = widen(wide, stacked, "depth", 2)
    lists = jnp.concatenate(lists, axis=1).astype(jnp.float32)

    def edge(axis):
        at = lax.axis_index(axis)
        return [at > 0, at < lax.axis_size(axis) - 1]

    edges = jnp.stack(edge("brick") + edge("depth")).astype(jnp.float32)
    n_dev = lax.axis_size("brick") * lax.axis_size("depth")
    own, owna, sums = chain(edges, x0, cond[0], a0, lists, size_x, size_z, n_dev)
    every = lax.all_to_all(sums, BOTH, 0, 0, tiled=True)
    sums = jnp.sum(every, axis=(0, 1))
    mu = sums[:12].reshape(6, 2)
    gram = sums[12 : 12 + 12 * len(PAIRS)].reshape(6, len(PAIRS), 2)
    c = coefficients([mu[j] for j in range(6)])
    g = (jnp.ones_like(c[0]),) + c
    nu = []
    for j in range(6):
        total = 0.0
        for i, (k, l) in enumerate(PAIRS):
            total = total + (1.0 if k == l else 2.0) * g[k] * g[l] * gram[j, i]
        nu.append(total)
    d = coefficients(nu)
    coef = jnp.stack(list(c) + [d[j] * g[k] for j in range(3) for k in range(4)], axis=1)
    forward, gradient = combine(coef, initial_field, adjoint_initial, own, owna)
    every_block = lax.all_gather(gradient, "depth", axis=0, tiled=False)
    out = covariance(cov_rows[0, 0], cov_cols[0, 0], every_block, gradient, cov_blocks[0, 0])
    return (forward, out.reshape(size_x, size_z, size_y))


def solution(mesh):
    return jax.shard_map(
        local,
        mesh=mesh,
        in_specs=(
            P("brick", "depth", None),
            P(None, "brick", "depth", None),
            P(None, "brick", "depth", None),
            P("brick", "depth", None),
            P("brick", "depth", None, None),
            P("brick", "depth", None),
            P("brick", "depth", None, None),
            P("brick", "depth", None, None, None),
            P("brick", "depth", None),
            P("brick", "depth", None),
        ),
        out_specs=(P(None, "brick", "depth", None), P("brick", "depth", None)),
        check_vma=False,
    )
```

```python
import functools

import jax
import jax.numpy as jnp
from jax import lax
from jax.experimental import pallas as pl
from jax.experimental.pallas import tpu as pltpu
from jax.sharding import PartitionSpec as P

LAPLACE_SHIFTS = (0.5, 2.0)
BOTH = ("brick", "depth")
HX = 6
HC = 5
HA = 4
HU = 3
ZP = 8
THETA = 6.0
PAIRS = tuple((k, l) for k in range(4) for l in range(k, 4))
SLOTS = 32
VMEM = pl.BlockSpec(memory_space=pltpu.VMEM)
SMEM = pl.BlockSpec(memory_space=pltpu.SMEM)
ANY = pl.BlockSpec(memory_space=pl.ANY)
NT = (((1,), (1,)), ((), ()))
PARAMS = pltpu.CompilerParams(vmem_limit_bytes=28 * 1024 * 1024)


def held(a):
    return pltpu.with_memory_space_constraint(a, pltpu.VMEM)


def is_odd(axis):
    return lax.rem(lax.axis_index(axis), 2) == 1


def pairings(axis):
    size = lax.axis_size(axis)
    first = [(i, i ^ 1) for i in range(size) if (i ^ 1) < size]
    second = [(i, j) for i in range(size) for j in [((i + 1) ^ 1) - 1] if 0 <= j < size]
    return first, second


def swap(first, second, axis):
    one, two = pairings(axis)
    return lax.ppermute(first, axis, one), lax.ppermute(second, axis, two)


LX, LC, LA = 0, 2 * HX, 2 * HX + HC
LP = LA + 2 * HA


def pack_kernel(x0, cond, a0, src_cell, src_amp, rec_cell, observed, first, second, table):
    size_x, _, size_y = cond.shape
    odd = is_odd("brick")

    def split(v):
        one = v.astype(jnp.bfloat16).astype(jnp.float32)
        two = (v - one).astype(jnp.bfloat16).astype(jnp.float32)
        return one, two, v - one - two

    table[...] = jnp.zeros_like(table)
    for base, cells, amounts in ((0, src_cell, src_amp), (8, rec_cell, observed)):
        n = cells.shape[-1]
        at = cells[...].astype(jnp.float32)
        hi = jnp.floor((at + 0.5) * (1.0 / size_y))
        table[base : base + 1, :n] = hi + 1.0
        table[base + 1 : base + 2, :n] = at - hi * size_y
        for s, part in enumerate(split(amounts[...])):
            table[base + 2 + 2 * s : base + 4 + 2 * s, :n] = part
    points = table[...].astype(jnp.bfloat16)
    for out, low in ((first, odd), (second, jnp.logical_not(odd))):
        for f in range(2):
            for i in range(HX):
                out[LX + f * HX + i] = x0[f, jnp.where(low, i, size_x - HX + i)].astype(jnp.bfloat16)
            for i in range(HA):
                out[LA + f * HA + i] = a0[f, jnp.where(low, i, size_x - HA + i)].astype(jnp.bfloat16)
        for i in range(HC):
            out[LC + i] = cond[jnp.where(low, i, size_x - HC + i)].astype(jnp.bfloat16)
        out[LP] = points


def pack(x0, cond, a0, src_cell, src_amp, rec_cell, observed):
    shape = (LP + 1,) + cond.shape[1:]
    return pl.pallas_call(
        pack_kernel,
        out_shape=(jax.ShapeDtypeStruct(shape, jnp.bfloat16),) * 2,
        in_specs=[VMEM] * 7,
        out_specs=(VMEM, VMEM),
        scratch_shapes=[pltpu.VMEM(cond.shape[1:], jnp.float32)],
        compiler_params=PARAMS,
        name="pack",
    )(x0, cond, a0, src_cell, src_amp, rec_cell, observed)


def joined_rows(x0, cond, a0, first, second):
    size_x = cond.shape[0]
    odd = is_odd("brick")

    def low(at):
        return jnp.where(odd, first[at].astype(jnp.float32), second[at].astype(jnp.float32))

    def high(at):
        return jnp.where(odd, second[at].astype(jnp.float32), first[at].astype(jnp.float32))

    def reader(own, base, halo):
        def row(i):
            if i < halo:
                return low(base + i)
            if i >= halo + size_x:
                return high(base + i - halo - size_x)
            return own(i - halo)
        return row

    fields = [reader(lambda i, f=f: x0[f, i], LX + f * HX, HX) for f in range(2)]
    adjoints = [reader(lambda i, f=f: a0[f, i], LA + f * HA, HA) for f in range(2)]
    return fields, reader(lambda i: cond[i], LC, HC), adjoints, low, high


def mid_kernel(x0, cond, a0, sent, first, second, out_first, out_second):
    size_x, size_z, size_y = cond.shape
    fields, conds, adjoints, low, high = joined_rows(x0, cond, a0, first, second)
    odd = is_odd("depth")
    n = size_y // 4
    points = low(LP) + pltpu.roll(sent[LP].astype(jnp.float32), n, 1) + pltpu.roll(high(LP), 2 * n, 1)

    def put(at, down, up):
        down = jnp.concatenate(down, axis=0)
        up = jnp.concatenate(up, axis=0)
        out_first[at] = jnp.where(odd, down, up).astype(jnp.bfloat16)
        out_second[at] = jnp.where(odd, up, down).astype(jnp.bfloat16)

    at = 0
    for i in range(1, size_x + 2 * HX - 1):
        rows = [r(i) for r in fields]
        put(at, [r[:ZP] for r in rows], [r[size_z - ZP :] for r in rows])
        at += 1
    for i in range(1, size_x + 2 * HC - 1, 2):
        rows = [conds(i), conds(i + 1)]
        put(at, [r[:ZP] for r in rows], [r[size_z - ZP :] for r in rows])
        at += 1
    for i in range(1, size_x + 2 * HA - 1, 2):
        rows = [r(j) for j in (i, i + 1) for r in adjoints]
        put(at, [r[:HA] for r in rows], [r[size_z - HA :] for r in rows])
        at += 1
    out_first[at] = points.astype(jnp.bfloat16)
    out_second[at] = points.astype(jnp.bfloat16)


def depth_layers(size_x):
    return (size_x + 2 * HX - 2) + (size_x + 2 * HC - 2) // 2 + (size_x + 2 * HA - 2) // 2 + 1


def mid(x0, cond, a0, sent, first, second):
    size_x, size_z, size_y = cond.shape
    shape = (depth_layers(size_x), size_z, size_y)
    return pl.pallas_call(
        mid_kernel,
        out_shape=(jax.ShapeDtypeStruct(shape, jnp.bfloat16),) * 2,
        in_specs=[VMEM] * 6,
        out_specs=(VMEM, VMEM),
        compiler_params=PARAMS,
        name="mid",
    )(x0, cond, a0, sent, first, second)


def place(t, q, weights, halo, dst, lists, size_x, size_z, size_y):
    n_list = lists.shape[-1]
    each = n_list // 4
    lane = lax.broadcasted_iota(jnp.int32, (1, n_list), 1)
    dx = jnp.where(lane < each, -1, jnp.where(lane < 2 * each, 0, 1))
    nx = size_x + 2 * halo
    hi = lists[q : q + 1] - 1.0
    lo = lists[q + 1 : q + 2].astype(jnp.int32)
    x = jnp.floor((hi + 0.5) * (1.0 / size_z))
    z = (hi - x * size_z).astype(jnp.int32)
    row_x = x.astype(jnp.int32) + halo + size_x * dx
    ok = (hi >= 0.0) & (row_x >= 0) & (row_x < nx)
    if t == 1:
        depth, z0 = size_z, ZP
        target = row_x * size_z + z
    elif t == 0:
        depth, z0 = ZP, 0
        target = row_x * ZP + z - (size_z - ZP)
        ok = ok & (z >= size_z - ZP)
    else:
        depth, z0 = ZP, ZP + size_z
        target = row_x * ZP + z
        ok = ok & (z < ZP)
    target = jnp.where(ok, target, -1)
    hit = lax.broadcasted_iota(jnp.int32, (nx * depth, n_list), 0) == target
    right = (lax.broadcasted_iota(jnp.int32, (size_y, n_list), 0) == lo).astype(jnp.float32).astype(jnp.bfloat16)
    for at_out, parts in weights:
        total = None
        for p in parts:
            amount = 1.0 if p is None else lists[p : p + 1]
            left = jnp.where(hit, amount, 0.0).astype(jnp.bfloat16)
            d = lax.dot_general(left, right, NT, preferred_element_type=jnp.float32)
            total = d if total is None else total + d
        dst[at_out, :, z0 : z0 + depth, :] = total.reshape(nx, depth, size_y)


SRC_WEIGHTS = ((0, (2, 4, 6)), (1, (3, 5, 7)))
REC_WEIGHTS = ((0, (10, 12, 14)), (1, (11, 13, 15)), (2, (None,)))


def prep_kernel(x0, cond, a0, sent2, first, second, x0_w, cond_w, a0_w, src, rec):
    size_x, size_z, size_y = cond.shape
    fields, conds, adjoints, _, _ = joined_rows(x0, cond, a0, first, second)
    own = slice(ZP, ZP + size_z)
    for f in range(2):
        for i in range(size_x + 2 * HX):
            x0_w[f, i, own] = fields[f](i)
        for i in range(size_x + 2 * HA):
            a0_w[f, i, own] = adjoints[f](i)
    for i in range(size_x + 2 * HC):
        cond_w[i, own] = conds(i)
    lists = sent2[sent2.shape[0] - 1].astype(jnp.float32)
    place(1, 0, SRC_WEIGHTS, HC, src, lists, size_x, size_z, size_y)
    place(1, 8, REC_WEIGHTS, HU, rec, lists, size_x, size_z, size_y)


def wide_shapes(size_x, size_z, size_y):
    slab = (size_z + 2 * ZP, size_y)
    return (
        (2, size_x + 2 * HX) + slab,
        (size_x + 2 * HC,) + slab,
        (2, size_x + 2 * HA) + slab,
        (2, size_x + 2 * HC) + slab,
        (3, size_x + 2 * HU) + slab,
    )


def prep(x0, cond, a0, sent2, first, second):
    shapes = wide_shapes(*cond.shape)
    return pl.pallas_call(
        prep_kernel,
        out_shape=tuple(pltpu.VMEM(s, jnp.float32) for s in shapes),
        in_specs=[VMEM] * 6,
        out_specs=(VMEM,) * 5,
        compiler_params=PARAMS,
        name="prep",
    )(x0, cond, a0, sent2, first, second)


def beside_z_y(c):
    rows, width = c.shape
    half = width // 2
    total = pltpu.roll(c, 1, 0) + pltpu.roll(c, rows - 1, 0)
    lane = lax.broadcasted_iota(jnp.int32, (rows, half), 1)
    first = lane == 0
    last = lane == half - 1
    a, b = c[:, :half], c[:, half:]
    ra, rb = pltpu.roll(a, 1, 1), pltpu.roll(b, 1, 1)
    la, lb = pltpu.roll(a, half - 1, 1), pltpu.roll(b, half - 1, 1)
    ya = jnp.where(first, 0.0, ra) + jnp.where(last, lb, la)
    yb = jnp.where(first, ra, rb) + jnp.where(last, 0.0, lb)
    return total + jnp.concatenate([ya, yb], axis=1)


def chain_kernel(size_x, size_z, x0_in, cond_in, a0_in, src_in, rec_in, first, second, blocks,
                 x0, cond, a0, src, rec, v_out, w_out, sums_out, blocks_out,
                 v0, v1, v2, u, w1, w2, w3, acc, sem):
    prefetch = pltpu.make_async_copy(blocks, blocks_out, sem)
    prefetch.start()
    rows_z = x0.shape[-2]
    size_y = x0.shape[-1]
    own = slice(ZP, ZP + size_z)
    top = ZP + size_z

    odd = is_odd("depth")

    def low(at):
        return jnp.where(odd, first[at].astype(jnp.float32), second[at].astype(jnp.float32))

    def high(at):
        return jnp.where(odd, second[at].astype(jnp.float32), first[at].astype(jnp.float32))

    blank = jnp.zeros((ZP, size_y), jnp.float32)
    gap = jnp.zeros((ZP - HA, size_y), jnp.float32)
    at = 0
    for i in range(1, size_x + 2 * HX - 1):
        a, b = low(at), high(at)
        for f in range(2):
            x0[f, i, 0:ZP] = a[f * ZP : (f + 1) * ZP]
            x0[f, i, top : top + ZP] = b[f * ZP : (f + 1) * ZP]
        at += 1
    for i in range(1, size_x + 2 * HC - 1, 2):
        a, b = low(at), high(at)
        for j in range(2):
            cond[i + j, 0:ZP] = a[j * ZP : (j + 1) * ZP]
            cond[i + j, top : top + ZP] = b[j * ZP : (j + 1) * ZP]
        at += 1
    for i in range(1, size_x + 2 * HA - 1, 2):
        a, b = low(at), high(at)
        for j in range(2):
            for f in range(2):
                part = slice((2 * j + f) * HA, (2 * j + f + 1) * HA)
                a0[f, i + j, 0:ZP] = jnp.concatenate([gap, a[part]], axis=0)
                a0[f, i + j, top : top + ZP] = jnp.concatenate([b[part], gap], axis=0)
        at += 1
    for ref, lead in ((x0, 2), (cond, 0), (a0, 2)):
        n = ref.shape[-3]
        for i in (0, n - 1):
            for z in (slice(0, ZP), slice(top, top + ZP)):
                if lead:
                    for f in range(lead):
                        ref[f, i, z] = blank
                else:
                    ref[i, z] = blank
    for t, lists in ((0, low(at)), (2, high(at))):
        place(t, 0, SRC_WEIGHTS, HC, src, lists, size_x, size_z, size_y)
        place(t, 8, REC_WEIGHTS, HU, rec, lists, size_x, size_z, size_y)

    def edge(axis):
        at = lax.axis_index(axis)
        return (at > 0).astype(jnp.float32), (at < lax.axis_size(axis) - 1).astype(jnp.float32)

    low_x, high_x = edge("brick")
    low_z, high_z = edge("depth")
    row = lax.broadcasted_iota(jnp.int32, (rows_z, size_y), 0)
    in_z = jnp.where(row < ZP, low_z, jnp.where(row >= ZP + size_z, high_z, 1.0))

    def mask(i, halo):
        return in_z * jnp.where(i < halo, low_x, jnp.where(i >= halo + size_x, high_x, 1.0))

    def apply(ref, idx, i, damp):
        c = ref[idx + (i,)]
        return damp * c - (ref[idx + (i - 1,)] + ref[idx + (i + 1,)] + beside_z_y(c))

    def loop(n, body):
        def step(i, carry):
            body(i)
            return carry
        lax.fori_loop(0, n, step, 0)

    def first(i):
        m = mask(i, HC)
        for f, s in enumerate(LAPLACE_SHIFTS):
            v0[f, i] = m * (src[f, i] - apply(x0, (f,), i + 1, s * cond[i] + THETA))

    loop(size_x + 2 * HC, first)

    def second(i):
        m = mask(i, 4)
        for f, s in enumerate(LAPLACE_SHIFTS):
            v1[f, i] = m * apply(v0, (f,), i + 1, s * cond[i + 1])

    loop(size_x + 8, second)

    def third(i):
        m = mask(i, 3)
        for f, s in enumerate(LAPLACE_SHIFTS):
            v2[f, i] = m * apply(v1, (f,), i + 1, s * cond[i + 2])

    loop(size_x + 6, third)

    def start(i):
        m = mask(i, HU)
        many = rec[2, i]
        for f, s in enumerate(LAPLACE_SHIFTS):
            u[0, f, i] = m * (many * x0[f, i + 3] - rec[f, i] - apply(a0, (f,), i + 1, s * cond[i + 2] + THETA))
            u[1, f, i] = many * v0[f, i + 2]
            u[2, f, i] = many * v1[f, i + 1]
            u[3, f, i] = many * v2[f, i]

    loop(size_x + 2 * HU, start)

    def level(src_ref, dst_ref, halo):
        def body(i):
            m = mask(i, halo)
            for f, s in enumerate(LAPLACE_SHIFTS):
                damp = s * cond[i + HC - halo]
                for k in range(4):
                    dst_ref[k, f, i] = m * apply(src_ref, (k, f), i + 1, damp)
        loop(size_x + 2 * halo, body)

    level(u, w1, 2)
    level(w1, w2, 1)

    def last(i):
        for f, s in enumerate(LAPLACE_SHIFTS):
            damp = s * cond[i + HC]
            for k in range(4):
                w3[k, f, i] = apply(w2, (k, f), i + 1, damp)[own]

    loop(size_x, last)

    def tiles(a):
        total = None
        for z in range(0, a.shape[0], 8):
            for y in range(0, a.shape[1], 128):
                t = a[z : z + 8, y : y + 128]
                total = t if total is None else total + t
        return total

    zero = jnp.zeros((8, 128), jnp.float32)
    for f, s in enumerate(LAPLACE_SHIFTS):
        def forward_sums(i, carry, f=f, s=s):
            p0 = v0[f, i + 5, own]
            p1 = v1[f, i + 4, own]
            p2 = v2[f, i + 3, own]
            p3 = apply(v2, (f,), i + 3, s * cond[i + 5])[own]
            v_out[0, f, i] = p0
            v_out[1, f, i] = p1
            v_out[2, f, i] = p2
            made = (p0 * p0, p0 * p1, p1 * p1, p1 * p2, p2 * p2, p2 * p3)
            return tuple(c + tiles(a) for c, a in zip(carry, made))
        done = lax.fori_loop(0, size_x, forward_sums, (zero,) * 6)
        for j in range(6):
            acc[j * SLOTS + 2 * len(PAIRS) + f] = done[j]

    levels = ((u, 3, own), (w1, 2, own), (w2, 1, own), (w3, 0, slice(0, size_z)))
    for j in range(6):
        ra, oa, za = levels[j // 2]
        rb, ob, zb = levels[j - j // 2]
        for f in range(2):
            def pair_sums(i, carry, f=f, j=j):
                a = [ra[k, f, i + oa, za] for k in range(4)]
                b = a if j % 2 == 0 else [rb[k, f, i + ob, zb] for k in range(4)]
                if j % 2 == 0:
                    for k in range(4):
                        w_out[j // 2, k, f, i] = a[k]
                return tuple(c + tiles(a[k] * b[l]) for c, (k, l) in zip(carry, PAIRS))
            done = lax.fori_loop(0, size_x, pair_sums, (zero,) * len(PAIRS))
            for n in range(len(PAIRS)):
                acc[j * SLOTS + 2 * n + f] = done[n]

    for j in range(acc.shape[0] // SLOTS):
        for n in range(0 if j >= 6 else 2 * len(PAIRS) + 2, SLOTS):
            acc[j * SLOTS + n] = zero
    by_lane = jnp.sum(acc[...], axis=1)
    ones = jnp.ones((8, 128), jnp.float32)
    out = lax.dot_general(ones, by_lane, NT, precision=lax.Precision.HIGHEST, preferred_element_type=jnp.float32)
    sums_out[...] = jnp.broadcast_to(out[0:1][None], sums_out.shape)
    prefetch.wait()


def chain(wide, first, second, blocks, size_x, size_z, n_dev):
    size_y = wide[0].shape[-1]
    f32 = jnp.float32
    slab = (size_z + 2 * ZP, size_y)
    outs = tuple(pltpu.VMEM(a.shape, f32) for a in wide) + (
        pltpu.VMEM((3, 2, size_x, size_z, size_y), f32),
        pltpu.VMEM((3, 4, 2, size_x, size_z, size_y), f32),
        jax.ShapeDtypeStruct((n_dev, 1, 256), f32),
        pltpu.VMEM(blocks.shape, blocks.dtype),
    )
    scratch = [
        pltpu.VMEM((2, size_x + 2 * HC) + slab, f32),
        pltpu.VMEM((2, size_x + 8) + slab, f32),
        pltpu.VMEM((2, size_x + 6) + slab, f32),
        pltpu.VMEM((4, 2, size_x + 6) + slab, f32),
        pltpu.VMEM((4, 2, size_x + 4) + slab, f32),
        pltpu.VMEM((4, 2, size_x + 2) + slab, f32),
        pltpu.VMEM((4, 2, size_x, size_z, size_y), f32),
        pltpu.VMEM((256, 8, 128), f32),
        pltpu.SemaphoreType.DMA,
    ]
    return pl.pallas_call(
        functools.partial(chain_kernel, size_x, size_z),
        out_shape=outs,
        in_specs=[VMEM] * 7 + [ANY],
        out_specs=(VMEM,) * 9,
        scratch_shapes=scratch,
        input_output_aliases={i: i for i in range(5)},
        compiler_params=PARAMS,
        name="chain",
    )(*[held(a) for a in wide], first, second, blocks)[5:]


def coefficients(mu):
    a = [[mu[i + j + 1] + THETA * mu[i + j] for j in range(3)] for i in range(3)]

    def inverse(pivot, size):
        good = pivot > 1e-6 * size
        return jnp.where(good, 1.0 / jnp.where(good, pivot, 1.0), 0.0)

    i0 = inverse(a[0][0], 0.0)
    l10 = a[0][1] * i0
    l20 = a[0][2] * i0
    i1 = inverse(a[1][1] - l10 * a[0][1], a[1][1])
    e21 = a[1][2] - l10 * a[0][2]
    l21 = e21 * i1
    i2 = inverse(a[2][2] - l20 * a[0][2] - l21 * e21, a[2][2])
    y0 = mu[0]
    y1 = mu[1] - l10 * y0
    y2 = mu[2] - l20 * y0 - l21 * y1
    c2 = y2 * i2
    c1 = y1 * i1 - l21 * c2
    c0 = y0 * i0 - l10 * c1 - l20 * c2
    return c0, c1, c2


def combine_kernel(every, x0, a0, v, w, forward, gradient):
    total = jnp.sum(every[...], axis=0)
    rows = jnp.concatenate([total[:, j * SLOTS : (j + 1) * SLOTS] for j in range(6)], axis=0)
    rows = jnp.concatenate([rows, jnp.zeros((2, SLOTS), jnp.float32)], axis=0)
    rows = jnp.concatenate([rows, jnp.zeros((8, 128 - SLOTS), jnp.float32)], axis=1)
    n_pair = 2 * len(PAIRS)
    at = lax.broadcasted_iota(jnp.int32, (128, 128), 0)
    to = lax.broadcasted_iota(jnp.int32, (128, 128), 1)
    same = (at & 1) == (to & 1)

    def gather_lanes(values, chosen):
        table = jnp.where(same & chosen, 1.0, 0.0)
        return jnp.dot(values, table, precision=lax.Precision.HIGHEST, preferred_element_type=jnp.float32)

    mu = gather_lanes(rows, (at >= n_pair) & (at < n_pair + 2))
    c = coefficients([mu[j : j + 1] for j in range(6)])
    basis = (jnp.ones_like(c[0]),) + c
    pair = lax.broadcasted_iota(jnp.int32, (1, 128), 1) // 2
    weight = jnp.zeros((1, 128), jnp.float32)
    for n, (k, l) in enumerate(PAIRS):
        product = basis[k] * basis[l] * (1.0 if k == l else 2.0)
        weight = jnp.where(pair == n, product, weight)
    nu = gather_lanes(rows * weight, at < n_pair)
    d = coefficients([nu[j : j + 1] for j in range(6)])
    size_x = x0.shape[1]
    scale = []
    for f in range(2):
        up = [c[k][:, f : f + 1] for k in range(3)]
        down = [[(d[j] * basis[k])[:, f : f + 1] for k in range(4)] for j in range(3)]
        scale.append((up, down))
    for i in range(size_x):
        total = None
        for f, s in enumerate(LAPLACE_SHIFTS):
            up, down = scale[f]
            field = x0[f, i]
            for k in range(3):
                field = field + up[k] * v[k, f, i]
            other = a0[f, i]
            for j in range(3):
                for k in range(4):
                    other = other + down[j][k] * w[j, k, f, i]
            forward[f, i] = field
            part = s * field * other
            total = part if total is None else total + part
        gradient[i] = (-total).astype(gradient.dtype)


def combine(every, x0, a0, v, w):
    return pl.pallas_call(
        combine_kernel,
        out_shape=(
            jax.ShapeDtypeStruct(x0.shape, jnp.float32),
            jax.ShapeDtypeStruct(x0.shape[1:], jnp.bfloat16),
        ),
        in_specs=[VMEM] * 5,
        out_specs=(VMEM, VMEM),
        compiler_params=PARAMS,
        name="combine",
    )(every, x0, a0, held(v), held(w))


def covariance_kernel(rows, cols, every, own, blocks, out, wide):
    n_dev, size_x, size_z, width = every.shape
    n_rows = size_x * size_z
    per = blocks.shape[-1] // width
    for d in range(n_dev):
        wide[d * n_rows : (d + 1) * n_rows, :] = every[d].reshape(n_rows, width).astype(jnp.float32)
    out[...] = own[...].reshape(n_rows, width).astype(jnp.float32)
    for k in range(blocks.shape[0]):
        picked = jnp.concatenate([wide[pl.ds(cols[k] * per + i, 1), :] for i in range(per)], axis=1)
        picked = jnp.broadcast_to(picked, (16, picked.shape[1])).astype(jnp.bfloat16)
        term = lax.dot_general(picked, blocks[k], NT, preferred_element_type=jnp.float32)[0:1]
        for i in range(per):
            at = pl.ds(rows[k] * per + i, 1)
            out[at, :] = out[at, :] + term[:, i * width : (i + 1) * width]


def covariance(rows, cols, every, own, blocks):
    n_dev, size_x, size_z, width = every.shape
    return pl.pallas_call(
        covariance_kernel,
        out_shape=jax.ShapeDtypeStruct((size_x * size_z, width), jnp.float32),
        in_specs=[SMEM, SMEM, VMEM, VMEM, VMEM],
        out_specs=VMEM,
        scratch_shapes=[pltpu.VMEM((n_dev * size_x * size_z, width), jnp.float32)],
        compiler_params=PARAMS,
        name="covariance",
    )(rows, cols, every, own, held(blocks))


def local(
    conductivity,
    initial_field,
    adjoint_initial,
    src_cell,
    src_amp,
    rec_cell,
    observed,
    cov_blocks,
    cov_rows,
    cov_cols,
):
    size_x, size_z, size_y = conductivity.shape
    n_dev = lax.axis_size("brick") * lax.axis_size("depth")
    fields = (initial_field, conductivity, adjoint_initial)
    x0, cond, a0 = fields
    sent = pack(x0, cond, a0, src_cell[0], src_amp[0, 0], rec_cell[0], observed[0, 0])
    first, second = swap(*sent, "brick")
    sent2 = mid(x0, cond, a0, sent[0], first, second)
    wide = prep(x0, cond, a0, sent2[0], first, second)
    first2, second2 = swap(*sent2, "depth")
    v, w, sums, blocks = chain(wide, first2, second2, cov_blocks[0, 0], size_x, size_z, n_dev)
    every = lax.all_to_all(sums, BOTH, 0, 0, tiled=True)
    forward, gradient = combine(every, x0, a0, v, w)
    every_block = lax.all_gather(gradient, "depth", axis=0, tiled=False)
    out = covariance(cov_rows[0, 0], cov_cols[0, 0], every_block, gradient, blocks)
    return (forward, out.reshape(size_x, size_z, size_y))


def solution(mesh):
    return jax.shard_map(
        local,
        mesh=mesh,
        in_specs=(
            P("brick", "depth", None),
            P(None, "brick", "depth", None),
            P(None, "brick", "depth", None),
            P("brick", "depth", None),
            P("brick", "depth", None, None),
            P("brick", "depth", None),
            P("brick", "depth", None, None),
            P("brick", "depth", None, None, None),
            P("brick", "depth", None),
            P("brick", "depth", None),
        ),
        out_specs=(P(None, "brick", "depth", None), P("brick", "depth", None)),
        check_vma=False,
    )
```

```python
import functools

import jax
import jax.numpy as jnp
from jax import lax
from jax.experimental import pallas as pl
from jax.experimental.pallas import tpu as pltpu
from jax.sharding import PartitionSpec as P

LAPLACE_SHIFTS = (0.5, 2.0)
BOTH = ("brick", "depth")
HX = 6
HC = 5
HA = 4
HU = 3
ZP = 8
THETA = 6.0
PAIRS = tuple((k, l) for k in range(4) for l in range(k, 4))
SLOTS = 32
VMEM = pl.BlockSpec(memory_space=pltpu.VMEM)
SMEM = pl.BlockSpec(memory_space=pltpu.SMEM)
HBM = pl.BlockSpec(memory_space=pltpu.HBM)
NT = (((1,), (1,)), ((), ()))
PARAMS = pltpu.CompilerParams(vmem_limit_bytes=28 * 1024 * 1024)


def held(a):
    return pltpu.with_memory_space_constraint(a, pltpu.VMEM)


def in_hbm(a):
    return pltpu.with_memory_space_constraint(a, pltpu.HBM)


def is_odd(axis):
    return lax.rem(lax.axis_index(axis), 2) == 1


def pairings(axis):
    size = lax.axis_size(axis)
    first = [(i, i ^ 1) for i in range(size) if (i ^ 1) < size]
    second = [(i, j) for i in range(size) for j in [((i + 1) ^ 1) - 1] if 0 <= j < size]
    return first, second


def swap(first, second, axis):
    one, two = pairings(axis)
    return lax.ppermute(first, axis, one), lax.ppermute(second, axis, two)


LX, LC, LA = 0, 2 * HX, 2 * HX + HC
LP = LA + 2 * HA


def pack_kernel(*refs):
    ins, (first, second), kept, pieces = refs[:7], refs[7:9], refs[9:12], refs[12:16]
    table, sems = refs[16:]
    copies = [
        pltpu.make_async_copy(a, b, sems.at[i]) for i, (a, b) in enumerate(zip(ins, kept + pieces))
    ]
    for copy in copies:
        copy.start()
    for copy in copies:
        copy.wait()
    x0, cond, a0 = kept
    src_cell, src_amp, rec_cell, observed = pieces
    size_x, _, size_y = cond.shape
    odd = is_odd("brick")

    def split(v):
        one = v.astype(jnp.bfloat16).astype(jnp.float32)
        two = (v - one).astype(jnp.bfloat16).astype(jnp.float32)
        return one, two, v - one - two

    table[...] = jnp.zeros_like(table)
    for base, cells, amounts in ((0, src_cell, src_amp), (8, rec_cell, observed)):
        n = cells.shape[-1]
        at = cells[...].astype(jnp.float32)
        hi = jnp.floor((at + 0.5) * (1.0 / size_y))
        table[base : base + 1, :n] = hi + 1.0
        table[base + 1 : base + 2, :n] = at - hi * size_y
        for s, part in enumerate(split(amounts[...])):
            table[base + 2 + 2 * s : base + 4 + 2 * s, :n] = part
    points = table[...].astype(jnp.bfloat16)
    for out, low in ((first, odd), (second, jnp.logical_not(odd))):
        for f in range(2):
            for i in range(HX):
                out[LX + f * HX + i] = x0[f, jnp.where(low, i, size_x - HX + i)].astype(jnp.bfloat16)
            for i in range(HA):
                out[LA + f * HA + i] = a0[f, jnp.where(low, i, size_x - HA + i)].astype(jnp.bfloat16)
        for i in range(HC):
            out[LC + i] = cond[jnp.where(low, i, size_x - HC + i)].astype(jnp.bfloat16)
        out[LP] = points


def pack(*ins):
    x0, cond, a0 = ins[:3]
    shape = (LP + 1,) + cond.shape[1:]
    return pl.pallas_call(
        pack_kernel,
        out_shape=(jax.ShapeDtypeStruct(shape, jnp.bfloat16),) * 2
        + tuple(pltpu.VMEM(a.shape, a.dtype) for a in ins[:3]),
        in_specs=[HBM] * 7,
        out_specs=(VMEM,) * 5,
        scratch_shapes=[pltpu.VMEM(a.shape, a.dtype) for a in ins[3:]]
        + [pltpu.VMEM(cond.shape[1:], jnp.float32), pltpu.SemaphoreType.DMA((7,))],
        compiler_params=PARAMS,
        name="pack",
    )(*[in_hbm(a) for a in ins])


def joined_rows(x0, cond, a0, first, second):
    size_x = cond.shape[0]
    odd = is_odd("brick")

    def low(at):
        return jnp.where(odd, first[at].astype(jnp.float32), second[at].astype(jnp.float32))

    def high(at):
        return jnp.where(odd, second[at].astype(jnp.float32), first[at].astype(jnp.float32))

    def reader(own, base, halo):
        def row(i):
            if i < halo:
                return low(base + i)
            if i >= halo + size_x:
                return high(base + i - halo - size_x)
            return own(i - halo)
        return row

    fields = [reader(lambda i, f=f: x0[f, i], LX + f * HX, HX) for f in range(2)]
    adjoints = [reader(lambda i, f=f: a0[f, i], LA + f * HA, HA) for f in range(2)]
    return fields, reader(lambda i: cond[i], LC, HC), adjoints, low, high


def mid_kernel(x0, cond, a0, sent, first, second, out_first, out_second):
    size_x, size_z, size_y = cond.shape
    fields, conds, adjoints, low, high = joined_rows(x0, cond, a0, first, second)
    odd = is_odd("depth")
    n = size_y // 4
    points = low(LP) + pltpu.roll(sent[LP].astype(jnp.float32), n, 1) + pltpu.roll(high(LP), 2 * n, 1)

    def put(at, down, up):
        down = jnp.concatenate(down, axis=0)
        up = jnp.concatenate(up, axis=0)
        out_first[at] = jnp.where(odd, down, up).astype(jnp.bfloat16)
        out_second[at] = jnp.where(odd, up, down).astype(jnp.bfloat16)

    at = 0
    for i in range(1, size_x + 2 * HX - 1):
        rows = [r(i) for r in fields]
        put(at, [r[:ZP] for r in rows], [r[size_z - ZP :] for r in rows])
        at += 1
    for i in range(1, size_x + 2 * HC - 1, 2):
        rows = [conds(i), conds(i + 1)]
        put(at, [r[:ZP] for r in rows], [r[size_z - ZP :] for r in rows])
        at += 1
    for i in range(1, size_x + 2 * HA - 1, 2):
        rows = [r(j) for j in (i, i + 1) for r in adjoints]
        put(at, [r[:HA] for r in rows], [r[size_z - HA :] for r in rows])
        at += 1
    out_first[at] = points.astype(jnp.bfloat16)
    out_second[at] = points.astype(jnp.bfloat16)


def depth_layers(size_x):
    return (size_x + 2 * HX - 2) + (size_x + 2 * HC - 2) // 2 + (size_x + 2 * HA - 2) // 2 + 1


def mid(x0, cond, a0, sent, first, second):
    size_x, size_z, size_y = cond.shape
    shape = (depth_layers(size_x), size_z, size_y)
    return pl.pallas_call(
        mid_kernel,
        out_shape=(jax.ShapeDtypeStruct(shape, jnp.bfloat16),) * 2,
        in_specs=[VMEM] * 6,
        out_specs=(VMEM, VMEM),
        compiler_params=PARAMS,
        name="mid",
    )(x0, cond, a0, sent, first, second)


def place(t, q, weights, halo, dst, lists, size_x, size_z, size_y):
    n_list = lists.shape[-1]
    each = n_list // 4
    lane = lax.broadcasted_iota(jnp.int32, (1, n_list), 1)
    dx = jnp.where(lane < each, -1, jnp.where(lane < 2 * each, 0, 1))
    nx = size_x + 2 * halo
    hi = lists[q : q + 1] - 1.0
    lo = lists[q + 1 : q + 2].astype(jnp.int32)
    x = jnp.floor((hi + 0.5) * (1.0 / size_z))
    z = (hi - x * size_z).astype(jnp.int32)
    row_x = x.astype(jnp.int32) + halo + size_x * dx
    ok = (hi >= 0.0) & (row_x >= 0) & (row_x < nx)
    if t == 1:
        depth, z0 = size_z, ZP
        target = row_x * size_z + z
    elif t == 0:
        depth, z0 = ZP, 0
        target = row_x * ZP + z - (size_z - ZP)
        ok = ok & (z >= size_z - ZP)
    else:
        depth, z0 = ZP, ZP + size_z
        target = row_x * ZP + z
        ok = ok & (z < ZP)
    target = jnp.where(ok, target, -1)
    hit = lax.broadcasted_iota(jnp.int32, (nx * depth, n_list), 0) == target
    right = (lax.broadcasted_iota(jnp.int32, (size_y, n_list), 0) == lo).astype(jnp.float32).astype(jnp.bfloat16)
    for at_out, parts in weights:
        total = None
        for p in parts:
            amount = 1.0 if p is None else lists[p : p + 1]
            left = jnp.where(hit, amount, 0.0).astype(jnp.bfloat16)
            d = lax.dot_general(left, right, NT, preferred_element_type=jnp.float32)
            total = d if total is None else total + d
        dst[at_out, :, z0 : z0 + depth, :] = total.reshape(nx, depth, size_y)


SRC_WEIGHTS = ((0, (2, 4, 6)), (1, (3, 5, 7)))
REC_WEIGHTS = ((0, (10, 12, 14)), (1, (11, 13, 15)), (2, (None,)))


def prep_kernel(x0, cond, a0, sent2, first, second, x0_w, cond_w, a0_w, src, rec):
    size_x, size_z, size_y = cond.shape
    fields, conds, adjoints, _, _ = joined_rows(x0, cond, a0, first, second)
    own = slice(ZP, ZP + size_z)
    for f in range(2):
        for i in range(size_x + 2 * HX):
            x0_w[f, i, own] = fields[f](i)
        for i in range(size_x + 2 * HA):
            a0_w[f, i, own] = adjoints[f](i)
    for i in range(size_x + 2 * HC):
        cond_w[i, own] = conds(i)
    lists = sent2[sent2.shape[0] - 1].astype(jnp.float32)
    place(1, 0, SRC_WEIGHTS, HC, src, lists, size_x, size_z, size_y)
    place(1, 8, REC_WEIGHTS, HU, rec, lists, size_x, size_z, size_y)


def wide_shapes(size_x, size_z, size_y):
    slab = (size_z + 2 * ZP, size_y)
    return (
        (2, size_x + 2 * HX) + slab,
        (size_x + 2 * HC,) + slab,
        (2, size_x + 2 * HA) + slab,
        (2, size_x + 2 * HC) + slab,
        (3, size_x + 2 * HU) + slab,
    )


def prep(x0, cond, a0, sent2, first, second):
    shapes = wide_shapes(*cond.shape)
    return pl.pallas_call(
        prep_kernel,
        out_shape=tuple(pltpu.VMEM(s, jnp.float32) for s in shapes),
        in_specs=[VMEM] * 6,
        out_specs=(VMEM,) * 5,
        compiler_params=PARAMS,
        name="prep",
    )(x0, cond, a0, sent2, first, second)


def beside_z_y(c):
    rows, width = c.shape
    half = width // 2
    total = pltpu.roll(c, 1, 0) + pltpu.roll(c, rows - 1, 0)
    lane = lax.broadcasted_iota(jnp.int32, (rows, half), 1)
    first = lane == 0
    last = lane == half - 1
    a, b = c[:, :half], c[:, half:]
    ra, rb = pltpu.roll(a, 1, 1), pltpu.roll(b, 1, 1)
    la, lb = pltpu.roll(a, half - 1, 1), pltpu.roll(b, half - 1, 1)
    ya = jnp.where(first, 0.0, ra) + jnp.where(last, lb, la)
    yb = jnp.where(first, ra, rb) + jnp.where(last, 0.0, lb)
    return total + jnp.concatenate([ya, yb], axis=1)


def chain_kernel(size_x, size_z, x0_in, cond_in, a0_in, src_in, rec_in, first, second, blocks,
                 x0, cond, a0, src, rec, v_out, w_out, sums_out, blocks_out,
                 v0, v1, v2, u, w1, w2, w3, acc, sem):
    prefetch = pltpu.make_async_copy(blocks, blocks_out, sem)
    prefetch.start()
    rows_z = x0.shape[-2]
    size_y = x0.shape[-1]
    own = slice(ZP, ZP + size_z)
    top = ZP + size_z

    odd = is_odd("depth")

    def low(at):
        return jnp.where(odd, first[at].astype(jnp.float32), second[at].astype(jnp.float32))

    def high(at):
        return jnp.where(odd, second[at].astype(jnp.float32), first[at].astype(jnp.float32))

    blank = jnp.zeros((ZP, size_y), jnp.float32)
    gap = jnp.zeros((ZP - HA, size_y), jnp.float32)
    at = 0
    for i in range(1, size_x + 2 * HX - 1):
        a, b = low(at), high(at)
        for f in range(2):
            x0[f, i, 0:ZP] = a[f * ZP : (f + 1) * ZP]
            x0[f, i, top : top + ZP] = b[f * ZP : (f + 1) * ZP]
        at += 1
    for i in range(1, size_x + 2 * HC - 1, 2):
        a, b = low(at), high(at)
        for j in range(2):
            cond[i + j, 0:ZP] = a[j * ZP : (j + 1) * ZP]
            cond[i + j, top : top + ZP] = b[j * ZP : (j + 1) * ZP]
        at += 1
    for i in range(1, size_x + 2 * HA - 1, 2):
        a, b = low(at), high(at)
        for j in range(2):
            for f in range(2):
                part = slice((2 * j + f) * HA, (2 * j + f + 1) * HA)
                a0[f, i + j, 0:ZP] = jnp.concatenate([gap, a[part]], axis=0)
                a0[f, i + j, top : top + ZP] = jnp.concatenate([b[part], gap], axis=0)
        at += 1
    for ref, lead in ((x0, 2), (cond, 0), (a0, 2)):
        n = ref.shape[-3]
        for i in (0, n - 1):
            for z in (slice(0, ZP), slice(top, top + ZP)):
                if lead:
                    for f in range(lead):
                        ref[f, i, z] = blank
                else:
                    ref[i, z] = blank
    for t, lists in ((0, low(at)), (2, high(at))):
        place(t, 0, SRC_WEIGHTS, HC, src, lists, size_x, size_z, size_y)
        place(t, 8, REC_WEIGHTS, HU, rec, lists, size_x, size_z, size_y)

    def edge(axis):
        at = lax.axis_index(axis)
        return (at > 0).astype(jnp.float32), (at < lax.axis_size(axis) - 1).astype(jnp.float32)

    low_x, high_x = edge("brick")
    low_z, high_z = edge("depth")
    row = lax.broadcasted_iota(jnp.int32, (rows_z, size_y), 0)
    in_z = jnp.where(row < ZP, low_z, jnp.where(row >= ZP + size_z, high_z, 1.0))

    def mask(i, halo):
        return in_z * jnp.where(i < halo, low_x, jnp.where(i >= halo + size_x, high_x, 1.0))

    def apply(ref, idx, i, damp):
        c = ref[idx + (i,)]
        return damp * c - (ref[idx + (i - 1,)] + ref[idx + (i + 1,)] + beside_z_y(c))

    def loop(n, body, unroll):
        while n % unroll:
            unroll -= 1

        def step(i, carry):
            for j in range(unroll):
                body(i * unroll + j)
            return carry

        lax.fori_loop(0, n // unroll, step, 0)

    def first(i):
        m = mask(i, HC)
        for f, s in enumerate(LAPLACE_SHIFTS):
            v0[f, i] = m * (src[f, i] - apply(x0, (f,), i + 1, s * cond[i] + THETA))

    loop(size_x + 2 * HC, first, 18)

    def second(i):
        m = mask(i, 4)
        for f, s in enumerate(LAPLACE_SHIFTS):
            v1[f, i] = m * apply(v0, (f,), i + 1, s * cond[i + 1])

    loop(size_x + 8, second, 18)

    def third(i):
        m = mask(i, 3)
        for f, s in enumerate(LAPLACE_SHIFTS):
            v2[f, i] = m * apply(v1, (f,), i + 1, s * cond[i + 2])

    loop(size_x + 6, third, 18)

    def start(i):
        m = mask(i, HU)
        many = rec[2, i]
        for f, s in enumerate(LAPLACE_SHIFTS):
            u[0, f, i] = m * (many * x0[f, i + 3] - rec[f, i] - apply(a0, (f,), i + 1, s * cond[i + 2] + THETA))
            u[1, f, i] = many * v0[f, i + 2]
            u[2, f, i] = many * v1[f, i + 1]
            u[3, f, i] = many * v2[f, i]

    loop(size_x + 2 * HU, start, 18)

    def level(src_ref, dst_ref, halo):
        def body(i):
            m = mask(i, halo)
            for f, s in enumerate(LAPLACE_SHIFTS):
                damp = s * cond[i + HC - halo]
                for k in range(4):
                    dst_ref[k, f, i] = m * apply(src_ref, (k, f), i + 1, damp)
        loop(size_x + 2 * halo, body, 6)

    level(u, w1, 2)
    level(w1, w2, 1)

    def last(i):
        for f, s in enumerate(LAPLACE_SHIFTS):
            damp = s * cond[i + HC]
            for k in range(4):
                w3[k, f, i] = apply(w2, (k, f), i + 1, damp)[own]

    loop(size_x, last, 4)

    def tiles(a):
        total = None
        for z in range(0, a.shape[0], 8):
            for y in range(0, a.shape[1], 128):
                t = a[z : z + 8, y : y + 128]
                total = t if total is None else total + t
        return total

    zero = jnp.zeros((8, 128), jnp.float32)

    def over_rows(body, carry, unroll=2):
        def step(i, carry):
            for j in range(unroll):
                carry = body(i * unroll + j, carry)
            return carry

        return lax.fori_loop(0, size_x // unroll, step, carry)

    for f, s in enumerate(LAPLACE_SHIFTS):
        def forward_sums(i, carry, f=f, s=s):
            p0 = v0[f, i + 5, own]
            p1 = v1[f, i + 4, own]
            p2 = v2[f, i + 3, own]
            p3 = apply(v2, (f,), i + 3, s * cond[i + 5])[own]
            v_out[0, f, i] = p0
            v_out[1, f, i] = p1
            v_out[2, f, i] = p2
            made = (p0 * p0, p0 * p1, p1 * p1, p1 * p2, p2 * p2, p2 * p3)
            return tuple(c + tiles(a) for c, a in zip(carry, made))
        done = over_rows(forward_sums, (zero,) * 6)
        for j in range(6):
            acc[j * SLOTS + 2 * len(PAIRS) + f] = done[j]

    levels = ((u, 3, own), (w1, 2, own), (w2, 1, own), (w3, 0, slice(0, size_z)))
    for j in range(6):
        ra, oa, za = levels[j // 2]
        rb, ob, zb = levels[j - j // 2]
        for f in range(2):
            def pair_sums(i, carry, f=f, j=j):
                a = [ra[k, f, i + oa, za] for k in range(4)]
                b = a if j % 2 == 0 else [rb[k, f, i + ob, zb] for k in range(4)]
                if j % 2 == 0:
                    for k in range(4):
                        w_out[j // 2, k, f, i] = a[k]
                return tuple(c + tiles(a[k] * b[l]) for c, (k, l) in zip(carry, PAIRS))
            done = over_rows(pair_sums, (zero,) * len(PAIRS))
            for n in range(len(PAIRS)):
                acc[j * SLOTS + 2 * n + f] = done[n]

    for j in range(acc.shape[0] // SLOTS):
        for n in range(0 if j >= 6 else 2 * len(PAIRS) + 2, SLOTS):
            acc[j * SLOTS + n] = zero
    by_lane = jnp.sum(acc[...], axis=1)
    ones = jnp.ones((8, 128), jnp.float32)
    out = lax.dot_general(ones, by_lane, NT, precision=lax.Precision.HIGHEST, preferred_element_type=jnp.float32)
    out = jnp.concatenate([out[0:1, :128], out[0:1, 128:]], axis=0)
    sums_out[...] = jnp.broadcast_to(out[None], sums_out.shape)
    prefetch.wait()


def chain(wide, first, second, blocks, size_x, size_z, n_dev):
    size_y = wide[0].shape[-1]
    f32 = jnp.float32
    slab = (size_z + 2 * ZP, size_y)
    outs = tuple(pltpu.VMEM(a.shape, f32) for a in wide) + (
        pltpu.VMEM((3, 2, size_x, size_z, size_y), f32),
        pltpu.VMEM((3, 4, 2, size_x, size_z, size_y), f32),
        jax.ShapeDtypeStruct((n_dev, 2, 128), f32),
        pltpu.VMEM(blocks.shape, blocks.dtype),
    )
    scratch = [
        pltpu.VMEM((2, size_x + 2 * HC) + slab, f32),
        pltpu.VMEM((2, size_x + 8) + slab, f32),
        pltpu.VMEM((2, size_x + 6) + slab, f32),
        pltpu.VMEM((4, 2, size_x + 6) + slab, f32),
        pltpu.VMEM((4, 2, size_x + 4) + slab, f32),
        pltpu.VMEM((4, 2, size_x + 2) + slab, f32),
        pltpu.VMEM((4, 2, size_x, size_z, size_y), f32),
        pltpu.VMEM((256, 8, 128), f32),
        pltpu.SemaphoreType.DMA,
    ]
    return pl.pallas_call(
        functools.partial(chain_kernel, size_x, size_z),
        out_shape=outs,
        in_specs=[VMEM] * 7 + [HBM],
        out_specs=(VMEM,) * 9,
        scratch_shapes=scratch,
        input_output_aliases={i: i for i in range(5)},
        compiler_params=PARAMS,
        name="chain",
    )(*[held(a) for a in wide], first, second, in_hbm(blocks))[5:]


def coefficients(mu):
    a = [[mu[i + j + 1] + THETA * mu[i + j] for j in range(3)] for i in range(3)]

    def inverse(pivot, size):
        good = pivot > 1e-6 * size
        return jnp.where(good, 1.0 / jnp.where(good, pivot, 1.0), 0.0)

    i0 = inverse(a[0][0], 0.0)
    l10 = a[0][1] * i0
    l20 = a[0][2] * i0
    i1 = inverse(a[1][1] - l10 * a[0][1], a[1][1])
    e21 = a[1][2] - l10 * a[0][2]
    l21 = e21 * i1
    i2 = inverse(a[2][2] - l20 * a[0][2] - l21 * e21, a[2][2])
    y0 = mu[0]
    y1 = mu[1] - l10 * y0
    y2 = mu[2] - l20 * y0 - l21 * y1
    c2 = y2 * i2
    c1 = y1 * i1 - l21 * c2
    c0 = y0 * i0 - l10 * c1 - l20 * c2
    return c0, c1, c2


def combine_kernel(every, x0, a0, v, w, forward, gradient):
    total = jnp.sum(every[...], axis=0)
    per = 128 // SLOTS
    rows = jnp.concatenate(
        [total[j // per : j // per + 1, j % per * SLOTS : (j % per + 1) * SLOTS] for j in range(6)], axis=0
    )
    rows = jnp.concatenate([rows, jnp.zeros((2, SLOTS), jnp.float32)], axis=0)
    rows = jnp.concatenate([rows, jnp.zeros((8, 128 - SLOTS), jnp.float32)], axis=1)
    n_pair = 2 * len(PAIRS)
    at = lax.broadcasted_iota(jnp.int32, (128, 128), 0)
    to = lax.broadcasted_iota(jnp.int32, (128, 128), 1)
    same = (at & 1) == (to & 1)

    def gather_lanes(values, chosen):
        table = jnp.where(same & chosen, 1.0, 0.0)
        return jnp.dot(values, table, precision=lax.Precision.HIGHEST, preferred_element_type=jnp.float32)

    mu = gather_lanes(rows, (at >= n_pair) & (at < n_pair + 2))
    c = coefficients([mu[j : j + 1] for j in range(6)])
    basis = (jnp.ones_like(c[0]),) + c
    pair = lax.broadcasted_iota(jnp.int32, (1, 128), 1) // 2
    weight = jnp.zeros((1, 128), jnp.float32)
    for n, (k, l) in enumerate(PAIRS):
        product = basis[k] * basis[l] * (1.0 if k == l else 2.0)
        weight = jnp.where(pair == n, product, weight)
    nu = gather_lanes(rows * weight, at < n_pair)
    d = coefficients([nu[j : j + 1] for j in range(6)])
    size_x = x0.shape[1]
    scale = []
    for f in range(2):
        up = [c[k][:, f : f + 1] for k in range(3)]
        down = [[(d[j] * basis[k])[:, f : f + 1] for k in range(4)] for j in range(3)]
        scale.append((up, down))
    for i in range(size_x):
        total = None
        for f, s in enumerate(LAPLACE_SHIFTS):
            up, down = scale[f]
            field = x0[f, i]
            for k in range(3):
                field = field + up[k] * v[k, f, i]
            other = a0[f, i]
            for j in range(3):
                for k in range(4):
                    other = other + down[j][k] * w[j, k, f, i]
            forward[f, i] = field
            part = s * field * other
            total = part if total is None else total + part
        gradient[i] = (-total).astype(gradient.dtype)


def combine(every, x0, a0, v, w):
    return pl.pallas_call(
        combine_kernel,
        out_shape=(
            jax.ShapeDtypeStruct(x0.shape, jnp.float32),
            jax.ShapeDtypeStruct(x0.shape[1:], jnp.bfloat16),
        ),
        in_specs=[VMEM] * 5,
        out_specs=(VMEM, VMEM),
        compiler_params=PARAMS,
        name="combine",
    )(every, x0, a0, held(v), held(w))


def covariance_kernel(cols, rows, every, own, blocks, out, wide):
    n_dev, size_x, size_z, width = every.shape
    n_rows = size_x * size_z
    n_blocks, size, _ = blocks.shape
    per = size // width
    for d in range(n_dev):
        wide[d * n_rows : (d + 1) * n_rows, :] = every[d].reshape(n_rows, width).astype(jnp.float32)
    picked = jnp.concatenate(
        [
            jnp.concatenate([wide[pl.ds(cols[k] * per + i, 1), :] for i in range(per)], axis=1)
            for k in range(n_blocks)
        ],
        axis=0,
    ).astype(jnp.bfloat16)
    which = lax.broadcasted_iota(jnp.int32, (n_blocks, size), 0)
    terms = jnp.zeros((n_blocks, size), jnp.float32)
    for k in range(n_blocks):
        product = lax.dot_general(picked, blocks[k], NT, preferred_element_type=jnp.float32)
        terms = jnp.where(which == k, product, terms)
    total = own[...].reshape(n_rows, width).astype(jnp.float32)
    at = lax.broadcasted_iota(jnp.int32, (n_rows, n_blocks), 0)
    for i in range(per):
        hit = jnp.where(at == rows[...] * per + i, 1.0, 0.0)
        total = total + jnp.dot(
            hit,
            terms[:, i * width : (i + 1) * width],
            precision=lax.Precision.HIGHEST,
            preferred_element_type=jnp.float32,
        )
    out[...] = total


def covariance(cols, rows, every, own, blocks):
    n_dev, size_x, size_z, width = every.shape
    return pl.pallas_call(
        covariance_kernel,
        out_shape=jax.ShapeDtypeStruct((size_x * size_z, width), jnp.float32),
        in_specs=[SMEM, VMEM, VMEM, VMEM, VMEM],
        out_specs=VMEM,
        scratch_shapes=[pltpu.VMEM((n_dev * size_x * size_z, width), jnp.float32)],
        compiler_params=PARAMS,
        name="covariance",
    )(cols, rows, every, own, held(blocks))


def local(
    conductivity,
    initial_field,
    adjoint_initial,
    src_cell,
    src_amp,
    rec_cell,
    observed,
    cov_blocks,
    cov_rows,
    cov_cols,
):
    size_x, size_z, size_y = conductivity.shape
    n_dev = lax.axis_size("brick") * lax.axis_size("depth")
    *sent, x0, cond, a0 = pack(
        initial_field, conductivity, adjoint_initial, src_cell[0], src_amp[0, 0], rec_cell[0], observed[0, 0]
    )
    x0, cond, a0 = held(x0), held(cond), held(a0)
    first, second = swap(*sent, "brick")
    sent2 = mid(x0, cond, a0, sent[0], first, second)
    wide = prep(x0, cond, a0, sent2[0], first, second)
    first2, second2 = swap(*sent2, "depth")
    v, w, sums, blocks = chain(wide, first2, second2, cov_blocks[0, 0], size_x, size_z, n_dev)
    every = lax.all_to_all(sums, BOTH, 0, 0, tiled=True)
    forward, gradient = combine(every, x0, a0, v, w)
    every_block = lax.all_gather(gradient, "depth", axis=0, tiled=False)
    out = covariance(cov_cols[0, 0], cov_rows[0], every_block, gradient, blocks)
    return (forward, out.reshape(size_x, size_z, size_y))


def solution(mesh):
    return jax.shard_map(
        local,
        mesh=mesh,
        in_specs=(
            P("brick", "depth", None),
            P(None, "brick", "depth", None),
            P(None, "brick", "depth", None),
            P("brick", "depth", None),
            P("brick", "depth", None, None),
            P("brick", "depth", None),
            P("brick", "depth", None, None),
            P("brick", "depth", None, None, None),
            P("brick", "depth", None),
            P("brick", "depth", None),
        ),
        out_specs=(P(None, "brick", "depth", None), P("brick", "depth", None)),
        check_vma=False,
    )
```

```python
import functools

import jax
import jax.numpy as jnp
from jax import lax
from jax.experimental import pallas as pl
from jax.experimental.pallas import tpu as pltpu
from jax.sharding import PartitionSpec as P

LAPLACE_SHIFTS = (0.5, 2.0)
BOTH = ("brick", "depth")
HX = 6
HC = 5
HA = 4
HU = 3
ZP = 8
THETA = 6.0
PAIRS = tuple((k, l) for k in range(4) for l in range(k, 4))
SLOTS = 32
VMEM = pl.BlockSpec(memory_space=pltpu.VMEM)
SMEM = pl.BlockSpec(memory_space=pltpu.SMEM)
HBM = pl.BlockSpec(memory_space=pltpu.HBM)
NT = (((1,), (1,)), ((), ()))
PARAMS = pltpu.CompilerParams(vmem_limit_bytes=28 * 1024 * 1024)


def held(a):
    return pltpu.with_memory_space_constraint(a, pltpu.VMEM)


def in_hbm(a):
    return pltpu.with_memory_space_constraint(a, pltpu.HBM)


def is_odd(axis):
    return lax.rem(lax.axis_index(axis), 2) == 1


def pairings(axis):
    size = lax.axis_size(axis)
    first = [(i, i ^ 1) for i in range(size) if (i ^ 1) < size]
    second = [(i, j) for i in range(size) for j in [((i + 1) ^ 1) - 1] if 0 <= j < size]
    return first, second


def swap(first, second, axis):
    one, two = pairings(axis)
    return lax.ppermute(first, axis, one), lax.ppermute(second, axis, two)


LX, LC, LA = 0, 2 * HX, 2 * HX + HC
LP = LA + 2 * HA


def pack_kernel(*refs):
    ins, (first, second), kept, pieces = refs[:7], refs[7:9], refs[9:12], refs[12:16]
    table, sems = refs[16:]
    copies = [
        pltpu.make_async_copy(a, b, sems.at[i]) for i, (a, b) in enumerate(zip(ins, kept + pieces))
    ]
    for copy in copies:
        copy.start()
    for copy in copies:
        copy.wait()
    x0, cond, a0 = kept
    src_cell, src_amp, rec_cell, observed = pieces
    size_x, _, size_y = cond.shape
    odd = is_odd("brick")

    def split(v):
        one = v.astype(jnp.bfloat16).astype(jnp.float32)
        two = (v - one).astype(jnp.bfloat16).astype(jnp.float32)
        return one, two, v - one - two

    table[...] = jnp.zeros_like(table)
    for base, cells, amounts in ((0, src_cell, src_amp), (8, rec_cell, observed)):
        n = cells.shape[-1]
        at = cells[...].astype(jnp.float32)
        hi = jnp.floor((at + 0.5) * (1.0 / size_y))
        table[base : base + 1, :n] = hi + 1.0
        table[base + 1 : base + 2, :n] = at - hi * size_y
        for s, part in enumerate(split(amounts[...])):
            table[base + 2 + 2 * s : base + 4 + 2 * s, :n] = part
    points = table[...].astype(jnp.bfloat16)
    for out, low in ((first, odd), (second, jnp.logical_not(odd))):
        for f in range(2):
            for i in range(HX):
                out[LX + f * HX + i] = x0[f, jnp.where(low, i, size_x - HX + i)].astype(jnp.bfloat16)
            for i in range(HA):
                out[LA + f * HA + i] = a0[f, jnp.where(low, i, size_x - HA + i)].astype(jnp.bfloat16)
        for i in range(HC):
            out[LC + i] = cond[jnp.where(low, i, size_x - HC + i)].astype(jnp.bfloat16)
        out[LP] = points


def pack(*ins):
    x0, cond, a0 = ins[:3]
    shape = (LP + 1,) + cond.shape[1:]
    return pl.pallas_call(
        pack_kernel,
        out_shape=(jax.ShapeDtypeStruct(shape, jnp.bfloat16),) * 2
        + tuple(pltpu.VMEM(a.shape, a.dtype) for a in ins[:3]),
        in_specs=[HBM] * 7,
        out_specs=(VMEM,) * 5,
        scratch_shapes=[pltpu.VMEM(a.shape, a.dtype) for a in ins[3:]]
        + [pltpu.VMEM(cond.shape[1:], jnp.float32), pltpu.SemaphoreType.DMA((7,))],
        compiler_params=PARAMS,
        name="pack",
    )(*[in_hbm(a) for a in ins])


def joined_rows(x0, cond, a0, first, second):
    size_x = cond.shape[0]
    odd = is_odd("brick")

    def low(at):
        return jnp.where(odd, first[at].astype(jnp.float32), second[at].astype(jnp.float32))

    def high(at):
        return jnp.where(odd, second[at].astype(jnp.float32), first[at].astype(jnp.float32))

    def reader(own, base, halo):
        def row(i):
            if i < halo:
                return low(base + i)
            if i >= halo + size_x:
                return high(base + i - halo - size_x)
            return own(i - halo)
        return row

    fields = [reader(lambda i, f=f: x0[f, i], LX + f * HX, HX) for f in range(2)]
    adjoints = [reader(lambda i, f=f: a0[f, i], LA + f * HA, HA) for f in range(2)]
    return fields, reader(lambda i: cond[i], LC, HC), adjoints, low, high


def mid_kernel(x0, cond, a0, sent, first, second, _, out_first, out_second):
    size_x, size_z, size_y = cond.shape
    fields, conds, adjoints, low, high = joined_rows(x0, cond, a0, first, second)
    odd = is_odd("depth")
    n = size_y // 4
    points = low(LP) + pltpu.roll(sent[LP].astype(jnp.float32), n, 1) + pltpu.roll(high(LP), 2 * n, 1)

    def put(at, down, up):
        down = jnp.concatenate(down, axis=0)
        up = jnp.concatenate(up, axis=0)
        out_first[at] = jnp.where(odd, down, up).astype(jnp.bfloat16)
        out_second[at] = jnp.where(odd, up, down).astype(jnp.bfloat16)

    at = 0
    for i in range(1, size_x + 2 * HX - 1):
        rows = [r(i) for r in fields]
        put(at, [r[:ZP] for r in rows], [r[size_z - ZP :] for r in rows])
        at += 1
    for i in range(1, size_x + 2 * HC - 1, 2):
        rows = [conds(i), conds(i + 1)]
        put(at, [r[:ZP] for r in rows], [r[size_z - ZP :] for r in rows])
        at += 1
    for i in range(1, size_x + 2 * HA - 1, 2):
        rows = [r(j) for j in (i, i + 1) for r in adjoints]
        put(at, [r[:HA] for r in rows], [r[size_z - HA :] for r in rows])
        at += 1
    out_first[at] = points.astype(jnp.bfloat16)
    out_second[at] = points.astype(jnp.bfloat16)


def depth_layers(size_x):
    return (size_x + 2 * HX - 2) + (size_x + 2 * HC - 2) // 2 + (size_x + 2 * HA - 2) // 2 + 1


def mid(x0, cond, a0, sent, first, second, ready):
    size_x, size_z, size_y = cond.shape
    shape = (depth_layers(size_x), size_z, size_y)
    return pl.pallas_call(
        mid_kernel,
        out_shape=(jax.ShapeDtypeStruct(shape, jnp.bfloat16),) * 2,
        in_specs=[VMEM] * 7,
        out_specs=(VMEM, VMEM),
        compiler_params=PARAMS,
        name="mid",
    )(x0, cond, a0, sent, first, second, held(ready))


def place(t, q, weights, halo, dst, lists, size_x, size_z, size_y):
    n_list = lists.shape[-1]
    each = n_list // 4
    lane = lax.broadcasted_iota(jnp.int32, (1, n_list), 1)
    dx = jnp.where(lane < each, -1, jnp.where(lane < 2 * each, 0, 1))
    nx = size_x + 2 * halo
    hi = lists[q : q + 1] - 1.0
    lo = lists[q + 1 : q + 2].astype(jnp.int32)
    x = jnp.floor((hi + 0.5) * (1.0 / size_z))
    z = (hi - x * size_z).astype(jnp.int32)
    row_x = x.astype(jnp.int32) + halo + size_x * dx
    ok = (hi >= 0.0) & (row_x >= 0) & (row_x < nx)
    if t == 1:
        depth, z0 = size_z, ZP
        target = row_x * size_z + z
    elif t == 0:
        depth, z0 = ZP, 0
        target = row_x * ZP + z - (size_z - ZP)
        ok = ok & (z >= size_z - ZP)
    else:
        depth, z0 = ZP, ZP + size_z
        target = row_x * ZP + z
        ok = ok & (z < ZP)
    target = jnp.where(ok, target, -1)
    hit = lax.broadcasted_iota(jnp.int32, (nx * depth, n_list), 0) == target
    right = (lax.broadcasted_iota(jnp.int32, (size_y, n_list), 0) == lo).astype(jnp.float32).astype(jnp.bfloat16)
    for at_out, parts in weights:
        total = None
        for p in parts:
            amount = 1.0 if p is None else lists[p : p + 1]
            left = jnp.where(hit, amount, 0.0).astype(jnp.bfloat16)
            d = lax.dot_general(left, right, NT, preferred_element_type=jnp.float32)
            total = d if total is None else total + d
        dst[at_out, :, z0 : z0 + depth, :] = total.reshape(nx, depth, size_y)


SRC_WEIGHTS = ((0, (2, 4, 6)), (1, (3, 5, 7)))
REC_WEIGHTS = ((0, (10, 12, 14)), (1, (11, 13, 15)), (2, (None,)))


def prep_kernel(x0, cond, a0, sent2, first, second, x0_w, cond_w, a0_w, src, rec):
    size_x, size_z, size_y = cond.shape
    fields, conds, adjoints, _, _ = joined_rows(x0, cond, a0, first, second)
    own = slice(ZP, ZP + size_z)
    for f in range(2):
        for i in range(size_x + 2 * HX):
            x0_w[f, i, own] = fields[f](i)
        for i in range(size_x + 2 * HA):
            a0_w[f, i, own] = adjoints[f](i)
    for i in range(size_x + 2 * HC):
        cond_w[i, own] = conds(i)
    lists = sent2[sent2.shape[0] - 1].astype(jnp.float32)
    place(1, 0, SRC_WEIGHTS, HC, src, lists, size_x, size_z, size_y)
    place(1, 8, REC_WEIGHTS, HU, rec, lists, size_x, size_z, size_y)


def wide_shapes(size_x, size_z, size_y):
    slab = (size_z + 2 * ZP, size_y)
    return (
        (2, size_x + 2 * HX) + slab,
        (size_x + 2 * HC,) + slab,
        (2, size_x + 2 * HA) + slab,
        (2, size_x + 2 * HC) + slab,
        (3, size_x + 2 * HU) + slab,
    )


def prep(x0, cond, a0, sent2, first, second):
    shapes = wide_shapes(*cond.shape)
    return pl.pallas_call(
        prep_kernel,
        out_shape=tuple(pltpu.VMEM(s, jnp.float32) for s in shapes),
        in_specs=[VMEM] * 6,
        out_specs=(VMEM,) * 5,
        compiler_params=PARAMS,
        name="prep",
    )(x0, cond, a0, sent2, first, second)


def beside_z_y(c):
    rows, width = c.shape
    half = width // 2
    total = pltpu.roll(c, 1, 0) + pltpu.roll(c, rows - 1, 0)
    lane = lax.broadcasted_iota(jnp.int32, (rows, half), 1)
    first = lane == 0
    last = lane == half - 1
    a, b = c[:, :half], c[:, half:]
    ra, rb = pltpu.roll(a, 1, 1), pltpu.roll(b, 1, 1)
    la, lb = pltpu.roll(a, half - 1, 1), pltpu.roll(b, half - 1, 1)
    ya = jnp.where(first, 0.0, ra) + jnp.where(last, lb, la)
    yb = jnp.where(first, ra, rb) + jnp.where(last, 0.0, lb)
    return total + jnp.concatenate([ya, yb], axis=1)


def chain_kernel(size_x, size_z, x0_in, cond_in, a0_in, src_in, rec_in, first, second,
                 x0, cond, a0, src, rec, v_out, w_out, sums_out,
                 v0, v1, v2, u, w1, w2, w3, acc):
    rows_z = x0.shape[-2]
    size_y = x0.shape[-1]
    own = slice(ZP, ZP + size_z)
    top = ZP + size_z

    odd = is_odd("depth")

    def low(at):
        return jnp.where(odd, first[at].astype(jnp.float32), second[at].astype(jnp.float32))

    def high(at):
        return jnp.where(odd, second[at].astype(jnp.float32), first[at].astype(jnp.float32))

    blank = jnp.zeros((ZP, size_y), jnp.float32)
    gap = jnp.zeros((ZP - HA, size_y), jnp.float32)
    at = 0
    for i in range(1, size_x + 2 * HX - 1):
        a, b = low(at), high(at)
        for f in range(2):
            x0[f, i, 0:ZP] = a[f * ZP : (f + 1) * ZP]
            x0[f, i, top : top + ZP] = b[f * ZP : (f + 1) * ZP]
        at += 1
    for i in range(1, size_x + 2 * HC - 1, 2):
        a, b = low(at), high(at)
        for j in range(2):
            cond[i + j, 0:ZP] = a[j * ZP : (j + 1) * ZP]
            cond[i + j, top : top + ZP] = b[j * ZP : (j + 1) * ZP]
        at += 1
    for i in range(1, size_x + 2 * HA - 1, 2):
        a, b = low(at), high(at)
        for j in range(2):
            for f in range(2):
                part = slice((2 * j + f) * HA, (2 * j + f + 1) * HA)
                a0[f, i + j, 0:ZP] = jnp.concatenate([gap, a[part]], axis=0)
                a0[f, i + j, top : top + ZP] = jnp.concatenate([b[part], gap], axis=0)
        at += 1
    for ref, lead in ((x0, 2), (cond, 0), (a0, 2)):
        n = ref.shape[-3]
        for i in (0, n - 1):
            for z in (slice(0, ZP), slice(top, top + ZP)):
                if lead:
                    for f in range(lead):
                        ref[f, i, z] = blank
                else:
                    ref[i, z] = blank
    for t, lists in ((0, low(at)), (2, high(at))):
        place(t, 0, SRC_WEIGHTS, HC, src, lists, size_x, size_z, size_y)
        place(t, 8, REC_WEIGHTS, HU, rec, lists, size_x, size_z, size_y)

    def edge(axis):
        at = lax.axis_index(axis)
        return (at > 0).astype(jnp.float32), (at < lax.axis_size(axis) - 1).astype(jnp.float32)

    low_x, high_x = edge("brick")
    low_z, high_z = edge("depth")
    row = lax.broadcasted_iota(jnp.int32, (rows_z, size_y), 0)
    in_z = jnp.where(row < ZP, low_z, jnp.where(row >= ZP + size_z, high_z, 1.0))

    def mask(i, halo):
        return in_z * jnp.where(i < halo, low_x, jnp.where(i >= halo + size_x, high_x, 1.0))

    def apply(ref, idx, i, damp):
        c = ref[idx + (i,)]
        return damp * c - (ref[idx + (i - 1,)] + ref[idx + (i + 1,)] + beside_z_y(c))

    def loop(n, body, unroll):
        while n % unroll:
            unroll -= 1
        if n == unroll:
            for j in range(n):
                body(j)
            return

        def step(i, carry):
            for j in range(unroll):
                body(i * unroll + j)
            return carry

        lax.fori_loop(0, n // unroll, step, 0)

    def first(i):
        m = mask(i, HC)
        for f, s in enumerate(LAPLACE_SHIFTS):
            v0[f, i] = m * (src[f, i] - apply(x0, (f,), i + 1, s * cond[i] + THETA))

    loop(size_x + 2 * HC, first, 18)

    def second(i):
        m = mask(i, 4)
        for f, s in enumerate(LAPLACE_SHIFTS):
            v1[f, i] = m * apply(v0, (f,), i + 1, s * cond[i + 1])

    loop(size_x + 8, second, 18)

    def third(i):
        m = mask(i, 3)
        for f, s in enumerate(LAPLACE_SHIFTS):
            v2[f, i] = m * apply(v1, (f,), i + 1, s * cond[i + 2])

    loop(size_x + 6, third, 18)

    def start(i):
        m = mask(i, HU)
        many = rec[2, i]
        for f, s in enumerate(LAPLACE_SHIFTS):
            u[0, f, i] = m * (many * x0[f, i + 3] - rec[f, i] - apply(a0, (f,), i + 1, s * cond[i + 2] + THETA))
            u[1, f, i] = many * v0[f, i + 2]
            u[2, f, i] = many * v1[f, i + 1]
            u[3, f, i] = many * v2[f, i]

    loop(size_x + 2 * HU, start, 18)

    def level(src_ref, dst_ref, halo):
        def body(i):
            m = mask(i, halo)
            for f, s in enumerate(LAPLACE_SHIFTS):
                damp = s * cond[i + HC - halo]
                for k in range(4):
                    dst_ref[k, f, i] = m * apply(src_ref, (k, f), i + 1, damp)
        loop(size_x + 2 * halo, body, 6)

    level(u, w1, 2)
    level(w1, w2, 1)

    def last(i):
        for f, s in enumerate(LAPLACE_SHIFTS):
            damp = s * cond[i + HC]
            for k in range(4):
                w3[k, f, i] = apply(w2, (k, f), i + 1, damp)[own]

    loop(size_x, last, 4)

    def tiles(a):
        total = None
        for z in range(0, a.shape[0], 8):
            for y in range(0, a.shape[1], 128):
                t = a[z : z + 8, y : y + 128]
                total = t if total is None else total + t
        return total

    zero = jnp.zeros((8, 128), jnp.float32)

    def over_rows(body, carry, unroll=8):
        def step(i, carry):
            for j in range(unroll):
                carry = body(i * unroll + j, carry)
            return carry

        return lax.fori_loop(0, size_x // unroll, step, carry)

    for f, s in enumerate(LAPLACE_SHIFTS):
        def forward_sums(i, carry, f=f, s=s):
            p0 = v0[f, i + 5, own]
            p1 = v1[f, i + 4, own]
            p2 = v2[f, i + 3, own]
            p3 = apply(v2, (f,), i + 3, s * cond[i + 5])[own]
            v_out[0, f, i] = p0
            v_out[1, f, i] = p1
            v_out[2, f, i] = p2
            made = (p0 * p0, p0 * p1, p1 * p1, p1 * p2, p2 * p2, p2 * p3)
            return tuple(c + tiles(a) for c, a in zip(carry, made))
        done = over_rows(forward_sums, (zero,) * 6)
        for j in range(6):
            acc[j * SLOTS + 2 * len(PAIRS) + f] = done[j]

    levels = ((u, 3, own), (w1, 2, own), (w2, 1, own), (w3, 0, slice(0, size_z)))
    for j in range(6):
        ra, oa, za = levels[j // 2]
        rb, ob, zb = levels[j - j // 2]
        for f in range(2):
            def pair_sums(i, carry, f=f, j=j):
                a = [ra[k, f, i + oa, za] for k in range(4)]
                b = a if j % 2 == 0 else [rb[k, f, i + ob, zb] for k in range(4)]
                if j % 2 == 0:
                    for k in range(4):
                        w_out[j // 2, k, f, i] = a[k]
                return tuple(c + tiles(a[k] * b[l]) for c, (k, l) in zip(carry, PAIRS))
            done = over_rows(pair_sums, (zero,) * len(PAIRS))
            for n in range(len(PAIRS)):
                acc[j * SLOTS + 2 * n + f] = done[n]

    for j in range(acc.shape[0] // SLOTS):
        for n in range(0 if j >= 6 else 2 * len(PAIRS) + 2, SLOTS):
            acc[j * SLOTS + n] = zero
    by_lane = jnp.sum(acc[...], axis=1)
    ones = jnp.ones((8, 128), jnp.float32)
    out = lax.dot_general(ones, by_lane, NT, precision=lax.Precision.HIGHEST, preferred_element_type=jnp.float32)
    out = jnp.concatenate([out[0:1, :128], out[0:1, 128:]], axis=0)
    sums_out[...] = jnp.broadcast_to(out[None], sums_out.shape)


def chain(wide, first, second, size_x, size_z, n_dev):
    size_y = wide[0].shape[-1]
    f32 = jnp.float32
    slab = (size_z + 2 * ZP, size_y)
    outs = tuple(pltpu.VMEM(a.shape, f32) for a in wide) + (
        pltpu.VMEM((3, 2, size_x, size_z, size_y), f32),
        pltpu.VMEM((3, 4, 2, size_x, size_z, size_y), f32),
        jax.ShapeDtypeStruct((n_dev, 2, 128), f32),
    )
    scratch = [
        pltpu.VMEM((2, size_x + 2 * HC) + slab, f32),
        pltpu.VMEM((2, size_x + 8) + slab, f32),
        pltpu.VMEM((2, size_x + 6) + slab, f32),
        pltpu.VMEM((4, 2, size_x + 6) + slab, f32),
        pltpu.VMEM((4, 2, size_x + 4) + slab, f32),
        pltpu.VMEM((4, 2, size_x + 2) + slab, f32),
        pltpu.VMEM((4, 2, size_x, size_z, size_y), f32),
        pltpu.VMEM((256, 8, 128), f32),
    ]
    return pl.pallas_call(
        functools.partial(chain_kernel, size_x, size_z),
        out_shape=outs,
        in_specs=[VMEM] * 7,
        out_specs=(VMEM,) * 8,
        scratch_shapes=scratch,
        input_output_aliases={i: i for i in range(5)},
        compiler_params=PARAMS,
        name="chain",
    )(*[held(a) for a in wide], first, second)[5:]


def coefficients(mu):
    a = [[mu[i + j + 1] + THETA * mu[i + j] for j in range(3)] for i in range(3)]

    def inverse(pivot, size):
        good = pivot > 1e-6 * size
        return jnp.where(good, 1.0 / jnp.where(good, pivot, 1.0), 0.0)

    i0 = inverse(a[0][0], 0.0)
    l10 = a[0][1] * i0
    l20 = a[0][2] * i0
    i1 = inverse(a[1][1] - l10 * a[0][1], a[1][1])
    e21 = a[1][2] - l10 * a[0][2]
    l21 = e21 * i1
    i2 = inverse(a[2][2] - l20 * a[0][2] - l21 * e21, a[2][2])
    y0 = mu[0]
    y1 = mu[1] - l10 * y0
    y2 = mu[2] - l20 * y0 - l21 * y1
    c2 = y2 * i2
    c1 = y1 * i1 - l21 * c2
    c0 = y0 * i0 - l10 * c1 - l20 * c2
    return c0, c1, c2


def combine_kernel(every, x0, a0, v, w, forward, gradient):
    total = jnp.sum(every[...], axis=0)
    per = 128 // SLOTS
    rows = jnp.concatenate(
        [total[j // per : j // per + 1, j % per * SLOTS : (j % per + 1) * SLOTS] for j in range(6)], axis=0
    )
    rows = jnp.concatenate([rows, jnp.zeros((2, SLOTS), jnp.float32)], axis=0)
    rows = jnp.concatenate([rows, jnp.zeros((8, 128 - SLOTS), jnp.float32)], axis=1)
    n_pair = 2 * len(PAIRS)
    at = lax.broadcasted_iota(jnp.int32, (128, 128), 0)
    to = lax.broadcasted_iota(jnp.int32, (128, 128), 1)
    same = (at & 1) == (to & 1)

    def gather_lanes(values, chosen):
        table = jnp.where(same & chosen, 1.0, 0.0)
        return jnp.dot(values, table, precision=lax.Precision.HIGHEST, preferred_element_type=jnp.float32)

    mu = gather_lanes(rows, (at >= n_pair) & (at < n_pair + 2))
    c = coefficients([mu[j : j + 1] for j in range(6)])
    basis = (jnp.ones_like(c[0]),) + c
    pair = lax.broadcasted_iota(jnp.int32, (1, 128), 1) // 2
    weight = jnp.zeros((1, 128), jnp.float32)
    for n, (k, l) in enumerate(PAIRS):
        product = basis[k] * basis[l] * (1.0 if k == l else 2.0)
        weight = jnp.where(pair == n, product, weight)
    nu = gather_lanes(rows * weight, at < n_pair)
    d = coefficients([nu[j : j + 1] for j in range(6)])
    size_x = x0.shape[1]
    scale = []
    for f in range(2):
        up = [c[k][:, f : f + 1] for k in range(3)]
        down = [[(d[j] * basis[k])[:, f : f + 1] for k in range(4)] for j in range(3)]
        scale.append((up, down))
    for i in range(size_x):
        total = None
        for f, s in enumerate(LAPLACE_SHIFTS):
            up, down = scale[f]
            field = x0[f, i]
            for k in range(3):
                field = field + up[k] * v[k, f, i]
            other = a0[f, i]
            for j in range(3):
                for k in range(4):
                    other = other + down[j][k] * w[j, k, f, i]
            forward[f, i] = field
            part = s * field * other
            total = part if total is None else total + part
        gradient[i] = (-total).astype(gradient.dtype)


def combine(every, x0, a0, v, w):
    return pl.pallas_call(
        combine_kernel,
        out_shape=(
            jax.ShapeDtypeStruct(x0.shape, jnp.float32),
            jax.ShapeDtypeStruct(x0.shape[1:], jnp.bfloat16),
        ),
        in_specs=[VMEM] * 5,
        out_specs=(VMEM, VMEM),
        compiler_params=PARAMS,
        name="combine",
    )(every, x0, a0, held(v), held(w))


def turn_kernel(blocks, out, buf, sems):
    n = buf.shape[0]
    copies = [pltpu.make_async_copy(blocks.at[k], buf.at[k], sems.at[k]) for k in range(n)]
    for copy in copies:
        copy.start()
    for k, copy in enumerate(copies):
        copy.wait()
        out[k] = buf[k].T


def turn(blocks):
    return pl.pallas_call(
        turn_kernel,
        out_shape=pltpu.VMEM(blocks.shape, blocks.dtype),
        in_specs=[HBM],
        out_specs=VMEM,
        scratch_shapes=[
            pltpu.VMEM(blocks.shape, blocks.dtype),
            pltpu.SemaphoreType.DMA((blocks.shape[0],)),
        ],
        compiler_params=PARAMS,
        name="turn",
    )(in_hbm(blocks))


def covariance_kernel(cols, rows, every, own, blocks, out):
    n_dev, size_x, size_z, width = every.shape
    n_rows = size_x * size_z
    n_blocks, size, _ = blocks.shape
    per = size // width
    table = every[...].reshape(n_dev * n_rows, width)
    at = lax.broadcasted_iota(jnp.int32, (n_dev * n_rows, n_blocks), 0)
    hits = jnp.concatenate([jnp.where(at == cols[...] * per + i, 1.0, 0.0) for i in range(per)], axis=1)
    picked = lax.dot_general(
        hits.astype(jnp.bfloat16), table, (((0,), (0,)), ((), ())), preferred_element_type=jnp.float32
    )
    picked = jnp.concatenate([picked[i * n_blocks : (i + 1) * n_blocks] for i in range(per)], axis=1)
    picked = picked.astype(jnp.bfloat16)
    which = lax.broadcasted_iota(jnp.int32, (n_blocks, size), 0)
    terms = jnp.zeros((n_blocks, size), jnp.float32)
    for k in range(n_blocks):
        terms = jnp.where(which == k, jnp.dot(picked, blocks[k], preferred_element_type=jnp.float32), terms)
    one = terms.astype(jnp.bfloat16)
    rest = terms - one.astype(jnp.float32)
    two = rest.astype(jnp.bfloat16)
    three = (rest - two.astype(jnp.float32)).astype(jnp.bfloat16)
    right = jnp.concatenate(
        [p[:, i * width : (i + 1) * width] for p in (one, two, three) for i in range(per)], axis=0
    )
    at = lax.broadcasted_iota(jnp.int32, (n_rows, n_blocks), 0)
    hits = [jnp.where(at == rows[...] * per + i, 1.0, 0.0) for i in range(per)]
    left = jnp.concatenate(hits * 3, axis=1).astype(jnp.bfloat16)
    out[...] = own[...].reshape(n_rows, width).astype(jnp.float32) + jnp.dot(
        left, right, preferred_element_type=jnp.float32
    )


def covariance(cols, rows, every, own, blocks):
    n_dev, size_x, size_z, width = every.shape
    return pl.pallas_call(
        covariance_kernel,
        out_shape=jax.ShapeDtypeStruct((size_x * size_z, width), jnp.float32),
        in_specs=[VMEM] * 5,
        out_specs=VMEM,
        compiler_params=PARAMS,
        name="covariance",
    )(cols, rows, every, own, held(blocks))


def local(
    conductivity,
    initial_field,
    adjoint_initial,
    src_cell,
    src_amp,
    rec_cell,
    observed,
    cov_blocks,
    cov_rows,
    cov_cols,
):
    size_x, size_z, size_y = conductivity.shape
    n_dev = lax.axis_size("brick") * lax.axis_size("depth")
    *sent, x0, cond, a0 = pack(
        initial_field, conductivity, adjoint_initial, src_cell[0], src_amp[0, 0], rec_cell[0], observed[0, 0]
    )
    x0, cond, a0 = held(x0), held(cond), held(a0)
    first, second = swap(*sent, "brick")
    blocks = turn(cov_blocks[0, 0])
    sent2 = mid(x0, cond, a0, sent[0], first, second, blocks)
    wide = prep(x0, cond, a0, sent2[0], first, second)
    first2, second2 = swap(*sent2, "depth")
    v, w, sums = chain(wide, first2, second2, size_x, size_z, n_dev)
    every = lax.all_to_all(sums, BOTH, 0, 0, tiled=True)
    forward, gradient = combine(every, x0, a0, v, w)
    every_block = lax.all_gather(gradient, "depth", axis=0, tiled=False)
    out = covariance(cov_cols[0], cov_rows[0], every_block, gradient, blocks)
    return (forward, out.reshape(size_x, size_z, size_y))


def solution(mesh):
    return jax.shard_map(
        local,
        mesh=mesh,
        in_specs=(
            P("brick", "depth", None),
            P(None, "brick", "depth", None),
            P(None, "brick", "depth", None),
            P("brick", "depth", None),
            P("brick", "depth", None, None),
            P("brick", "depth", None),
            P("brick", "depth", None, None),
            P("brick", "depth", None, None, None),
            P("brick", "depth", None),
            P("brick", "depth", None),
        ),
        out_specs=(P(None, "brick", "depth", None), P("brick", "depth", None)),
        check_vma=False,
    )
```

```python
import functools

import jax
import jax.numpy as jnp
from jax import lax
from jax.experimental import pallas as pl
from jax.experimental.pallas import tpu as pltpu
from jax.sharding import PartitionSpec as P

LAPLACE_SHIFTS = (0.5, 2.0)
BOTH = ("brick", "depth")
HX = 6
HC = 5
HA = 4
HU = 3
ZP = 8
THETA = 6.0
PAIRS = tuple((k, l) for k in range(4) for l in range(k, 4))
SLOTS = 32
VMEM = pl.BlockSpec(memory_space=pltpu.VMEM)
SMEM = pl.BlockSpec(memory_space=pltpu.SMEM)
HBM = pl.BlockSpec(memory_space=pltpu.HBM)
NT = (((1,), (1,)), ((), ()))
PARAMS = pltpu.CompilerParams(vmem_limit_bytes=28 * 1024 * 1024)


def held(a):
    return pltpu.with_memory_space_constraint(a, pltpu.VMEM)


def in_hbm(a):
    return pltpu.with_memory_space_constraint(a, pltpu.HBM)


def is_odd(axis):
    return lax.rem(lax.axis_index(axis), 2) == 1


def pairings(axis):
    size = lax.axis_size(axis)
    first = [(i, i ^ 1) for i in range(size) if (i ^ 1) < size]
    second = [(i, j) for i in range(size) for j in [((i + 1) ^ 1) - 1] if 0 <= j < size]
    return first, second


def swap(first, second, axis):
    one, two = pairings(axis)
    return lax.ppermute(first, axis, one), lax.ppermute(second, axis, two)


LX, LC, LA = 0, 2 * HX, 2 * HX + HC
LP = LA + 2 * HA


def pack_kernel(*refs):
    ins, (first, second), sides, kept, pieces = refs[:7], refs[7:9], refs[9:11], refs[11:14], refs[14:18]
    table, sems = refs[18:]
    copies = [
        pltpu.make_async_copy(a, b, sems.at[i]) for i, (a, b) in enumerate(zip(ins, kept + pieces))
    ]
    for copy in copies:
        copy.start()
    for copy in copies:
        copy.wait()
    x0, cond, a0 = kept
    src_cell, src_amp, rec_cell, observed = pieces
    size_x, size_z, size_y = cond.shape
    odd = is_odd("brick")

    def split(v):
        one = v.astype(jnp.bfloat16).astype(jnp.float32)
        two = (v - one).astype(jnp.bfloat16).astype(jnp.float32)
        return one, two, v - one - two

    table[...] = jnp.zeros_like(table)
    for base, cells, amounts in ((0, src_cell, src_amp), (8, rec_cell, observed)):
        n = cells.shape[-1]
        at = cells[...].astype(jnp.float32)
        hi = jnp.floor((at + 0.5) * (1.0 / size_y))
        table[base : base + 1, :n] = hi + 1.0
        table[base + 1 : base + 2, :n] = at - hi * size_y
        for s, part in enumerate(split(amounts[...])):
            table[base + 2 + 2 * s : base + 4 + 2 * s, :n] = part
    points = table[...].astype(jnp.bfloat16)
    for out, low in ((first, odd), (second, jnp.logical_not(odd))):
        for f in range(2):
            for i in range(HX):
                out[LX + f * HX + i] = x0[f, jnp.where(low, i, size_x - HX + i)].astype(jnp.bfloat16)
            for i in range(HA):
                out[LA + f * HA + i] = a0[f, jnp.where(low, i, size_x - HA + i)].astype(jnp.bfloat16)
        for i in range(HC):
            out[LC + i] = cond[jnp.where(low, i, size_x - HC + i)].astype(jnp.bfloat16)
        out[LP] = points
    put = depth_writer(*sides, size_z)
    fill_depth(
        put,
        [[(lambda i, f=f: x0[f, i]) for f in range(2)], lambda i: cond[i], [(lambda i, f=f: a0[f, i]) for f in range(2)]],
        [list(range(size_x))] * 3,
        size_z,
    )


def depth_writer(out_first, out_second, size_z):
    odd = is_odd("depth")

    def put(at, down, up):
        down = jnp.concatenate(down, axis=0)
        up = jnp.concatenate(up, axis=0)
        out_first[at] = jnp.where(odd, down, up).astype(jnp.bfloat16)
        out_second[at] = jnp.where(odd, up, down).astype(jnp.bfloat16)

    return put


def fill_depth(put, readers, chosen, size_z):
    fields, conds, adjoints = readers
    at = 0
    for i in chosen[0]:
        rows = [r(i) for r in fields]
        put(at, [r[:ZP] for r in rows], [r[size_z - ZP :] for r in rows])
        at += 1
    for i, j in zip(chosen[1][::2], chosen[1][1::2]):
        rows = [conds(i), conds(j)]
        put(at, [r[:ZP] for r in rows], [r[size_z - ZP :] for r in rows])
        at += 1
    for i, j in zip(chosen[2][::2], chosen[2][1::2]):
        rows = [r(n) for n in (i, j) for r in adjoints]
        put(at, [r[:HA] for r in rows], [r[size_z - HA :] for r in rows])
        at += 1
    return at


def empty_depth(x0, cond, a0, chosen, low, high, top):
    gap = jnp.zeros((ZP - HA, x0.shape[-1]), jnp.float32)
    at = 0
    for i in chosen[0]:
        a, b = low(at), high(at)
        for f in range(2):
            x0[f, i, 0:ZP] = a[f * ZP : (f + 1) * ZP]
            x0[f, i, top : top + ZP] = b[f * ZP : (f + 1) * ZP]
        at += 1
    for pair in zip(chosen[1][::2], chosen[1][1::2]):
        a, b = low(at), high(at)
        for n, i in enumerate(pair):
            cond[i, 0:ZP] = a[n * ZP : (n + 1) * ZP]
            cond[i, top : top + ZP] = b[n * ZP : (n + 1) * ZP]
        at += 1
    for pair in zip(chosen[2][::2], chosen[2][1::2]):
        a, b = low(at), high(at)
        for n, i in enumerate(pair):
            for f in range(2):
                part = slice((2 * n + f) * HA, (2 * n + f + 1) * HA)
                a0[f, i, 0:ZP] = jnp.concatenate([gap, a[part]], axis=0)
                a0[f, i, top : top + ZP] = jnp.concatenate([b[part], gap], axis=0)
        at += 1
    return at


def own_rows(size_x):
    return [list(range(h, h + size_x)) for h in (HX, HC, HA)]


def corner_rows(size_x):
    return [list(range(1, h)) + list(range(h + size_x, size_x + 2 * h - 1)) for h in (HX, HC, HA)]


def tiles_of(chosen):
    return len(chosen[0]) + len(chosen[1]) // 2 + len(chosen[2]) // 2


def sides_of(axis, first, second):
    odd = is_odd(axis)

    def low(at):
        return jnp.where(odd, first[at].astype(jnp.float32), second[at].astype(jnp.float32))

    def high(at):
        return jnp.where(odd, second[at].astype(jnp.float32), first[at].astype(jnp.float32))

    return low, high


def pack(*ins):
    x0, cond, a0 = ins[:3]
    shape = (LP + 1,) + cond.shape[1:]
    return pl.pallas_call(
        pack_kernel,
        out_shape=(jax.ShapeDtypeStruct(shape, jnp.bfloat16),) * 2
        + (jax.ShapeDtypeStruct((tiles_of(own_rows(cond.shape[0])),) + shape[1:], jnp.bfloat16),) * 2
        + tuple(pltpu.VMEM(a.shape, a.dtype) for a in ins[:3]),
        in_specs=[HBM] * 7,
        out_specs=(VMEM,) * 7,
        scratch_shapes=[pltpu.VMEM(a.shape, a.dtype) for a in ins[3:]]
        + [pltpu.VMEM(cond.shape[1:], jnp.float32), pltpu.SemaphoreType.DMA((7,))],
        compiler_params=PARAMS,
        name="pack",
    )(*[in_hbm(a) for a in ins])


def joined_rows(x0, cond, a0, first, second):
    size_x = cond.shape[0]
    low, high = sides_of("brick", first, second)

    def reader(own, base, halo):
        def row(i):
            if i < halo:
                return low(base + i)
            if i >= halo + size_x:
                return high(base + i - halo - size_x)
            return own(i - halo)
        return row

    fields = [reader(lambda i, f=f: x0[f, i], LX + f * HX, HX) for f in range(2)]
    adjoints = [reader(lambda i, f=f: a0[f, i], LA + f * HA, HA) for f in range(2)]
    return fields, reader(lambda i: cond[i], LC, HC), adjoints, low, high


def mid_kernel(x0, cond, a0, sent, first, second, *refs):
    out_first, out_second = refs[-2:]
    size_x, size_z, size_y = cond.shape
    fields, conds, adjoints, low, high = joined_rows(x0, cond, a0, first, second)
    n = size_y // 4
    points = low(LP) + pltpu.roll(sent[LP].astype(jnp.float32), n, 1) + pltpu.roll(high(LP), 2 * n, 1)
    at = fill_depth(
        depth_writer(out_first, out_second, size_z), [fields, conds, adjoints], corner_rows(size_x), size_z
    )
    out_first[at] = points.astype(jnp.bfloat16)
    out_second[at] = points.astype(jnp.bfloat16)


def mid(x0, cond, a0, sent, first, second, *ready):
    size_x, size_z, size_y = cond.shape
    shape = (tiles_of(corner_rows(size_x)) + 1, size_z, size_y)
    return pl.pallas_call(
        mid_kernel,
        out_shape=(jax.ShapeDtypeStruct(shape, jnp.bfloat16),) * 2,
        in_specs=[VMEM] * (6 + len(ready)),
        out_specs=(VMEM, VMEM),
        compiler_params=PARAMS,
        name="mid",
    )(x0, cond, a0, sent, first, second, *[held(a) for a in ready])


def place(t, q, weights, halo, dst, lists, size_x, size_z, size_y):
    n_list = lists.shape[-1]
    each = n_list // 4
    lane = lax.broadcasted_iota(jnp.int32, (1, n_list), 1)
    dx = jnp.where(lane < each, -1, jnp.where(lane < 2 * each, 0, 1))
    nx = size_x + 2 * halo
    hi = lists[q : q + 1] - 1.0
    lo = lists[q + 1 : q + 2].astype(jnp.int32)
    x = jnp.floor((hi + 0.5) * (1.0 / size_z))
    z = (hi - x * size_z).astype(jnp.int32)
    row_x = x.astype(jnp.int32) + halo + size_x * dx
    ok = (hi >= 0.0) & (row_x >= 0) & (row_x < nx)
    if t == 1:
        depth, z0 = size_z, ZP
        target = row_x * size_z + z
    elif t == 0:
        depth, z0 = ZP, 0
        target = row_x * ZP + z - (size_z - ZP)
        ok = ok & (z >= size_z - ZP)
    else:
        depth, z0 = ZP, ZP + size_z
        target = row_x * ZP + z
        ok = ok & (z < ZP)
    target = jnp.where(ok, target, -1)
    hit = lax.broadcasted_iota(jnp.int32, (nx * depth, n_list), 0) == target
    right = (lax.broadcasted_iota(jnp.int32, (size_y, n_list), 0) == lo).astype(jnp.float32).astype(jnp.bfloat16)
    terms = [(n, p) for n, parts in weights for p in parts]
    left = jnp.concatenate([jnp.where(hit, 1.0 if p is None else lists[p : p + 1], 0.0) for _, p in terms], axis=0)
    placed = lax.dot_general(left.astype(jnp.bfloat16), right, NT, preferred_element_type=jnp.float32)
    totals = {}
    for i, (n, _) in enumerate(terms):
        part = placed[i * nx * depth : (i + 1) * nx * depth]
        totals[n] = totals[n] + part if n in totals else part
    for n, total in totals.items():
        dst[n, :, z0 : z0 + depth, :] = total.reshape(nx, depth, size_y)


SRC_WEIGHTS = ((0, (2, 4, 6)), (1, (3, 5, 7)))
REC_WEIGHTS = ((0, (10, 12, 14)), (1, (11, 13, 15)), (2, (None,)))


def prep_kernel(x0, cond, a0, sent2, first, second, side_first, side_second, x0_w, cond_w, a0_w, src, rec):
    size_x, size_z, size_y = cond.shape
    fields, conds, adjoints, _, _ = joined_rows(x0, cond, a0, first, second)
    own = slice(ZP, ZP + size_z)
    for f in range(2):
        for i in range(size_x + 2 * HX):
            x0_w[f, i, own] = fields[f](i)
        for i in range(size_x + 2 * HA):
            a0_w[f, i, own] = adjoints[f](i)
    for i in range(size_x + 2 * HC):
        cond_w[i, own] = conds(i)
    empty_depth(x0_w, cond_w, a0_w, own_rows(size_x), *sides_of("depth", side_first, side_second), ZP + size_z)
    lists = sent2[sent2.shape[0] - 1].astype(jnp.float32)
    place(1, 0, SRC_WEIGHTS, HC, src, lists, size_x, size_z, size_y)
    place(1, 8, REC_WEIGHTS, HU, rec, lists, size_x, size_z, size_y)


def wide_shapes(size_x, size_z, size_y):
    slab = (size_z + 2 * ZP, size_y)
    return (
        (2, size_x + 2 * HX) + slab,
        (size_x + 2 * HC,) + slab,
        (2, size_x + 2 * HA) + slab,
        (2, size_x + 2 * HC) + slab,
        (3, size_x + 2 * HU) + slab,
    )


def prep(x0, cond, a0, sent2, first, second, side_first, side_second):
    shapes = wide_shapes(*cond.shape)
    return pl.pallas_call(
        prep_kernel,
        out_shape=tuple(pltpu.VMEM(s, jnp.float32) for s in shapes),
        in_specs=[VMEM] * 8,
        out_specs=(VMEM,) * 5,
        compiler_params=PARAMS,
        name="prep",
    )(x0, cond, a0, sent2, first, second, side_first, side_second)


def beside_z_y(c):
    rows, width = c.shape
    half = width // 2
    total = pltpu.roll(c, 1, 0) + pltpu.roll(c, rows - 1, 0)
    lane = lax.broadcasted_iota(jnp.int32, (rows, half), 1)
    first = lane == 0
    last = lane == half - 1
    a, b = c[:, :half], c[:, half:]
    ra, rb = pltpu.roll(a, 1, 1), pltpu.roll(b, 1, 1)
    la, lb = pltpu.roll(a, half - 1, 1), pltpu.roll(b, half - 1, 1)
    ya = jnp.where(first, 0.0, ra) + jnp.where(last, lb, la)
    yb = jnp.where(first, ra, rb) + jnp.where(last, 0.0, lb)
    return total + jnp.concatenate([ya, yb], axis=1)


def chain_kernel(size_x, size_z, x0_in, cond_in, a0_in, src_in, rec_in, first, second,
                 x0, cond, a0, src, rec, v0, v1, v2, u, w1, w2, sums_out, w3, acc):
    rows_z = x0.shape[-2]
    size_y = x0.shape[-1]
    own = slice(ZP, ZP + size_z)
    top = ZP + size_z

    low, high = sides_of("depth", first, second)
    blank = jnp.zeros((ZP, size_y), jnp.float32)
    at = empty_depth(x0, cond, a0, corner_rows(size_x), low, high, top)
    for ref, lead in ((x0, 2), (cond, 0), (a0, 2)):
        n = ref.shape[-3]
        for i in (0, n - 1):
            for z in (slice(0, ZP), slice(top, top + ZP)):
                if lead:
                    for f in range(lead):
                        ref[f, i, z] = blank
                else:
                    ref[i, z] = blank
    for t, lists in ((0, low(at)), (2, high(at))):
        place(t, 0, SRC_WEIGHTS, HC, src, lists, size_x, size_z, size_y)
        place(t, 8, REC_WEIGHTS, HU, rec, lists, size_x, size_z, size_y)

    def edge(axis):
        at = lax.axis_index(axis)
        return (at > 0).astype(jnp.float32), (at < lax.axis_size(axis) - 1).astype(jnp.float32)

    low_x, high_x = edge("brick")
    low_z, high_z = edge("depth")
    def inside(value, i, halo):
        in_x = low_x if i < halo else high_x if i >= halo + size_x else None
        parts = [value[:ZP] * low_z, value[own], value[top:] * high_z]
        if in_x is not None:
            parts = [p * in_x for p in parts]
        return jnp.concatenate(parts, axis=0)

    def apply(ref, idx, i, damp):
        c = ref[idx + (i,)]
        return damp * c - (ref[idx + (i - 1,)] + ref[idx + (i + 1,)] + beside_z_y(c))

    def loop(n, body):
        for i in range(n):
            body(i)

    def first(i):
        for f, s in enumerate(LAPLACE_SHIFTS):
            v0[f, i] = inside(src[f, i] - apply(x0, (f,), i + 1, s * cond[i] + THETA), i, HC)

    loop(size_x + 2 * HC, first)

    def second(i):
        for f, s in enumerate(LAPLACE_SHIFTS):
            v1[f, i] = inside(apply(v0, (f,), i + 1, s * cond[i + 1]), i, 4)

    loop(size_x + 8, second)

    def third(i):
        for f, s in enumerate(LAPLACE_SHIFTS):
            v2[f, i] = inside(apply(v1, (f,), i + 1, s * cond[i + 2]), i, 3)

    loop(size_x + 6, third)

    def start(i):
        many = rec[2, i]
        for f, s in enumerate(LAPLACE_SHIFTS):
            u[0, f, i] = inside(
                many * x0[f, i + 3] - rec[f, i] - apply(a0, (f,), i + 1, s * cond[i + 2] + THETA), i, HU
            )
            u[1, f, i] = many * v0[f, i + 2]
            u[2, f, i] = many * v1[f, i + 1]
            u[3, f, i] = many * v2[f, i]

    loop(size_x + 2 * HU, start)

    def level(src_ref, dst_ref, halo):
        def body(i):
            for f, s in enumerate(LAPLACE_SHIFTS):
                damp = s * cond[i + HC - halo]
                for k in range(4):
                    dst_ref[k, f, i] = inside(apply(src_ref, (k, f), i + 1, damp), i, halo)
        loop(size_x + 2 * halo, body)

    level(u, w1, 2)
    level(w1, w2, 1)

    def last(i):
        for f, s in enumerate(LAPLACE_SHIFTS):
            damp = s * cond[i + HC]
            for k in range(4):
                w3[k, f, i] = apply(w2, (k, f), i + 1, damp)[own]

    loop(size_x, last)

    def tiles(a):
        total = None
        for z in range(0, a.shape[0], 8):
            for y in range(0, a.shape[1], 128):
                t = a[z : z + 8, y : y + 128]
                total = t if total is None else total + t
        return total

    zero = jnp.zeros((8, 128), jnp.float32)

    def over_rows(body, carry, unroll=8):
        def step(i, carry):
            for j in range(unroll):
                carry = body(i * unroll + j, carry)
            return carry

        return lax.fori_loop(0, size_x // unroll, step, carry)

    for f, s in enumerate(LAPLACE_SHIFTS):
        def forward_sums(i, carry, f=f, s=s):
            p0 = v0[f, i + 5, own]
            p1 = v1[f, i + 4, own]
            p2 = v2[f, i + 3, own]
            p3 = apply(v2, (f,), i + 3, s * cond[i + 5])[own]
            made = (p0 * p0, p0 * p1, p1 * p1, p1 * p2, p2 * p2, p2 * p3)
            return tuple(c + tiles(a) for c, a in zip(carry, made))
        done = over_rows(forward_sums, (zero,) * 6)
        for j in range(6):
            acc[j * SLOTS + 2 * len(PAIRS) + f] = done[j]

    levels = ((u, 3, own), (w1, 2, own), (w2, 1, own), (w3, 0, slice(0, size_z)))
    for j in range(3):
        ra, oa, za = levels[j]
        rb, ob, zb = levels[j + 1]
        for f in range(2):
            def pair_sums(i, carry, f=f):
                a = [ra[k, f, i + oa, za] for k in range(4)]
                b = [rb[k, f, i + ob, zb] for k in range(4)]
                made = [a[k] * a[l] for k, l in PAIRS] + [a[k] * b[l] for k, l in PAIRS]
                return tuple(c + tiles(m) for c, m in zip(carry, made))
            done = over_rows(pair_sums, (zero,) * (2 * len(PAIRS)), 2)
            for n in range(len(PAIRS)):
                acc[2 * j * SLOTS + 2 * n + f] = done[n]
                acc[(2 * j + 1) * SLOTS + 2 * n + f] = done[len(PAIRS) + n]

    for j in range(acc.shape[0] // SLOTS):
        for n in range(0 if j >= 6 else 2 * len(PAIRS) + 2, SLOTS):
            acc[j * SLOTS + n] = zero
    by_lane = jnp.sum(acc[...], axis=1)
    ones = jnp.ones((8, 128), jnp.float32)
    out = lax.dot_general(ones, by_lane, NT, precision=lax.Precision.HIGHEST, preferred_element_type=jnp.float32)
    out = jnp.concatenate([out[0:1, :128], out[0:1, 128:]], axis=0)
    sums_out[...] = jnp.broadcast_to(out[None], sums_out.shape)


def chain(wide, first, second, size_x, size_z, n_dev):
    size_y = wide[0].shape[-1]
    f32 = jnp.float32
    slab = (size_z + 2 * ZP, size_y)
    outs = tuple(pltpu.VMEM(a.shape, f32) for a in wide) + (
        pltpu.VMEM((2, size_x + 2 * HC) + slab, f32),
        pltpu.VMEM((2, size_x + 8) + slab, f32),
        pltpu.VMEM((2, size_x + 6) + slab, f32),
        pltpu.VMEM((4, 2, size_x + 6) + slab, f32),
        pltpu.VMEM((4, 2, size_x + 4) + slab, f32),
        pltpu.VMEM((4, 2, size_x + 2) + slab, f32),
        jax.ShapeDtypeStruct((n_dev, 2, 128), f32),
    )
    scratch = [
        pltpu.VMEM((4, 2, size_x, size_z, size_y), f32),
        pltpu.VMEM((256, 8, 128), f32),
    ]
    return pl.pallas_call(
        functools.partial(chain_kernel, size_x, size_z),
        out_shape=outs,
        in_specs=[VMEM] * 7,
        out_specs=(VMEM,) * len(outs),
        scratch_shapes=scratch,
        input_output_aliases={i: i for i in range(5)},
        compiler_params=PARAMS,
        name="chain",
    )(*[held(a) for a in wide], first, second)[5:]


def coefficients(mu):
    a = [[mu[i + j + 1] + THETA * mu[i + j] for j in range(3)] for i in range(3)]

    def inverse(pivot, size):
        good = pivot > 1e-6 * size
        return jnp.where(good, 1.0 / jnp.where(good, pivot, 1.0), 0.0)

    i0 = inverse(a[0][0], 0.0)
    l10 = a[0][1] * i0
    l20 = a[0][2] * i0
    i1 = inverse(a[1][1] - l10 * a[0][1], a[1][1])
    e21 = a[1][2] - l10 * a[0][2]
    l21 = e21 * i1
    i2 = inverse(a[2][2] - l20 * a[0][2] - l21 * e21, a[2][2])
    y0 = mu[0]
    y1 = mu[1] - l10 * y0
    y2 = mu[2] - l20 * y0 - l21 * y1
    c2 = y2 * i2
    c1 = y1 * i1 - l21 * c2
    c0 = y0 * i0 - l10 * c1 - l20 * c2
    return c0, c1, c2


def combine_kernel(every, x0, a0, v0, v1, v2, u, w1, w2, forward, gradient):
    total = jnp.sum(every[...], axis=0)
    per = 128 // SLOTS
    rows = jnp.concatenate(
        [total[j // per : j // per + 1, j % per * SLOTS : (j % per + 1) * SLOTS] for j in range(6)], axis=0
    )
    rows = jnp.concatenate([rows, jnp.zeros((2, SLOTS), jnp.float32)], axis=0)
    rows = jnp.concatenate([rows, jnp.zeros((8, 128 - SLOTS), jnp.float32)], axis=1)
    n_pair = 2 * len(PAIRS)
    at = lax.broadcasted_iota(jnp.int32, (128, 128), 0)
    to = lax.broadcasted_iota(jnp.int32, (128, 128), 1)
    same = (at & 1) == (to & 1)

    def gather_lanes(values, chosen):
        table = jnp.where(same & chosen, 1.0, 0.0)
        return jnp.dot(values, table, precision=lax.Precision.HIGHEST, preferred_element_type=jnp.float32)

    mu = gather_lanes(rows, (at >= n_pair) & (at < n_pair + 2))
    c = coefficients([mu[j : j + 1] for j in range(6)])
    basis = (jnp.ones_like(c[0]),) + c
    pair = lax.broadcasted_iota(jnp.int32, (1, 128), 1) // 2
    weight = jnp.zeros((1, 128), jnp.float32)
    for n, (k, l) in enumerate(PAIRS):
        product = basis[k] * basis[l] * (1.0 if k == l else 2.0)
        weight = jnp.where(pair == n, product, weight)
    nu = gather_lanes(rows * weight, at < n_pair)
    d = coefficients([nu[j : j + 1] for j in range(6)])
    size_x, size_z = x0.shape[1:3]
    own = slice(ZP, ZP + size_z)
    v = ((v0, 5), (v1, 4), (v2, 3))
    w = ((u, 3), (w1, 2), (w2, 1))
    scale = []
    for f in range(2):
        up = [c[k][:, f : f + 1] for k in range(3)]
        down = [[(d[j] * basis[k])[:, f : f + 1] for k in range(4)] for j in range(3)]
        scale.append((up, down))
    for i in range(size_x):
        total = None
        for f, s in enumerate(LAPLACE_SHIFTS):
            up, down = scale[f]
            field = x0[f, i]
            for k in range(3):
                field = field + up[k] * v[k][0][f, i + v[k][1], own]
            other = a0[f, i]
            for j in range(3):
                for k in range(4):
                    other = other + down[j][k] * w[j][0][k, f, i + w[j][1], own]
            forward[f, i] = field
            part = s * field * other
            total = part if total is None else total + part
        gradient[i] = (-total).astype(gradient.dtype)


def combine(every, x0, a0, *made):
    return pl.pallas_call(
        combine_kernel,
        out_shape=(
            jax.ShapeDtypeStruct(x0.shape, jnp.float32),
            jax.ShapeDtypeStruct(x0.shape[1:], jnp.bfloat16),
        ),
        in_specs=[VMEM] * (3 + len(made)),
        out_specs=(VMEM, VMEM),
        compiler_params=PARAMS,
        name="combine",
    )(every, x0, a0, *[held(a) for a in made])


def turn_kernel(blocks, out, buf, sems):
    n = buf.shape[0]
    copies = [pltpu.make_async_copy(blocks.at[k], buf.at[k], sems.at[k]) for k in range(n)]
    for copy in copies:
        copy.start()
    for k, copy in enumerate(copies):
        copy.wait()
        out[k] = buf[k].T


def turn(blocks):
    return pl.pallas_call(
        turn_kernel,
        out_shape=pltpu.VMEM(blocks.shape, blocks.dtype),
        in_specs=[HBM],
        out_specs=VMEM,
        scratch_shapes=[
            pltpu.VMEM(blocks.shape, blocks.dtype),
            pltpu.SemaphoreType.DMA((blocks.shape[0],)),
        ],
        compiler_params=PARAMS,
        name="turn",
    )(in_hbm(blocks))


def covariance_kernel(cols, rows, every, own, blocks, out):
    n_dev, size_x, size_z, width = every.shape
    n_rows = size_x * size_z
    n_blocks, size, _ = blocks.shape
    per = size // width
    table = every[...].reshape(n_dev * n_rows, width)
    at = lax.broadcasted_iota(jnp.int32, (n_dev * n_rows, n_blocks), 0)
    hits = jnp.concatenate([jnp.where(at == cols[...] * per + i, 1.0, 0.0) for i in range(per)], axis=1)
    picked = lax.dot_general(
        hits.astype(jnp.bfloat16), table, (((0,), (0,)), ((), ())), preferred_element_type=jnp.float32
    )
    picked = jnp.concatenate([picked[i * n_blocks : (i + 1) * n_blocks] for i in range(per)], axis=1)
    picked = picked.astype(jnp.bfloat16)
    which = lax.broadcasted_iota(jnp.int32, (n_blocks, size), 0)
    terms = jnp.zeros((n_blocks, size), jnp.float32)
    for k in range(n_blocks):
        terms = jnp.where(which == k, jnp.dot(picked, blocks[k], preferred_element_type=jnp.float32), terms)
    one = terms.astype(jnp.bfloat16)
    rest = terms - one.astype(jnp.float32)
    two = rest.astype(jnp.bfloat16)
    three = (rest - two.astype(jnp.float32)).astype(jnp.bfloat16)
    right = jnp.concatenate(
        [p[:, i * width : (i + 1) * width] for p in (one, two, three) for i in range(per)], axis=0
    )
    at = lax.broadcasted_iota(jnp.int32, (n_rows, n_blocks), 0)
    hits = [jnp.where(at == rows[...] * per + i, 1.0, 0.0) for i in range(per)]
    left = jnp.concatenate(hits * 3, axis=1).astype(jnp.bfloat16)
    out[...] = own[...].reshape(n_rows, width).astype(jnp.float32) + jnp.dot(
        left, right, preferred_element_type=jnp.float32
    )


def covariance(cols, rows, every, own, blocks):
    n_dev, size_x, size_z, width = every.shape
    return pl.pallas_call(
        covariance_kernel,
        out_shape=jax.ShapeDtypeStruct((size_x * size_z, width), jnp.float32),
        in_specs=[VMEM] * 5,
        out_specs=VMEM,
        compiler_params=PARAMS,
        name="covariance",
    )(cols, rows, every, own, held(blocks))


def local(
    conductivity,
    initial_field,
    adjoint_initial,
    src_cell,
    src_amp,
    rec_cell,
    observed,
    cov_blocks,
    cov_rows,
    cov_cols,
):
    size_x, size_z, size_y = conductivity.shape
    n_dev = lax.axis_size("brick") * lax.axis_size("depth")
    *sent, side_low, side_high, x0, cond, a0 = pack(
        initial_field, conductivity, adjoint_initial, src_cell[0], src_amp[0, 0], rec_cell[0], observed[0, 0]
    )
    x0, cond, a0 = held(x0), held(cond), held(a0)
    first, second = swap(*sent, "brick")
    sides = swap(side_low, side_high, "depth")
    blocks = turn(cov_blocks[0, 0])
    sent2 = mid(x0, cond, a0, sent[0], first, second, blocks, *sides)
    wide = prep(x0, cond, a0, sent2[0], first, second, *sides)
    first2, second2 = swap(*sent2, "depth")
    *made, sums = chain(wide, first2, second2, size_x, size_z, n_dev)
    every = lax.all_to_all(sums, BOTH, 0, 0, tiled=True)
    forward, gradient = combine(every, x0, a0, *made)
    every_block = lax.all_gather(gradient, "depth", axis=0, tiled=False)
    out = covariance(cov_cols[0], cov_rows[0], every_block, gradient, blocks)
    return (forward, out.reshape(size_x, size_z, size_y))


def solution(mesh):
    return jax.shard_map(
        local,
        mesh=mesh,
        in_specs=(
            P("brick", "depth", None),
            P(None, "brick", "depth", None),
            P(None, "brick", "depth", None),
            P("brick", "depth", None),
            P("brick", "depth", None, None),
            P("brick", "depth", None),
            P("brick", "depth", None, None),
            P("brick", "depth", None, None, None),
            P("brick", "depth", None),
            P("brick", "depth", None),
        ),
        out_specs=(P(None, "brick", "depth", None), P("brick", "depth", None)),
        check_vma=False,
    )
```

```python
import functools

import jax
import jax.numpy as jnp
from jax import lax
from jax.experimental import pallas as pl
from jax.experimental.pallas import tpu as pltpu
from jax.sharding import PartitionSpec as P

LAPLACE_SHIFTS = (0.5, 2.0)
BOTH = ("brick", "depth")
HX = 6
HC = 5
HA = 4
HU = 3
ZP = 8
THETA = 6.0
PAIRS = tuple((k, l) for k in range(4) for l in range(k, 4))
SLOTS = 32
VMEM = pl.BlockSpec(memory_space=pltpu.VMEM)
SMEM = pl.BlockSpec(memory_space=pltpu.SMEM)
HBM = pl.BlockSpec(memory_space=pltpu.HBM)
NT = (((1,), (1,)), ((), ()))
PARAMS = pltpu.CompilerParams(vmem_limit_bytes=28 * 1024 * 1024)


def held(a):
    return pltpu.with_memory_space_constraint(a, pltpu.VMEM)


def in_hbm(a):
    return pltpu.with_memory_space_constraint(a, pltpu.HBM)


def is_odd(axis):
    return lax.rem(lax.axis_index(axis), 2) == 1


def pairings(axis):
    size = lax.axis_size(axis)
    first = [(i, i ^ 1) for i in range(size) if (i ^ 1) < size]
    second = [(i, j) for i in range(size) for j in [((i + 1) ^ 1) - 1] if 0 <= j < size]
    return first, second


def swap(first, second, axis):
    one, two = pairings(axis)
    return lax.ppermute(first, axis, one), lax.ppermute(second, axis, two)


LX, LC, LA = 0, 2 * HX, 2 * HX + HC
LP = LA + 2 * HA


def pack_kernel(*refs):
    ins, (first, second), sides, kept, pieces = refs[:7], refs[7:9], refs[9:11], refs[11:14], refs[14:18]
    table, sems = refs[18:]
    copies = [
        pltpu.make_async_copy(a, b, sems.at[i]) for i, (a, b) in enumerate(zip(ins, kept + pieces))
    ]
    for copy in copies:
        copy.start()
    for copy in copies:
        copy.wait()
    x0, cond, a0 = kept
    src_cell, src_amp, rec_cell, observed = pieces
    size_x, size_z, size_y = cond.shape
    odd = is_odd("brick")

    def split(v):
        one = v.astype(jnp.bfloat16).astype(jnp.float32)
        two = (v - one).astype(jnp.bfloat16).astype(jnp.float32)
        return one, two, v - one - two

    table[...] = jnp.zeros_like(table)
    for base, cells, amounts in ((0, src_cell, src_amp), (8, rec_cell, observed)):
        n = cells.shape[-1]
        at = cells[...].astype(jnp.float32)
        hi = jnp.floor((at + 0.5) * (1.0 / size_y))
        table[base : base + 1, :n] = hi + 1.0
        table[base + 1 : base + 2, :n] = at - hi * size_y
        for s, part in enumerate(split(amounts[...])):
            table[base + 2 + 2 * s : base + 4 + 2 * s, :n] = part
    points = table[...].astype(jnp.bfloat16)
    for out, low in ((first, odd), (second, jnp.logical_not(odd))):
        for f in range(2):
            for i in range(HX):
                out[LX + f * HX + i] = x0[f, jnp.where(low, i, size_x - HX + i)].astype(jnp.bfloat16)
            for i in range(HA):
                out[LA + f * HA + i] = a0[f, jnp.where(low, i, size_x - HA + i)].astype(jnp.bfloat16)
        for i in range(HC):
            out[LC + i] = cond[jnp.where(low, i, size_x - HC + i)].astype(jnp.bfloat16)
        out[LP] = points
    put = depth_writer(*sides, size_z)
    fill_depth(
        put,
        [[(lambda i, f=f: x0[f, i]) for f in range(2)], lambda i: cond[i], [(lambda i, f=f: a0[f, i]) for f in range(2)]],
        [list(range(size_x))] * 3,
        size_z,
    )


def depth_writer(out_first, out_second, size_z):
    odd = is_odd("depth")

    def put(at, down, up):
        down = jnp.concatenate(down, axis=0)
        up = jnp.concatenate(up, axis=0)
        out_first[at] = jnp.where(odd, down, up).astype(jnp.bfloat16)
        out_second[at] = jnp.where(odd, up, down).astype(jnp.bfloat16)

    return put


def fill_depth(put, readers, chosen, size_z):
    fields, conds, adjoints = readers
    at = 0
    for i in chosen[0]:
        rows = [r(i) for r in fields]
        put(at, [r[:ZP] for r in rows], [r[size_z - ZP :] for r in rows])
        at += 1
    for i, j in zip(chosen[1][::2], chosen[1][1::2]):
        rows = [conds(i), conds(j)]
        put(at, [r[:ZP] for r in rows], [r[size_z - ZP :] for r in rows])
        at += 1
    for i, j in zip(chosen[2][::2], chosen[2][1::2]):
        rows = [r(n) for n in (i, j) for r in adjoints]
        put(at, [r[:HA] for r in rows], [r[size_z - HA :] for r in rows])
        at += 1
    return at


def empty_depth(x0, cond, a0, chosen, low, high, top):
    at = 0
    for i in chosen[0]:
        a, b = low(at), high(at)
        for f in range(2):
            x0[f, i, top + ZP : top + 2 * ZP] = a[f * ZP : (f + 1) * ZP]
            x0[f, i, top : top + ZP] = b[f * ZP : (f + 1) * ZP]
        at += 1
    for pair in zip(chosen[1][::2], chosen[1][1::2]):
        a, b = low(at), high(at)
        for n, i in enumerate(pair):
            cond[i, top + ZP : top + 2 * ZP] = a[n * ZP : (n + 1) * ZP]
            cond[i, top : top + ZP] = b[n * ZP : (n + 1) * ZP]
        at += 1
    for pair in zip(chosen[2][::2], chosen[2][1::2]):
        a, b = low(at), high(at)
        for n, i in enumerate(pair):
            for f in range(2):
                part = slice((2 * n + f) * HA, (2 * n + f + 1) * HA)
                a0[f, i, top : top + 2 * HA] = jnp.concatenate([b[part], a[part]], axis=0)
        at += 1
    return at


def own_rows(size_x):
    return [list(range(h, h + size_x)) for h in (HX, HC, HA)]


def corner_rows(size_x):
    return [list(range(1, h)) + list(range(h + size_x, size_x + 2 * h - 1)) for h in (HX, HC, HA)]


def tiles_of(chosen):
    return len(chosen[0]) + len(chosen[1]) // 2 + len(chosen[2]) // 2


def sides_of(axis, first, second):
    odd = is_odd(axis)

    def low(at):
        return jnp.where(odd, first[at].astype(jnp.float32), second[at].astype(jnp.float32))

    def high(at):
        return jnp.where(odd, second[at].astype(jnp.float32), first[at].astype(jnp.float32))

    return low, high


def pack(*ins):
    x0, cond, a0 = ins[:3]
    shape = (LP + 1,) + cond.shape[1:]
    return pl.pallas_call(
        pack_kernel,
        out_shape=(jax.ShapeDtypeStruct(shape, jnp.bfloat16),) * 2
        + (jax.ShapeDtypeStruct((tiles_of(own_rows(cond.shape[0])),) + shape[1:], jnp.bfloat16),) * 2
        + tuple(pltpu.VMEM(a.shape, a.dtype) for a in ins[:3]),
        in_specs=[HBM] * 7,
        out_specs=(VMEM,) * 7,
        scratch_shapes=[pltpu.VMEM(a.shape, a.dtype) for a in ins[3:]]
        + [pltpu.VMEM(cond.shape[1:], jnp.float32), pltpu.SemaphoreType.DMA((7,))],
        compiler_params=PARAMS,
        name="pack",
    )(*[in_hbm(a) for a in ins])


def joined_rows(x0, cond, a0, first, second):
    size_x = cond.shape[0]
    low, high = sides_of("brick", first, second)

    def reader(own, base, halo):
        def row(i):
            if i < halo:
                return low(base + i)
            if i >= halo + size_x:
                return high(base + i - halo - size_x)
            return own(i - halo)
        return row

    fields = [reader(lambda i, f=f: x0[f, i], LX + f * HX, HX) for f in range(2)]
    adjoints = [reader(lambda i, f=f: a0[f, i], LA + f * HA, HA) for f in range(2)]
    return fields, reader(lambda i: cond[i], LC, HC), adjoints, low, high


def mid_kernel(x0, cond, a0, sent, first, second, *refs):
    out_first, out_second = refs[-2:]
    size_x, size_z, size_y = cond.shape
    fields, conds, adjoints, low, high = joined_rows(x0, cond, a0, first, second)
    n = size_y // 4
    points = low(LP) + pltpu.roll(sent[LP].astype(jnp.float32), n, 1) + pltpu.roll(high(LP), 2 * n, 1)
    at = fill_depth(
        depth_writer(out_first, out_second, size_z), [fields, conds, adjoints], corner_rows(size_x), size_z
    )
    out_first[at] = points.astype(jnp.bfloat16)
    out_second[at] = points.astype(jnp.bfloat16)


def mid(x0, cond, a0, sent, first, second, *ready):
    size_x, size_z, size_y = cond.shape
    shape = (tiles_of(corner_rows(size_x)) + 1, size_z, size_y)
    return pl.pallas_call(
        mid_kernel,
        out_shape=(jax.ShapeDtypeStruct(shape, jnp.bfloat16),) * 2,
        in_specs=[VMEM] * (6 + len(ready)),
        out_specs=(VMEM, VMEM),
        compiler_params=PARAMS,
        name="mid",
    )(x0, cond, a0, sent, first, second, *[held(a) for a in ready])


def place(t, q, weights, halo, dst, lists, size_x, size_z, size_y):
    n_list = lists.shape[-1]
    each = n_list // 4
    lane = lax.broadcasted_iota(jnp.int32, (1, n_list), 1)
    dx = jnp.where(lane < each, -1, jnp.where(lane < 2 * each, 0, 1))
    nx = size_x + 2 * halo
    hi = lists[q : q + 1] - 1.0
    lo = lists[q + 1 : q + 2].astype(jnp.int32)
    x = jnp.floor((hi + 0.5) * (1.0 / size_z))
    z = (hi - x * size_z).astype(jnp.int32)
    row_x = x.astype(jnp.int32) + halo + size_x * dx
    ok = (hi >= 0.0) & (row_x >= 0) & (row_x < nx)
    if t == 1:
        depth, z0 = size_z, 0
        target = row_x * size_z + z
    elif t == 0:
        depth, z0 = ZP, size_z + ZP
        target = row_x * ZP + z - (size_z - ZP)
        ok = ok & (z >= size_z - ZP)
    else:
        depth, z0 = ZP, size_z
        target = row_x * ZP + z
        ok = ok & (z < ZP)
    target = jnp.where(ok, target, -1)
    hit = lax.broadcasted_iota(jnp.int32, (nx * depth, n_list), 0) == target
    right = (lax.broadcasted_iota(jnp.int32, (size_y, n_list), 0) == lo).astype(jnp.float32).astype(jnp.bfloat16)
    terms = [(n, p) for n, parts in weights for p in parts]
    left = jnp.concatenate([jnp.where(hit, 1.0 if p is None else lists[p : p + 1], 0.0) for _, p in terms], axis=0)
    placed = lax.dot_general(left.astype(jnp.bfloat16), right, NT, preferred_element_type=jnp.float32)
    totals = {}
    for i, (n, _) in enumerate(terms):
        part = placed[i * nx * depth : (i + 1) * nx * depth]
        totals[n] = totals[n] + part if n in totals else part
    for n, total in totals.items():
        dst[n, :, z0 : z0 + depth, :] = total.reshape(nx, depth, size_y)


SRC_WEIGHTS = ((0, (2, 4, 6)), (1, (3, 5, 7)))
REC_WEIGHTS = ((0, (10, 12, 14)), (1, (11, 13, 15)), (2, (None,)))


def prep_kernel(x0, cond, a0, sent2, first, second, side_first, side_second, x0_w, cond_w, a0_w, src, rec):
    size_x, size_z, size_y = cond.shape
    fields, conds, adjoints, _, _ = joined_rows(x0, cond, a0, first, second)
    own = slice(0, size_z)
    for f in range(2):
        for i in range(size_x + 2 * HX):
            x0_w[f, i, own] = fields[f](i)
        for i in range(size_x + 2 * HA):
            a0_w[f, i, own] = adjoints[f](i)
    for i in range(size_x + 2 * HC):
        cond_w[i, own] = conds(i)
    empty_depth(x0_w, cond_w, a0_w, own_rows(size_x), *sides_of("depth", side_first, side_second), size_z)
    lists = sent2[sent2.shape[0] - 1].astype(jnp.float32)
    place(1, 0, SRC_WEIGHTS, HC, src, lists, size_x, size_z, size_y)
    place(1, 8, REC_WEIGHTS, HU, rec, lists, size_x, size_z, size_y)


def wide_shapes(size_x, size_z, size_y):
    slab = (size_z + 2 * ZP, size_y)
    return (
        (2, size_x + 2 * HX) + slab,
        (size_x + 2 * HC,) + slab,
        (2, size_x + 2 * HA) + (size_z + 2 * HA, size_y),
        (2, size_x + 2 * HC) + slab,
        (3, size_x + 2 * HU) + slab,
    )


def prep(x0, cond, a0, sent2, first, second, side_first, side_second):
    shapes = wide_shapes(*cond.shape)
    return pl.pallas_call(
        prep_kernel,
        out_shape=tuple(pltpu.VMEM(s, jnp.float32) for s in shapes),
        in_specs=[VMEM] * 8,
        out_specs=(VMEM,) * 5,
        compiler_params=PARAMS,
        name="prep",
    )(x0, cond, a0, sent2, first, second, side_first, side_second)


def beside_z_y(c):
    rows, width = c.shape
    half = width // 2
    total = pltpu.roll(c, 1, 0) + pltpu.roll(c, rows - 1, 0)
    lane = lax.broadcasted_iota(jnp.int32, (rows, half), 1)
    first = lane == 0
    last = lane == half - 1
    a, b = c[:, :half], c[:, half:]
    ra, rb = pltpu.roll(a, 1, 1), pltpu.roll(b, 1, 1)
    la, lb = pltpu.roll(a, half - 1, 1), pltpu.roll(b, half - 1, 1)
    ya = jnp.where(first, 0.0, ra) + jnp.where(last, lb, la)
    yb = jnp.where(first, ra, rb) + jnp.where(last, 0.0, lb)
    return total + jnp.concatenate([ya, yb], axis=1)


def chain_kernel(size_x, size_z, x0_in, cond_in, a0_in, src_in, rec_in, first, second,
                 x0, cond, a0, src, rec, v0, v1, v2, u, w1, w2, sums_out, w3, acc, cond_n):
    rows_z = x0.shape[-2]
    size_y = x0.shape[-1]
    own = slice(0, size_z)
    top = size_z

    low, high = sides_of("depth", first, second)
    at = empty_depth(x0, cond, a0, corner_rows(size_x), low, high, top)
    for ref in (x0, cond, a0):
        blank = jnp.zeros((ref.shape[-2] - top, size_y), jnp.float32)
        for i in (0, ref.shape[-3] - 1):
            if len(ref.shape) == 3:
                ref[i, top:] = blank
            else:
                for f in range(2):
                    ref[f, i, top:] = blank
    for t, lists in ((0, low(at)), (2, high(at))):
        place(t, 0, SRC_WEIGHTS, HC, src, lists, size_x, size_z, size_y)
        place(t, 8, REC_WEIGHTS, HU, rec, lists, size_x, size_z, size_y)

    def edge(axis):
        at = lax.axis_index(axis)
        return (at > 0).astype(jnp.float32), (at < lax.axis_size(axis) - 1).astype(jnp.float32)

    low_x, high_x = edge("brick")
    low_z, high_z = edge("depth")
    upper = lax.broadcasted_iota(jnp.int32, (2 * HA, size_y), 0) < HA
    both_z = jnp.where(upper, high_z, low_z)

    def narrow(value):
        return jnp.concatenate([value[own], jnp.where(upper, value[top : top + ZP], value[top + ZP :])], axis=0)

    def inside(value, i, halo):
        in_x = low_x if i < halo else high_x if i >= halo + size_x else None
        if value.shape[0] == rows_z:
            parts = [value[own], value[top : top + ZP] * high_z, value[top + ZP :] * low_z]
        else:
            parts = [value[own], value[top:] * both_z]
        if in_x is not None:
            parts = [p * in_x for p in parts]
        return jnp.concatenate(parts, axis=0)

    def apply(ref, idx, i, damp):
        c = ref[idx + (i,)]
        return damp * c - (ref[idx + (i - 1,)] + ref[idx + (i + 1,)] + beside_z_y(c))

    def loop(n, body):
        for i in range(n):
            body(i)

    def thin(i):
        cond_n[i] = narrow(cond[i])

    loop(size_x + 2 * HC, thin)

    def first(i):
        for f, s in enumerate(LAPLACE_SHIFTS):
            v0[f, i] = inside(src[f, i] - apply(x0, (f,), i + 1, s * cond[i] + THETA), i, HC)

    loop(size_x + 2 * HC, first)

    def second(i):
        for f, s in enumerate(LAPLACE_SHIFTS):
            v1[f, i] = inside(narrow(apply(v0, (f,), i + 1, s * cond[i + 1])), i, 4)

    loop(size_x + 8, second)

    def third(i):
        for f, s in enumerate(LAPLACE_SHIFTS):
            v2[f, i] = inside(apply(v1, (f,), i + 1, s * cond_n[i + 2]), i, 3)

    loop(size_x + 6, third)

    def start(i):
        many = narrow(rec[2, i])
        for f, s in enumerate(LAPLACE_SHIFTS):
            u[0, f, i] = inside(
                many * narrow(x0[f, i + 3]) - narrow(rec[f, i]) - apply(a0, (f,), i + 1, s * cond_n[i + 2] + THETA),
                i,
                HU,
            )
            u[1, f, i] = many * narrow(v0[f, i + 2])
            u[2, f, i] = many * v1[f, i + 1]
            u[3, f, i] = many * v2[f, i]

    loop(size_x + 2 * HU, start)

    def level(src_ref, dst_ref, halo):
        def body(i):
            for f, s in enumerate(LAPLACE_SHIFTS):
                damp = s * cond_n[i + HC - halo]
                for k in range(4):
                    dst_ref[k, f, i] = inside(apply(src_ref, (k, f), i + 1, damp), i, halo)
        loop(size_x + 2 * halo, body)

    level(u, w1, 2)
    level(w1, w2, 1)

    def last(i):
        for f, s in enumerate(LAPLACE_SHIFTS):
            damp = s * cond_n[i + HC]
            for k in range(4):
                w3[k, f, i] = apply(w2, (k, f), i + 1, damp)[own]

    loop(size_x, last)

    def tiles(a):
        total = None
        for z in range(0, a.shape[0], 8):
            for y in range(0, a.shape[1], 128):
                t = a[z : z + 8, y : y + 128]
                total = t if total is None else total + t
        return total

    zero = jnp.zeros((8, 128), jnp.float32)

    def over_rows(body, carry, unroll=8):
        def step(i, carry):
            for j in range(unroll):
                carry = body(i * unroll + j, carry)
            return carry

        return lax.fori_loop(0, size_x // unroll, step, carry)

    for f, s in enumerate(LAPLACE_SHIFTS):
        def forward_sums(i, carry, f=f, s=s):
            p0 = v0[f, i + 5, own]
            p1 = v1[f, i + 4, own]
            p2 = v2[f, i + 3, own]
            p3 = apply(v2, (f,), i + 3, s * cond_n[i + 5])[own]
            made = (p0 * p0, p0 * p1, p1 * p1, p1 * p2, p2 * p2, p2 * p3)
            return tuple(c + tiles(a) for c, a in zip(carry, made))
        done = over_rows(forward_sums, (zero,) * 6)
        for j in range(6):
            acc[j * SLOTS + 2 * len(PAIRS) + f] = done[j]

    levels = ((u, 3, own), (w1, 2, own), (w2, 1, own), (w3, 0, slice(0, size_z)))
    for j in range(3):
        ra, oa, za = levels[j]
        rb, ob, zb = levels[j + 1]
        for f in range(2):
            def pair_sums(i, carry, f=f):
                a = [ra[k, f, i + oa, za] for k in range(4)]
                b = [rb[k, f, i + ob, zb] for k in range(4)]
                made = [a[k] * a[l] for k, l in PAIRS] + [a[k] * b[l] for k, l in PAIRS]
                return tuple(c + tiles(m) for c, m in zip(carry, made))
            done = over_rows(pair_sums, (zero,) * (2 * len(PAIRS)), 2)
            for n in range(len(PAIRS)):
                acc[2 * j * SLOTS + 2 * n + f] = done[n]
                acc[(2 * j + 1) * SLOTS + 2 * n + f] = done[len(PAIRS) + n]

    for j in range(acc.shape[0] // SLOTS):
        for n in range(0 if j >= 6 else 2 * len(PAIRS) + 2, SLOTS):
            acc[j * SLOTS + n] = zero
    by_lane = jnp.sum(acc[...], axis=1)
    ones = jnp.ones((8, 128), jnp.float32)
    out = lax.dot_general(ones, by_lane, NT, precision=lax.Precision.HIGHEST, preferred_element_type=jnp.float32)
    out = jnp.concatenate([out[0:1, :128], out[0:1, 128:]], axis=0)
    sums_out[...] = jnp.broadcast_to(out[None], sums_out.shape)


def chain(wide, first, second, size_x, size_z, n_dev):
    size_y = wide[0].shape[-1]
    f32 = jnp.float32
    slab = (size_z + 2 * ZP, size_y)
    thin = (size_z + 2 * HA, size_y)
    outs = tuple(pltpu.VMEM(a.shape, f32) for a in wide) + (
        pltpu.VMEM((2, size_x + 2 * HC) + slab, f32),
        pltpu.VMEM((2, size_x + 8) + thin, f32),
        pltpu.VMEM((2, size_x + 6) + thin, f32),
        pltpu.VMEM((4, 2, size_x + 6) + thin, f32),
        pltpu.VMEM((4, 2, size_x + 4) + thin, f32),
        pltpu.VMEM((4, 2, size_x + 2) + thin, f32),
        jax.ShapeDtypeStruct((n_dev, 2, 128), f32),
    )
    scratch = [
        pltpu.VMEM((4, 2, size_x, size_z, size_y), f32),
        pltpu.VMEM((256, 8, 128), f32),
        pltpu.VMEM((size_x + 2 * HC,) + thin, f32),
    ]
    return pl.pallas_call(
        functools.partial(chain_kernel, size_x, size_z),
        out_shape=outs,
        in_specs=[VMEM] * 7,
        out_specs=(VMEM,) * len(outs),
        scratch_shapes=scratch,
        input_output_aliases={i: i for i in range(5)},
        compiler_params=PARAMS,
        name="chain",
    )(*[held(a) for a in wide], first, second)[5:]


def coefficients(mu):
    a = [[mu[i + j + 1] + THETA * mu[i + j] for j in range(3)] for i in range(3)]

    def inverse(pivot, size):
        good = pivot > 1e-6 * size
        return jnp.where(good, 1.0 / jnp.where(good, pivot, 1.0), 0.0)

    i0 = inverse(a[0][0], 0.0)
    l10 = a[0][1] * i0
    l20 = a[0][2] * i0
    i1 = inverse(a[1][1] - l10 * a[0][1], a[1][1])
    e21 = a[1][2] - l10 * a[0][2]
    l21 = e21 * i1
    i2 = inverse(a[2][2] - l20 * a[0][2] - l21 * e21, a[2][2])
    y0 = mu[0]
    y1 = mu[1] - l10 * y0
    y2 = mu[2] - l20 * y0 - l21 * y1
    c2 = y2 * i2
    c1 = y1 * i1 - l21 * c2
    c0 = y0 * i0 - l10 * c1 - l20 * c2
    return c0, c1, c2


def combine_kernel(every, x0, a0, v0, v1, v2, u, w1, w2, forward, gradient):
    total = jnp.sum(every[...], axis=0)
    per = 128 // SLOTS
    rows = jnp.concatenate(
        [total[j // per : j // per + 1, j % per * SLOTS : (j % per + 1) * SLOTS] for j in range(6)], axis=0
    )
    rows = jnp.concatenate([rows, jnp.zeros((2, SLOTS), jnp.float32)], axis=0)
    rows = jnp.concatenate([rows, jnp.zeros((8, 128 - SLOTS), jnp.float32)], axis=1)
    n_pair = 2 * len(PAIRS)
    at = lax.broadcasted_iota(jnp.int32, (128, 128), 0)
    to = lax.broadcasted_iota(jnp.int32, (128, 128), 1)
    same = (at & 1) == (to & 1)

    def gather_lanes(values, chosen):
        table = jnp.where(same & chosen, 1.0, 0.0)
        return jnp.dot(values, table, precision=lax.Precision.HIGHEST, preferred_element_type=jnp.float32)

    mu = gather_lanes(rows, (at >= n_pair) & (at < n_pair + 2))
    c = coefficients([mu[j : j + 1] for j in range(6)])
    basis = (jnp.ones_like(c[0]),) + c
    pair = lax.broadcasted_iota(jnp.int32, (1, 128), 1) // 2
    weight = jnp.zeros((1, 128), jnp.float32)
    for n, (k, l) in enumerate(PAIRS):
        product = basis[k] * basis[l] * (1.0 if k == l else 2.0)
        weight = jnp.where(pair == n, product, weight)
    nu = gather_lanes(rows * weight, at < n_pair)
    d = coefficients([nu[j : j + 1] for j in range(6)])
    size_x, size_z = x0.shape[1:3]
    own = slice(0, size_z)
    v = ((v0, 5), (v1, 4), (v2, 3))
    w = ((u, 3), (w1, 2), (w2, 1))
    scale = []
    for f in range(2):
        up = [c[k][:, f : f + 1] for k in range(3)]
        down = [[(d[j] * basis[k])[:, f : f + 1] for k in range(4)] for j in range(3)]
        scale.append((up, down))
    for i in range(size_x):
        total = None
        for f, s in enumerate(LAPLACE_SHIFTS):
            up, down = scale[f]
            field = x0[f, i]
            for k in range(3):
                field = field + up[k] * v[k][0][f, i + v[k][1], own]
            other = a0[f, i]
            for j in range(3):
                for k in range(4):
                    other = other + down[j][k] * w[j][0][k, f, i + w[j][1], own]
            forward[f, i] = field
            part = s * field * other
            total = part if total is None else total + part
        gradient[i] = (-total).astype(gradient.dtype)


def combine(every, x0, a0, *made):
    return pl.pallas_call(
        combine_kernel,
        out_shape=(
            jax.ShapeDtypeStruct(x0.shape, jnp.float32),
            jax.ShapeDtypeStruct(x0.shape[1:], jnp.bfloat16),
        ),
        in_specs=[VMEM] * (3 + len(made)),
        out_specs=(VMEM, VMEM),
        compiler_params=PARAMS,
        name="combine",
    )(every, x0, a0, *[held(a) for a in made])


def turn_kernel(blocks, out, buf, sems):
    n = buf.shape[0]
    copies = [pltpu.make_async_copy(blocks.at[k], buf.at[k], sems.at[k]) for k in range(n)]
    for copy in copies:
        copy.start()
    for k, copy in enumerate(copies):
        copy.wait()
        out[k] = buf[k].T


def turn(blocks):
    return pl.pallas_call(
        turn_kernel,
        out_shape=pltpu.VMEM(blocks.shape, blocks.dtype),
        in_specs=[HBM],
        out_specs=VMEM,
        scratch_shapes=[
            pltpu.VMEM(blocks.shape, blocks.dtype),
            pltpu.SemaphoreType.DMA((blocks.shape[0],)),
        ],
        compiler_params=PARAMS,
        name="turn",
    )(in_hbm(blocks))


def covariance_kernel(cols, rows, every, own, blocks, out):
    n_dev, size_x, size_z, width = every.shape
    n_rows = size_x * size_z
    n_blocks, size, _ = blocks.shape
    per = size // width
    table = every[...].reshape(n_dev * n_rows, width)
    at = lax.broadcasted_iota(jnp.int32, (n_dev * n_rows, n_blocks), 0)
    hits = jnp.concatenate([jnp.where(at == cols[...] * per + i, 1.0, 0.0) for i in range(per)], axis=1)
    picked = lax.dot_general(
        hits.astype(jnp.bfloat16), table, (((0,), (0,)), ((), ())), preferred_element_type=jnp.float32
    )
    picked = jnp.concatenate([picked[i * n_blocks : (i + 1) * n_blocks] for i in range(per)], axis=1)
    picked = picked.astype(jnp.bfloat16)
    which = lax.broadcasted_iota(jnp.int32, (n_blocks, size), 0)
    terms = jnp.zeros((n_blocks, size), jnp.float32)
    for k in range(n_blocks):
        terms = jnp.where(which == k, jnp.dot(picked, blocks[k], preferred_element_type=jnp.float32), terms)
    one = terms.astype(jnp.bfloat16)
    rest = terms - one.astype(jnp.float32)
    two = rest.astype(jnp.bfloat16)
    three = (rest - two.astype(jnp.float32)).astype(jnp.bfloat16)
    right = jnp.concatenate(
        [p[:, i * width : (i + 1) * width] for p in (one, two, three) for i in range(per)], axis=0
    )
    at = lax.broadcasted_iota(jnp.int32, (n_rows, n_blocks), 0)
    hits = [jnp.where(at == rows[...] * per + i, 1.0, 0.0) for i in range(per)]
    left = jnp.concatenate(hits * 3, axis=1).astype(jnp.bfloat16)
    out[...] = own[...].reshape(n_rows, width).astype(jnp.float32) + jnp.dot(
        left, right, preferred_element_type=jnp.float32
    )


def covariance(cols, rows, every, own, blocks):
    n_dev, size_x, size_z, width = every.shape
    return pl.pallas_call(
        covariance_kernel,
        out_shape=jax.ShapeDtypeStruct((size_x * size_z, width), jnp.float32),
        in_specs=[VMEM] * 5,
        out_specs=VMEM,
        compiler_params=PARAMS,
        name="covariance",
    )(cols, rows, every, own, held(blocks))


def local(
    conductivity,
    initial_field,
    adjoint_initial,
    src_cell,
    src_amp,
    rec_cell,
    observed,
    cov_blocks,
    cov_rows,
    cov_cols,
):
    size_x, size_z, size_y = conductivity.shape
    n_dev = lax.axis_size("brick") * lax.axis_size("depth")
    *sent, side_low, side_high, x0, cond, a0 = pack(
        initial_field, conductivity, adjoint_initial, src_cell[0], src_amp[0, 0], rec_cell[0], observed[0, 0]
    )
    x0, cond, a0 = held(x0), held(cond), held(a0)
    first, second = swap(*sent, "brick")
    sides = swap(side_low, side_high, "depth")
    blocks = turn(cov_blocks[0, 0])
    sent2 = mid(x0, cond, a0, sent[0], first, second, blocks, *sides)
    wide = prep(x0, cond, a0, sent2[0], first, second, *sides)
    first2, second2 = swap(*sent2, "depth")
    *made, sums = chain(wide, first2, second2, size_x, size_z, n_dev)
    every = lax.all_to_all(sums, BOTH, 0, 0, tiled=True)
    forward, gradient = combine(every, x0, a0, *made)
    every_block = lax.all_gather(gradient, "depth", axis=0, tiled=False)
    out = covariance(cov_cols[0], cov_rows[0], every_block, gradient, blocks)
    return (forward, out.reshape(size_x, size_z, size_y))


def solution(mesh):
    return jax.shard_map(
        local,
        mesh=mesh,
        in_specs=(
            P("brick", "depth", None),
            P(None, "brick", "depth", None),
            P(None, "brick", "depth", None),
            P("brick", "depth", None),
            P("brick", "depth", None, None),
            P("brick", "depth", None),
            P("brick", "depth", None, None),
            P("brick", "depth", None, None, None),
            P("brick", "depth", None),
            P("brick", "depth", None),
        ),
        out_specs=(P(None, "brick", "depth", None), P("brick", "depth", None)),
        check_vma=False,
    )
```

```python
import functools

import jax
import jax.numpy as jnp
from jax import lax
from jax.experimental import pallas as pl
from jax.experimental.pallas import tpu as pltpu
from jax.sharding import PartitionSpec as P

LAPLACE_SHIFTS = (0.5, 2.0)
BOTH = ("brick", "depth")
HX = 6
HC = 5
HA = 4
HU = 3
ZP = 8
THETA = 6.0
PAIRS = tuple((k, l) for k in range(4) for l in range(k, 4))
SLOTS = 32
VMEM = pl.BlockSpec(memory_space=pltpu.VMEM)
SMEM = pl.BlockSpec(memory_space=pltpu.SMEM)
HBM = pl.BlockSpec(memory_space=pltpu.HBM)
NT = (((1,), (1,)), ((), ()))
PARAMS = pltpu.CompilerParams(vmem_limit_bytes=28 * 1024 * 1024)


def held(a):
    return pltpu.with_memory_space_constraint(a, pltpu.VMEM)


def in_hbm(a):
    return pltpu.with_memory_space_constraint(a, pltpu.HBM)


def is_odd(axis):
    return lax.rem(lax.axis_index(axis), 2) == 1


def pairings(axis):
    size = lax.axis_size(axis)
    first = [(i, i ^ 1) for i in range(size) if (i ^ 1) < size]
    second = [(i, j) for i in range(size) for j in [((i + 1) ^ 1) - 1] if 0 <= j < size]
    return first, second


def swap(first, second, axis):
    one, two = pairings(axis)
    return lax.ppermute(first, axis, one), lax.ppermute(second, axis, two)


LX, LC, LA = 0, 2 * HX, 2 * HX + HC
LP = LA + 2 * HA


def pack_kernel(*refs):
    ins, (first, second), sides, kept, pieces = refs[:7], refs[7:9], refs[9:11], refs[11:14], refs[14:18]
    table, sems = refs[18:]
    copies = [
        pltpu.make_async_copy(a, b, sems.at[i]) for i, (a, b) in enumerate(zip(ins, kept + pieces))
    ]
    for copy in copies:
        copy.start()
    for copy in copies:
        copy.wait()
    x0, cond, a0 = kept
    src_cell, src_amp, rec_cell, observed = pieces
    size_x, size_z, size_y = cond.shape
    odd = is_odd("brick")

    def split(v):
        one = v.astype(jnp.bfloat16).astype(jnp.float32)
        two = (v - one).astype(jnp.bfloat16).astype(jnp.float32)
        return one, two, v - one - two

    table[...] = jnp.zeros_like(table)
    for base, cells, amounts in ((0, src_cell, src_amp), (8, rec_cell, observed)):
        n = cells.shape[-1]
        at = cells[...].astype(jnp.float32)
        hi = jnp.floor((at + 0.5) * (1.0 / size_y))
        table[base : base + 1, :n] = hi + 1.0
        table[base + 1 : base + 2, :n] = at - hi * size_y
        for s, part in enumerate(split(amounts[...])):
            table[base + 2 + 2 * s : base + 4 + 2 * s, :n] = part
    points = table[...].astype(jnp.bfloat16)
    for out, low in ((first, odd), (second, jnp.logical_not(odd))):
        for f in range(2):
            for i in range(HX):
                out[LX + f * HX + i] = x0[f, jnp.where(low, i, size_x - HX + i)].astype(jnp.bfloat16)
            for i in range(HA):
                out[LA + f * HA + i] = a0[f, jnp.where(low, i, size_x - HA + i)].astype(jnp.bfloat16)
        for i in range(HC):
            out[LC + i] = cond[jnp.where(low, i, size_x - HC + i)].astype(jnp.bfloat16)
        out[LP] = points
    put = depth_writer(*sides, size_z)
    fill_depth(
        put,
        [[(lambda i, f=f: x0[f, i]) for f in range(2)], lambda i: cond[i], [(lambda i, f=f: a0[f, i]) for f in range(2)]],
        [list(range(size_x))] * 3,
        size_z,
    )


def depth_writer(out_first, out_second, size_z):
    odd = is_odd("depth")

    def put(at, down, up):
        down = jnp.concatenate(down, axis=0)
        up = jnp.concatenate(up, axis=0)
        out_first[at] = jnp.where(odd, down, up).astype(jnp.bfloat16)
        out_second[at] = jnp.where(odd, up, down).astype(jnp.bfloat16)

    return put


def fill_depth(put, readers, chosen, size_z):
    fields, conds, adjoints = readers
    at = 0
    for i in chosen[0]:
        rows = [r(i) for r in fields]
        put(at, [r[:ZP] for r in rows], [r[size_z - ZP :] for r in rows])
        at += 1
    for i, j in zip(chosen[1][::2], chosen[1][1::2]):
        rows = [conds(i), conds(j)]
        put(at, [r[:ZP] for r in rows], [r[size_z - ZP :] for r in rows])
        at += 1
    for i, j in zip(chosen[2][::2], chosen[2][1::2]):
        rows = [r(n) for n in (i, j) for r in adjoints]
        put(at, [r[:HA] for r in rows], [r[size_z - HA :] for r in rows])
        at += 1
    return at


def empty_depth(x0, cond, a0, chosen, low, high, top):
    at = 0
    for i in chosen[0]:
        a, b = low(at), high(at)
        for f in range(2):
            x0[f, i, top + ZP : top + 2 * ZP] = a[f * ZP : (f + 1) * ZP]
            x0[f, i, top : top + ZP] = b[f * ZP : (f + 1) * ZP]
        at += 1
    for pair in zip(chosen[1][::2], chosen[1][1::2]):
        a, b = low(at), high(at)
        for n, i in enumerate(pair):
            cond[i, top + ZP : top + 2 * ZP] = a[n * ZP : (n + 1) * ZP]
            cond[i, top : top + ZP] = b[n * ZP : (n + 1) * ZP]
        at += 1
    for pair in zip(chosen[2][::2], chosen[2][1::2]):
        a, b = low(at), high(at)
        for n, i in enumerate(pair):
            for f in range(2):
                part = slice((2 * n + f) * HA, (2 * n + f + 1) * HA)
                a0[f, i, top : top + 2 * HA] = jnp.concatenate([b[part], a[part]], axis=0)
        at += 1
    return at


def own_rows(size_x):
    return [list(range(h, h + size_x)) for h in (HX, HC, HA)]


def corner_rows(size_x):
    return [list(range(1, h)) + list(range(h + size_x, size_x + 2 * h - 1)) for h in (HX, HC, HA)]


def tiles_of(chosen):
    return len(chosen[0]) + len(chosen[1]) // 2 + len(chosen[2]) // 2


def sides_of(axis, first, second):
    odd = is_odd(axis)

    def low(at):
        return jnp.where(odd, first[at].astype(jnp.float32), second[at].astype(jnp.float32))

    def high(at):
        return jnp.where(odd, second[at].astype(jnp.float32), first[at].astype(jnp.float32))

    return low, high


def pack(*ins):
    x0, cond, a0 = ins[:3]
    shape = (LP + 1,) + cond.shape[1:]
    return pl.pallas_call(
        pack_kernel,
        out_shape=(jax.ShapeDtypeStruct(shape, jnp.bfloat16),) * 2
        + (jax.ShapeDtypeStruct((tiles_of(own_rows(cond.shape[0])),) + shape[1:], jnp.bfloat16),) * 2
        + tuple(pltpu.VMEM(a.shape, a.dtype) for a in ins[:3]),
        in_specs=[HBM] * 7,
        out_specs=(VMEM,) * 7,
        scratch_shapes=[pltpu.VMEM(a.shape, a.dtype) for a in ins[3:]]
        + [pltpu.VMEM(cond.shape[1:], jnp.float32), pltpu.SemaphoreType.DMA((7,))],
        compiler_params=PARAMS,
        name="pack",
    )(*[in_hbm(a) for a in ins])


def joined_rows(x0, cond, a0, first, second):
    size_x = cond.shape[0]
    low, high = sides_of("brick", first, second)

    def reader(own, base, halo):
        def row(i):
            if i < halo:
                return low(base + i)
            if i >= halo + size_x:
                return high(base + i - halo - size_x)
            return own(i - halo)
        return row

    fields = [reader(lambda i, f=f: x0[f, i], LX + f * HX, HX) for f in range(2)]
    adjoints = [reader(lambda i, f=f: a0[f, i], LA + f * HA, HA) for f in range(2)]
    return fields, reader(lambda i: cond[i], LC, HC), adjoints, low, high


def mid_kernel(x0, cond, a0, sent, first, second, *refs):
    out_first, out_second = refs[-2:]
    size_x, size_z, size_y = cond.shape
    fields, conds, adjoints, low, high = joined_rows(x0, cond, a0, first, second)
    n = size_y // 4
    points = low(LP) + pltpu.roll(sent[LP].astype(jnp.float32), n, 1) + pltpu.roll(high(LP), 2 * n, 1)
    at = fill_depth(
        depth_writer(out_first, out_second, size_z), [fields, conds, adjoints], corner_rows(size_x), size_z
    )
    out_first[at] = points.astype(jnp.bfloat16)
    out_second[at] = points.astype(jnp.bfloat16)


def mid(x0, cond, a0, sent, first, second, *ready):
    size_x, size_z, size_y = cond.shape
    shape = (tiles_of(corner_rows(size_x)) + 1, size_z, size_y)
    return pl.pallas_call(
        mid_kernel,
        out_shape=(jax.ShapeDtypeStruct(shape, jnp.bfloat16),) * 2,
        in_specs=[VMEM] * (6 + len(ready)),
        out_specs=(VMEM, VMEM),
        compiler_params=PARAMS,
        name="mid",
    )(x0, cond, a0, sent, first, second, *[held(a) for a in ready])


def place(t, q, weights, halo, dst, lists, size_x, size_z, size_y):
    n_list = lists.shape[-1]
    each = n_list // 4
    lane = lax.broadcasted_iota(jnp.int32, (1, n_list), 1)
    dx = jnp.where(lane < each, -1, jnp.where(lane < 2 * each, 0, 1))
    nx = size_x + 2 * halo
    hi = lists[q : q + 1] - 1.0
    lo = lists[q + 1 : q + 2].astype(jnp.int32)
    x = jnp.floor((hi + 0.5) * (1.0 / size_z))
    z = (hi - x * size_z).astype(jnp.int32)
    row_x = x.astype(jnp.int32) + halo + size_x * dx
    ok = (hi >= 0.0) & (row_x >= 0) & (row_x < nx)
    if t == 1:
        depth, z0 = size_z, 0
        target = row_x * size_z + z
    elif t == 0:
        depth, z0 = ZP, size_z + ZP
        target = row_x * ZP + z - (size_z - ZP)
        ok = ok & (z >= size_z - ZP)
    else:
        depth, z0 = ZP, size_z
        target = row_x * ZP + z
        ok = ok & (z < ZP)
    target = jnp.where(ok, target, -1)
    hit = lax.broadcasted_iota(jnp.int32, (nx * depth, n_list), 0) == target
    right = (lax.broadcasted_iota(jnp.int32, (size_y, n_list), 0) == lo).astype(jnp.float32).astype(jnp.bfloat16)
    terms = [(n, p) for n, parts in weights for p in parts]
    left = jnp.concatenate([jnp.where(hit, 1.0 if p is None else lists[p : p + 1], 0.0) for _, p in terms], axis=0)
    placed = lax.dot_general(left.astype(jnp.bfloat16), right, NT, preferred_element_type=jnp.float32)
    totals = {}
    for i, (n, _) in enumerate(terms):
        part = placed[i * nx * depth : (i + 1) * nx * depth]
        totals[n] = totals[n] + part if n in totals else part
    for n, total in totals.items():
        dst[n, :, z0 : z0 + depth, :] = total.reshape(nx, depth, size_y)


SRC_WEIGHTS = ((0, (2, 4, 6)), (1, (3, 5, 7)))
REC_WEIGHTS = ((0, (10, 12, 14)), (1, (11, 13, 15)), (2, (None,)))


def prep_kernel(x0, cond, a0, sent2, first, second, side_first, side_second, x0_w, cond_w, a0_w, src, rec):
    size_x, size_z, size_y = cond.shape
    fields, conds, adjoints, _, _ = joined_rows(x0, cond, a0, first, second)
    own = slice(0, size_z)
    for f in range(2):
        for i in range(size_x + 2 * HX):
            x0_w[f, i, own] = fields[f](i)
        for i in range(size_x + 2 * HA):
            a0_w[f, i, own] = adjoints[f](i)
    for i in range(size_x + 2 * HC):
        cond_w[i, own] = conds(i)
    empty_depth(x0_w, cond_w, a0_w, own_rows(size_x), *sides_of("depth", side_first, side_second), size_z)
    lists = sent2[sent2.shape[0] - 1].astype(jnp.float32)
    place(1, 0, SRC_WEIGHTS, HC, src, lists, size_x, size_z, size_y)
    place(1, 8, REC_WEIGHTS, HU, rec, lists, size_x, size_z, size_y)


def wide_shapes(size_x, size_z, size_y):
    slab = (size_z + 2 * ZP, size_y)
    return (
        (2, size_x + 2 * HX) + slab,
        (size_x + 2 * HC,) + slab,
        (2, size_x + 2 * HA) + (size_z + 2 * HA, size_y),
        (2, size_x + 2 * HC) + slab,
        (3, size_x + 2 * HU) + slab,
    )


def prep(x0, cond, a0, sent2, first, second, side_first, side_second):
    shapes = wide_shapes(*cond.shape)
    return pl.pallas_call(
        prep_kernel,
        out_shape=tuple(pltpu.VMEM(s, jnp.float32) for s in shapes),
        in_specs=[VMEM] * 8,
        out_specs=(VMEM,) * 5,
        compiler_params=PARAMS,
        name="prep",
    )(x0, cond, a0, sent2, first, second, side_first, side_second)


def beside_z_y(c):
    rows, width = c.shape
    half = width // 2
    total = pltpu.roll(c, 1, 0) + pltpu.roll(c, rows - 1, 0)
    lane = lax.broadcasted_iota(jnp.int32, (rows, half), 1)
    first = lane == 0
    last = lane == half - 1
    a, b = c[:, :half], c[:, half:]
    ra, rb = pltpu.roll(a, 1, 1), pltpu.roll(b, 1, 1)
    la, lb = pltpu.roll(a, half - 1, 1), pltpu.roll(b, half - 1, 1)
    ya = jnp.where(first, 0.0, ra) + jnp.where(last, lb, la)
    yb = jnp.where(first, ra, rb) + jnp.where(last, 0.0, lb)
    return total + jnp.concatenate([ya, yb], axis=1)


def chain_kernel(size_x, size_z, x0_in, cond_in, a0_in, src_in, rec_in, first, second,
                 x0, cond, a0, src, rec, v0, v1, v2, u, w1, w2, sums_out, w3, acc, cond_n):
    rows_z = x0.shape[-2]
    size_y = x0.shape[-1]
    own = slice(0, size_z)
    top = size_z

    low, high = sides_of("depth", first, second)
    at = empty_depth(x0, cond, a0, corner_rows(size_x), low, high, top)
    for ref in (x0, cond, a0):
        blank = jnp.zeros((ref.shape[-2] - top, size_y), jnp.float32)
        for i in (0, ref.shape[-3] - 1):
            if len(ref.shape) == 3:
                ref[i, top:] = blank
            else:
                for f in range(2):
                    ref[f, i, top:] = blank
    for t, lists in ((0, low(at)), (2, high(at))):
        place(t, 0, SRC_WEIGHTS, HC, src, lists, size_x, size_z, size_y)
        place(t, 8, REC_WEIGHTS, HU, rec, lists, size_x, size_z, size_y)

    def edge(axis):
        at = lax.axis_index(axis)
        return (at > 0).astype(jnp.float32), (at < lax.axis_size(axis) - 1).astype(jnp.float32)

    low_x, high_x = edge("brick")
    low_z, high_z = edge("depth")
    upper = lax.broadcasted_iota(jnp.int32, (2 * HA, size_y), 0) < HA
    both_z = jnp.where(upper, high_z, low_z)

    def narrow(value):
        return jnp.concatenate([value[own], jnp.where(upper, value[top : top + ZP], value[top + ZP :])], axis=0)

    def inside(value, i, halo):
        in_x = low_x if i < halo else high_x if i >= halo + size_x else None
        if value.shape[0] == rows_z:
            parts = [value[own], value[top : top + ZP] * high_z, value[top + ZP :] * low_z]
        else:
            parts = [value[own], value[top:] * both_z]
        if in_x is not None:
            parts = [p * in_x for p in parts]
        return jnp.concatenate(parts, axis=0)

    def apply(ref, idx, i, damp):
        c = ref[idx + (i,)]
        return damp * c - (ref[idx + (i - 1,)] + ref[idx + (i + 1,)] + beside_z_y(c))

    def loop(n, body):
        for i in range(n):
            body(i)

    def thin(i):
        cond_n[i] = narrow(cond[i])

    loop(size_x + 2 * HC, thin)

    def first(i):
        for f, s in enumerate(LAPLACE_SHIFTS):
            v0[f, i] = inside(src[f, i] - apply(x0, (f,), i + 1, s * cond[i] + THETA), i, HC)

    loop(size_x + 2 * HC, first)

    def second(i):
        for f, s in enumerate(LAPLACE_SHIFTS):
            v1[f, i] = inside(narrow(apply(v0, (f,), i + 1, s * cond[i + 1])), i, 4)

    loop(size_x + 8, second)

    def third(i):
        for f, s in enumerate(LAPLACE_SHIFTS):
            v2[f, i] = inside(apply(v1, (f,), i + 1, s * cond_n[i + 2]), i, 3)

    loop(size_x + 6, third)

    def start(i):
        many = narrow(rec[2, i])
        for f, s in enumerate(LAPLACE_SHIFTS):
            u[0, f, i] = inside(
                many * narrow(x0[f, i + 3]) - narrow(rec[f, i]) - apply(a0, (f,), i + 1, s * cond_n[i + 2] + THETA),
                i,
                HU,
            )
            u[1, f, i] = many * narrow(v0[f, i + 2])
            u[2, f, i] = many * v1[f, i + 1]
            u[3, f, i] = many * v2[f, i]

    loop(size_x + 2 * HU, start)

    def level(src_ref, dst_ref, halo):
        def body(i):
            for f, s in enumerate(LAPLACE_SHIFTS):
                damp = s * cond_n[i + HC - halo]
                for k in range(4):
                    dst_ref[k, f, i] = inside(apply(src_ref, (k, f), i + 1, damp), i, halo)
        loop(size_x + 2 * halo, body)

    level(u, w1, 2)
    level(w1, w2, 1)

    def last(i):
        for f, s in enumerate(LAPLACE_SHIFTS):
            damp = s * cond_n[i + HC]
            for k in range(4):
                w3[k, f, i] = apply(w2, (k, f), i + 1, damp)[own]

    loop(size_x, last)

    def tiles(a):
        total = None
        for z in range(0, a.shape[0], 8):
            for y in range(0, a.shape[1], 128):
                t = a[z : z + 8, y : y + 128]
                total = t if total is None else total + t
        return total

    zero = jnp.zeros((8, 128), jnp.float32)

    def over_rows(body, carry, unroll=8):
        def step(i, carry):
            for j in range(unroll):
                carry = body(i * unroll + j, carry)
            return carry

        return lax.fori_loop(0, size_x // unroll, step, carry)

    for f, s in enumerate(LAPLACE_SHIFTS):
        def forward_sums(i, carry, f=f, s=s):
            p0 = v0[f, i + 5, own]
            p1 = v1[f, i + 4, own]
            p2 = v2[f, i + 3, own]
            p3 = apply(v2, (f,), i + 3, s * cond_n[i + 5])[own]
            made = (p0 * p0, p0 * p1, p1 * p1, p1 * p2, p2 * p2, p2 * p3)
            return tuple(c + tiles(a) for c, a in zip(carry, made))
        done = over_rows(forward_sums, (zero,) * 6)
        for j in range(6):
            acc[j * SLOTS + 2 * len(PAIRS) + f] = done[j]

    levels = ((u, 3, own), (w1, 2, own), (w2, 1, own), (w3, 0, slice(0, size_z)))
    for j in range(3):
        ra, oa, za = levels[j]
        rb, ob, zb = levels[j + 1]
        for f in range(2):
            def pair_sums(i, carry, f=f):
                a = [ra[k, f, i + oa, za] for k in range(4)]
                b = [rb[k, f, i + ob, zb] for k in range(4)]
                made = [a[k] * a[l] for k, l in PAIRS] + [a[k] * b[l] for k, l in PAIRS]
                return tuple(c + tiles(m) for c, m in zip(carry, made))
            done = over_rows(pair_sums, (zero,) * (2 * len(PAIRS)), 2)
            for n in range(len(PAIRS)):
                acc[2 * j * SLOTS + 2 * n + f] = done[n]
                acc[(2 * j + 1) * SLOTS + 2 * n + f] = done[len(PAIRS) + n]

    for j in range(acc.shape[0] // SLOTS):
        for n in range(0 if j >= 6 else 2 * len(PAIRS) + 2, SLOTS):
            acc[j * SLOTS + n] = zero
    by_lane = jnp.sum(acc[...], axis=1)
    ones = jnp.ones((8, 128), jnp.float32)
    out = lax.dot_general(ones, by_lane, NT, precision=lax.Precision.HIGHEST, preferred_element_type=jnp.float32)
    out = jnp.concatenate([out[0:1, :128], out[0:1, 128:]], axis=0)
    sums_out[...] = jnp.broadcast_to(out[None], sums_out.shape)


def chain(wide, first, second, size_x, size_z, n_dev):
    size_y = wide[0].shape[-1]
    f32 = jnp.float32
    slab = (size_z + 2 * ZP, size_y)
    thin = (size_z + 2 * HA, size_y)
    outs = tuple(pltpu.VMEM(a.shape, f32) for a in wide) + (
        pltpu.VMEM((2, size_x + 2 * HC) + slab, f32),
        pltpu.VMEM((2, size_x + 8) + thin, f32),
        pltpu.VMEM((2, size_x + 6) + thin, f32),
        pltpu.VMEM((4, 2, size_x + 6) + thin, f32),
        pltpu.VMEM((4, 2, size_x + 4) + thin, f32),
        pltpu.VMEM((4, 2, size_x + 2) + thin, f32),
        jax.ShapeDtypeStruct((n_dev, 2, 128), f32),
    )
    scratch = [
        pltpu.VMEM((4, 2, size_x, size_z, size_y), f32),
        pltpu.VMEM((256, 8, 128), f32),
        pltpu.VMEM((size_x + 2 * HC,) + thin, f32),
    ]
    return pl.pallas_call(
        functools.partial(chain_kernel, size_x, size_z),
        out_shape=outs,
        in_specs=[VMEM] * 7,
        out_specs=(VMEM,) * len(outs),
        scratch_shapes=scratch,
        input_output_aliases={i: i for i in range(5)},
        compiler_params=PARAMS,
        name="chain",
    )(*[held(a) for a in wide], first, second)[5:]


def coefficients(mu):
    a = [[mu[i + j + 1] + THETA * mu[i + j] for j in range(3)] for i in range(3)]

    def inverse(pivot, size):
        good = pivot > 1e-6 * size
        return jnp.where(good, 1.0 / jnp.where(good, pivot, 1.0), 0.0)

    i0 = inverse(a[0][0], 0.0)
    l10 = a[0][1] * i0
    l20 = a[0][2] * i0
    i1 = inverse(a[1][1] - l10 * a[0][1], a[1][1])
    e21 = a[1][2] - l10 * a[0][2]
    l21 = e21 * i1
    i2 = inverse(a[2][2] - l20 * a[0][2] - l21 * e21, a[2][2])
    y0 = mu[0]
    y1 = mu[1] - l10 * y0
    y2 = mu[2] - l20 * y0 - l21 * y1
    c2 = y2 * i2
    c1 = y1 * i1 - l21 * c2
    c0 = y0 * i0 - l10 * c1 - l20 * c2
    return c0, c1, c2


def combine_kernel(every, x0, a0, v0, v1, v2, u, w1, w2, forward, gradient):
    total = jnp.sum(every[...], axis=0)
    per = 128 // SLOTS
    rows = jnp.concatenate(
        [total[j // per : j // per + 1, j % per * SLOTS : (j % per + 1) * SLOTS] for j in range(6)], axis=0
    )
    rows = jnp.concatenate([rows, jnp.zeros((2, SLOTS), jnp.float32)], axis=0)
    rows = jnp.concatenate([rows, jnp.zeros((8, 128 - SLOTS), jnp.float32)], axis=1)
    n_pair = 2 * len(PAIRS)
    lane = lax.broadcasted_iota(jnp.int32, (8, 128), 1)
    even = (lane & 1) == 0

    def by_parity(values, chosen):
        values = jnp.where(chosen, values, 0.0)
        first = jnp.sum(jnp.where(even, values, 0.0), axis=1, keepdims=True)
        second = jnp.sum(jnp.where(even, 0.0, values), axis=1, keepdims=True)
        return jnp.where(even, first, second)

    mu = by_parity(rows, (lane >= n_pair) & (lane < n_pair + 2))
    c = coefficients([mu[j : j + 1] for j in range(6)])
    basis = (jnp.ones_like(c[0]),) + c
    pair = lax.broadcasted_iota(jnp.int32, (1, 128), 1) // 2
    weight = jnp.zeros((1, 128), jnp.float32)
    for n, (k, l) in enumerate(PAIRS):
        product = basis[k] * basis[l] * (1.0 if k == l else 2.0)
        weight = jnp.where(pair == n, product, weight)
    nu = by_parity(rows * weight, lane < n_pair)
    d = coefficients([nu[j : j + 1] for j in range(6)])
    size_x, size_z = x0.shape[1:3]
    own = slice(0, size_z)
    v = ((v0, 5), (v1, 4), (v2, 3))
    w = ((u, 3), (w1, 2), (w2, 1))
    scale = []
    for f in range(2):
        up = [c[k][:, f : f + 1] for k in range(3)]
        down = [[(d[j] * basis[k])[:, f : f + 1] for k in range(4)] for j in range(3)]
        scale.append((up, down))
    for i in range(size_x):
        total = None
        for f, s in enumerate(LAPLACE_SHIFTS):
            up, down = scale[f]
            field = x0[f, i]
            for k in range(3):
                field = field + up[k] * v[k][0][f, i + v[k][1], own]
            other = a0[f, i]
            for j in range(3):
                for k in range(4):
                    other = other + down[j][k] * w[j][0][k, f, i + w[j][1], own]
            forward[f, i] = field
            part = s * field * other
            total = part if total is None else total + part
        gradient[i] = (-total).astype(gradient.dtype)


def combine(every, x0, a0, *made):
    return pl.pallas_call(
        combine_kernel,
        out_shape=(
            jax.ShapeDtypeStruct(x0.shape, jnp.float32),
            jax.ShapeDtypeStruct(x0.shape[1:], jnp.bfloat16),
        ),
        in_specs=[VMEM] * (3 + len(made)),
        out_specs=(VMEM, VMEM),
        compiler_params=PARAMS,
        name="combine",
    )(every, x0, a0, *[held(a) for a in made])


def turn_kernel(blocks, out, buf, sems):
    n = buf.shape[0]
    copies = [pltpu.make_async_copy(blocks.at[k], buf.at[k], sems.at[k]) for k in range(n)]
    for copy in copies:
        copy.start()
    for k, copy in enumerate(copies):
        copy.wait()
        out[k] = buf[k].T


def turn(blocks):
    return pl.pallas_call(
        turn_kernel,
        out_shape=pltpu.VMEM(blocks.shape, blocks.dtype),
        in_specs=[HBM],
        out_specs=VMEM,
        scratch_shapes=[
            pltpu.VMEM(blocks.shape, blocks.dtype),
            pltpu.SemaphoreType.DMA((blocks.shape[0],)),
        ],
        compiler_params=PARAMS,
        name="turn",
    )(in_hbm(blocks))


def covariance_kernel(cols, rows, every, own, blocks, out):
    n_dev, size_x, size_z, width = every.shape
    n_rows = size_x * size_z
    n_blocks, size, _ = blocks.shape
    per = size // width
    table = every[...].reshape(n_dev * n_rows, width)
    at = lax.broadcasted_iota(jnp.int32, (n_dev * n_rows, n_blocks), 0)
    hits = jnp.concatenate([jnp.where(at == cols[...] * per + i, 1.0, 0.0) for i in range(per)], axis=1)
    picked = lax.dot_general(
        hits.astype(jnp.bfloat16), table, (((0,), (0,)), ((), ())), preferred_element_type=jnp.float32
    )
    picked = jnp.concatenate([picked[i * n_blocks : (i + 1) * n_blocks] for i in range(per)], axis=1)
    picked = picked.astype(jnp.bfloat16)
    which = lax.broadcasted_iota(jnp.int32, (n_blocks, size), 0)
    terms = jnp.zeros((n_blocks, size), jnp.float32)
    for k in range(n_blocks):
        terms = jnp.where(which == k, jnp.dot(picked, blocks[k], preferred_element_type=jnp.float32), terms)
    one = terms.astype(jnp.bfloat16)
    rest = terms - one.astype(jnp.float32)
    two = rest.astype(jnp.bfloat16)
    three = (rest - two.astype(jnp.float32)).astype(jnp.bfloat16)
    right = jnp.concatenate(
        [p[:, i * width : (i + 1) * width] for p in (one, two, three) for i in range(per)], axis=0
    )
    at = lax.broadcasted_iota(jnp.int32, (n_rows, n_blocks), 0)
    hits = [jnp.where(at == rows[...] * per + i, 1.0, 0.0) for i in range(per)]
    left = jnp.concatenate(hits * 3, axis=1).astype(jnp.bfloat16)
    out[...] = own[...].reshape(n_rows, width).astype(jnp.float32) + jnp.dot(
        left, right, preferred_element_type=jnp.float32
    )


def covariance(cols, rows, every, own, blocks):
    n_dev, size_x, size_z, width = every.shape
    return pl.pallas_call(
        covariance_kernel,
        out_shape=jax.ShapeDtypeStruct((size_x * size_z, width), jnp.float32),
        in_specs=[VMEM] * 5,
        out_specs=VMEM,
        compiler_params=PARAMS,
        name="covariance",
    )(cols, rows, every, own, held(blocks))


def local(
    conductivity,
    initial_field,
    adjoint_initial,
    src_cell,
    src_amp,
    rec_cell,
    observed,
    cov_blocks,
    cov_rows,
    cov_cols,
):
    size_x, size_z, size_y = conductivity.shape
    n_dev = lax.axis_size("brick") * lax.axis_size("depth")
    *sent, side_low, side_high, x0, cond, a0 = pack(
        initial_field, conductivity, adjoint_initial, src_cell[0], src_amp[0, 0], rec_cell[0], observed[0, 0]
    )
    x0, cond, a0 = held(x0), held(cond), held(a0)
    first, second = swap(*sent, "brick")
    sides = swap(side_low, side_high, "depth")
    blocks = turn(cov_blocks[0, 0])
    sent2 = mid(x0, cond, a0, sent[0], first, second, blocks, *sides)
    wide = prep(x0, cond, a0, sent2[0], first, second, *sides)
    first2, second2 = swap(*sent2, "depth")
    *made, sums = chain(wide, first2, second2, size_x, size_z, n_dev)
    every = lax.all_to_all(sums, BOTH, 0, 0, tiled=True)
    forward, gradient = combine(every, x0, a0, *made)
    every_block = lax.all_gather(gradient, "depth", axis=0, tiled=False)
    out = covariance(cov_cols[0], cov_rows[0], every_block, gradient, blocks)
    return (forward, out.reshape(size_x, size_z, size_y))


def solution(mesh):
    return jax.shard_map(
        local,
        mesh=mesh,
        in_specs=(
            P("brick", "depth", None),
            P(None, "brick", "depth", None),
            P(None, "brick", "depth", None),
            P("brick", "depth", None),
            P("brick", "depth", None, None),
            P("brick", "depth", None),
            P("brick", "depth", None, None),
            P("brick", "depth", None, None, None),
            P("brick", "depth", None),
            P("brick", "depth", None),
        ),
        out_specs=(P(None, "brick", "depth", None), P("brick", "depth", None)),
        check_vma=False,
    )
```
